256 devices in a mesh: replica: 16 (over z, core), mp: 16 (over y, x).
Axes of the slice: x: 4, y: 4, z: 8, core: 2. Of those that a mesh axis runs over, the one named last changes fastest.
Arguments:
- gradients: bfloat16 [16, 8, 768, 3072], P('replica', None, 'mp'), may hold values from -6 to 6
- feedback: bfloat16 [16, 8, 768, 3072], P('replica', None, 'mp'), may hold values from -4 to 4
- right_init: bfloat16 [8, 3072, 32], replicated, may hold values from -0.109375 to 0.109375
- gram_root: float32 [8, 32, 32], replicated, as said below
- owners: int32 [8], replicated, may hold values from 0 to 15, as said below
- momentum: float32 [16, 1, 768, 3072], P('mp', None, 'replica'), may hold values from -4 to 4
- master_weights: float32 [16, 1, 768, 3072], P('mp', None, 'replica'), may hold values from -1.5 to 1.5
- vector_grads: float32 [16, 10752], P('replica', 'mp'), may hold values from -6 to 6
- vector_momentum: float32 [10752], P('mp'), may hold values from -6 to 6
- vector_params: float32 [10752], P('mp'), may hold values from -6 to 6
Outputs:
- new_feedback: bfloat16 [16, 8, 768, 3072], P('replica', None, 'mp')
- new_momentum: float32 [16, 1, 768, 3072], P('mp', None, 'replica')
- new_master: float32 [16, 1, 768, 3072], P('mp', None, 'replica')
- new_weights: bfloat16 [8, 768, 3072], P(None, 'replica')
- new_vector_momentum: float32 [10752], P('mp')
- new_vector_params: float32 [10752], P('mp')
The draws below stay inside these ranges and needn't reach their ends.
Inputs may be any that keep to these rules, and one draw needn't show every extreme that they name: `owners`: every matrix has one owner; no owner holds more than 1 of the 8 matrices, and one owner holds exactly 1. `gram_root`: each matrix is the identity plus off-diagonal terms, times a positive scale.
All inputs are finite; a program needn't handle non-finite values.
Results may differ from the reference program's by a relative error of at most 0.007.
Values may be sent and summed in bfloat16 or wider, within the bound.
A program may use at most 192 MiB of HBM per device.

```python
import jax
import jax.numpy as jnp
from jax import lax

M = 768
N = 3072
RANK = 32
NMAT = 8
CAP = 1
NVEC = 10752
N_REPLICA = 16
N_MP = 16


def draw_owners(key, part):
    slot_key = jax.random.fold_in(key, 11)
    chosen = jax.random.permutation(slot_key, N_MP * CAP)[:NMAT]
    return (chosen // CAP).astype(jnp.int32)


def draw_gram_root(key, part):
    base_key = jax.random.fold_in(key, 23)
    spread = 0.5 * jax.random.normal(base_key, (NMAT, RANK, RANK), jnp.float32)
    eye = jnp.eye(RANK, dtype=jnp.float32)
    matrix = eye[None] + (1.0 - eye[None]) * spread * RANK ** (-0.5)
    return (matrix * (M * N_REPLICA) ** (-0.5)).astype(jnp.float32)


def steps_of(own_key, extent, pieces, smallest, high):
    def one(dim, shards_of):
        draws = jax.random.uniform(jax.random.fold_in(jax.random.fold_in(own_key, 6), dim), (shards_of,), jnp.float32, smallest / len(pieces), high / len(pieces))
        return jnp.repeat(jnp.exp(draws), extent[dim] // shards_of).reshape((-1,) + (1,) * (len(extent) - dim - 1))

    gain = one(*pieces[0])
    for cut in pieces[1:]:
        gain = gain * one(*cut)
    return gain


def centred(key, extent, deviation, most, pieces=(), kind=jnp.bfloat16):
    drawn = deviation * jax.random.normal(key, extent, jnp.float32)
    if pieces:
        drawn = drawn * steps_of(key, extent, pieces, -0.22, 0.18)
    return jnp.clip(drawn, -most, most).astype(kind)


def setup_inputs(seed: int = 0) -> dict:
    arg_keys = jax.random.split(jax.random.key(seed), 11)
    return {
        "gradients": centred(arg_keys[0], (N_REPLICA, NMAT, M, N), 1.0, 6.0, ((0, 16), (2, 16))),
        "feedback": centred(arg_keys[1], (N_REPLICA, NMAT, M, N), 0.3, 4.0, ((0, 16), (2, 16))),
        "right_init": centred(arg_keys[2], (NMAT, N, RANK), N ** -0.5, 0.109375),
        "gram_root": draw_gram_root(jax.random.fold_in(arg_keys[10], 71), 0),
        "owners": draw_owners(jax.random.fold_in(arg_keys[10], 71), 0),
        "momentum": centred(arg_keys[5], (N_MP, CAP, M, N), 0.3, 4.0, ((0, 16), (2, 16)), jnp.float32),
        "master_weights": centred(arg_keys[6], (N_MP, CAP, M, N), 0.1, 1.5, ((0, 16), (2, 16)), jnp.float32),
        "vector_grads": centred(arg_keys[7], (N_REPLICA, NVEC), 1.0, 6.0, ((0, 16), (1, 16)), jnp.float32),
        "vector_momentum": centred(arg_keys[8], (NVEC,), 1.0, 6.0, ((0, 16),), jnp.float32),
        "vector_params": centred(arg_keys[9], (NVEC,), 1.0, 6.0, ((0, 16),), jnp.float32),
    }


def reference(gradients, feedback, right_init, gram_root, owners, momentum, master_weights, vector_grads, vector_momentum, vector_params):
    highest = lax.Precision.HIGHEST
    replicas = gradients.shape[0]

    def compensated_of(index):
        return (gradients[index].astype(jnp.float32) + feedback[index].astype(jnp.float32)).astype(jnp.bfloat16)

    right_wide = right_init.astype(jnp.float32)

    def left_step(total, index):
        wide = compensated_of(index).astype(jnp.float32)
        return total + jnp.einsum("kmn,knr->kmr", wide, right_wide), None

    left_sum, _ = lax.scan(left_step, jnp.zeros((NMAT, M, RANK), jnp.float32), jnp.arange(replicas))
    left_hat = jnp.einsum("kmr,krs->kms", left_sum, gram_root, precision=highest).astype(jnp.bfloat16)
    left_wide = left_hat.astype(jnp.float32)

    def right_step(total, index):
        wide = compensated_of(index).astype(jnp.float32)
        return total + jnp.einsum("kmn,kms->kns", wide, left_wide), None

    right_new, _ = lax.scan(right_step, jnp.zeros((NMAT, N, RANK), jnp.float32), jnp.arange(replicas))
    approx = jnp.einsum("kms,kns->kmn", left_wide, right_new, precision=highest)
    new_feedback = lax.map(lambda index: (compensated_of(index).astype(jnp.float32) - approx).astype(jnp.bfloat16), jnp.arange(replicas))

    same_owner = owners[:, None] == owners[None, :]
    earlier = jnp.arange(NMAT)[:, None] < jnp.arange(NMAT)[None, :]
    ranks = jnp.sum((same_owner & earlier).astype(jnp.int32), axis=0)
    slots = owners * CAP + ranks
    slot_table = (slots[None, :] == jnp.arange(N_MP * CAP)[:, None]).astype(jnp.float32)
    approx_slots = jnp.einsum("sk,kmn->smn", slot_table, approx, precision=highest).reshape(N_MP, CAP, M, N)
    new_momentum = 0.9 * momentum + approx_slots
    new_master = master_weights - 0.1 * new_momentum
    new_weights = jnp.einsum("sk,smn->kmn", slot_table, new_master.reshape(N_MP * CAP, M, N), precision=highest).astype(jnp.bfloat16)
    vector_total = jnp.sum(vector_grads, axis=0)
    new_vector_momentum = 0.9 * vector_momentum + vector_total
    new_vector_params = vector_params - 0.1 * new_vector_momentum
    return new_feedback, new_momentum, new_master, new_weights, new_vector_momentum, new_vector_params
```

```python
import jax
import jax.numpy as jnp
from jax import lax
from jax.sharding import PartitionSpec as P


def per_device(
    gradients,
    feedback,
    right_init,
    gram_root,
    owners,
    momentum,
    master_weights,
    vector_grads,
    vector_momentum,
    vector_params,
):
    highest = lax.Precision.HIGHEST
    compensated = (gradients[0].astype(jnp.float32) + feedback[0].astype(jnp.float32)).astype(
        jnp.bfloat16
    )
    owner_count = lax.axis_size("mp")
    capacity = momentum.shape[1]
    matrices = owners.shape[0]
    replica_rows = momentum.shape[2]
    mp_index = lax.axis_index("mp")
    replica_index = lax.axis_index("replica")
    same_owner = owners[:, None] == owners[None, :]
    earlier = jnp.arange(matrices)[:, None] < jnp.arange(matrices)[None, :]
    ranks = jnp.sum((same_owner & earlier).astype(jnp.int32), axis=0)
    slots = owners * capacity + ranks
    mine = slots[None, :] == (mp_index * capacity + jnp.arange(capacity))[:, None]
    has = jnp.any(mine, axis=1)
    chosen = jnp.argmax(mine, axis=1)
    left_terms = jnp.einsum(
        "kmn,knr->kmr", compensated, right_init, preferred_element_type=jnp.float32
    )
    left_sum = lax.psum(left_terms, "replica")
    left_rows = jnp.einsum("kmr,krs->kms", left_sum, gram_root, precision=highest).astype(
        jnp.bfloat16
    )
    right_terms = jnp.einsum(
        "kmn,kms->kns", compensated, left_rows, preferred_element_type=jnp.float32
    )
    right_part = lax.psum_scatter(right_terms.reshape(-1), "mp", scatter_dimension=0, tiled=True)
    right_part = lax.psum(right_part, "replica")
    right_new = lax.all_gather(right_part.astype(jnp.bfloat16), "mp", axis=0, tiled=True).reshape(
        right_terms.shape
    )
    left_all = lax.all_gather(left_rows, "mp", axis=1, tiled=True)
    approx_rows = jnp.einsum(
        "kms,kns->kmn", left_rows, right_new, preferred_element_type=jnp.float32
    )
    new_feedback = (compensated.astype(jnp.float32) - approx_rows).astype(jnp.bfloat16)
    scale = has.astype(jnp.float32)[:, None, None]
    left_chosen = lax.dynamic_slice_in_dim(
        left_all[chosen], replica_index * replica_rows, replica_rows, 1
    ).astype(jnp.float32) * scale
    right_chosen = right_new[chosen].astype(jnp.float32) * scale
    approx_slots = jnp.einsum("cmr,cnr->cmn", left_chosen, right_chosen, precision=highest)
    new_momentum = 0.9 * momentum[0] + approx_slots
    new_master = master_weights[0] - 0.1 * new_momentum
    master_narrow = new_master.astype(jnp.bfloat16)
    weight_slots = lax.all_gather(master_narrow, "mp", axis=0, tiled=True)
    new_weights = jnp.take(weight_slots, slots, axis=0)
    vector_total = lax.psum(vector_grads[0], "replica")
    new_vector_momentum = 0.9 * vector_momentum + vector_total
    new_vector_params = vector_params - 0.1 * new_vector_momentum
    return (
        new_feedback[None],
        new_momentum[None],
        new_master[None],
        new_weights,
        new_vector_momentum,
        new_vector_params,
    )


def solution(mesh):
    return jax.shard_map(
        per_device,
        mesh=mesh,
        in_specs=(
            P("replica", None, "mp", None),
            P("replica", None, "mp", None),
            P(),
            P(),
            P(),
            P("mp", None, "replica", None),
            P("mp", None, "replica", None),
            P("replica", "mp"),
            P("mp"),
            P("mp"),
        ),
        out_specs=(
            P("replica", None, "mp", None),
            P("mp", None, "replica", None),
            P("mp", None, "replica", None),
            P(None, "replica", None),
            P("mp"),
            P("mp"),
        ),
        check_vma=False,
    )
```

```python
import functools

import jax
import jax.numpy as jnp
from jax import lax
from jax.experimental import pallas as pl
from jax.experimental.pallas import tpu as pltpu
from jax.sharding import PartitionSpec as P

MESH_IDS = pl.DeviceIdType.MESH


def _exchange_kernel(n, x_ref, o_ref, recv, send_sem, recv_sem):
    me = lax.axis_index("replica")
    mp = lax.axis_index("mp")
    barrier = pltpu.get_barrier_semaphore()
    for d in range(1, n):
        peer = lax.rem(me + d, n)
        pl.semaphore_signal(barrier, inc=1, device_id=(peer, mp), device_id_type=MESH_IDS)
    pl.semaphore_wait(barrier, n - 1)
    copies = []
    for d in range(1, n):
        peer = lax.rem(me + d, n)
        copy = pltpu.make_async_remote_copy(
            src_ref=x_ref.at[peer],
            dst_ref=recv.at[me],
            send_sem=send_sem.at[d],
            recv_sem=recv_sem.at[me],
            device_id=(peer, mp),
            device_id_type=MESH_IDS,
        )
        copy.start()
        copies.append(copy)
    recv[me] = x_ref[me]
    for d in range(1, n):
        source = lax.rem(me + n - d, n)
        pltpu.make_async_remote_copy(
            src_ref=x_ref.at[source],
            dst_ref=recv.at[source],
            send_sem=send_sem.at[d],
            recv_sem=recv_sem.at[source],
            device_id=(source, mp),
            device_id_type=MESH_IDS,
        ).wait_recv()
    for copy in copies:
        copy.wait_send()
    o_ref[...] = recv[...]


def exchange(x, cid):
    n = x.shape[0]
    return pl.pallas_call(
        functools.partial(_exchange_kernel, n),
        out_shape=jax.ShapeDtypeStruct(x.shape, x.dtype),
        in_specs=[pl.BlockSpec(memory_space=pltpu.VMEM)],
        out_specs=pl.BlockSpec(memory_space=pltpu.VMEM),
        scratch_shapes=[
            pltpu.VMEM(x.shape, x.dtype),
            pltpu.SemaphoreType.DMA((n,)),
            pltpu.SemaphoreType.DMA((n,)),
        ],
        compiler_params=pltpu.CompilerParams(collective_id=cid, has_side_effects=True),
    )(x)


def per_device(
    gradients,
    feedback,
    right_init,
    gram_root,
    owners,
    momentum,
    master_weights,
    vector_grads,
    vector_momentum,
    vector_params,
):
    highest = lax.Precision.HIGHEST
    compensated = (gradients[0].astype(jnp.float32) + feedback[0].astype(jnp.float32)).astype(
        jnp.bfloat16
    )
    owner_count = lax.axis_size("mp")
    capacity = momentum.shape[1]
    matrices = owners.shape[0]
    replica_rows = momentum.shape[2]
    mp_index = lax.axis_index("mp")
    replica_index = lax.axis_index("replica")
    same_owner = owners[:, None] == owners[None, :]
    earlier = jnp.arange(matrices)[:, None] < jnp.arange(matrices)[None, :]
    ranks = jnp.sum((same_owner & earlier).astype(jnp.int32), axis=0)
    slots = owners * capacity + ranks
    mine = slots[None, :] == (mp_index * capacity + jnp.arange(capacity))[:, None]
    has = jnp.any(mine, axis=1)
    chosen = jnp.argmax(mine, axis=1)
    left_terms = jnp.einsum(
        "kmn,knr->kmr", compensated, right_init, preferred_element_type=jnp.float32
    )
    replicas = lax.axis_size("replica")
    vector_len = vector_grads.shape[1]
    packed = jnp.concatenate([left_terms.reshape(-1), vector_grads[0]])
    lanes = 128
    rows = -(-packed.shape[0] // (8 * lanes)) * 8
    packed = jnp.pad(packed, (0, rows * lanes - packed.shape[0])).reshape(rows, lanes)
    packed = jnp.sum(exchange(jnp.broadcast_to(packed, (replicas, rows, lanes)), 0), axis=0)
    packed = packed.reshape(-1)
    left_sum = packed[: left_terms.size].reshape(left_terms.shape)
    vector_total = packed[left_terms.size : left_terms.size + vector_len]
    left_rows = jnp.einsum("kmr,krs->kms", left_sum, gram_root, precision=highest).astype(
        jnp.bfloat16
    )
    right_terms = jnp.einsum(
        "kmn,kms->kns", compensated, left_rows, preferred_element_type=jnp.float32
    )
    right_part = lax.psum_scatter(right_terms.reshape(-1), "mp", scatter_dimension=0, tiled=True)
    right_part = right_part.reshape(replicas, -1, lanes)
    right_chunk = jnp.sum(exchange(right_part, 1), axis=0)
    right_part = exchange(jnp.broadcast_to(right_chunk, right_part.shape), 2).reshape(-1)
    right_new = lax.all_gather(right_part.astype(jnp.bfloat16), "mp", axis=0, tiled=True).reshape(
        right_terms.shape
    )
    left_all = lax.all_gather(left_rows, "mp", axis=1, tiled=True)
    approx_rows = jnp.einsum(
        "kms,kns->kmn", left_rows, right_new, preferred_element_type=jnp.float32
    )
    new_feedback = (compensated.astype(jnp.float32) - approx_rows).astype(jnp.bfloat16)
    scale = has.astype(jnp.float32)[:, None, None]
    left_chosen = lax.dynamic_slice_in_dim(
        left_all[chosen], replica_index * replica_rows, replica_rows, 1
    ).astype(jnp.float32) * scale
    right_chosen = right_new[chosen].astype(jnp.float32) * scale
    approx_slots = jnp.einsum("cmr,cnr->cmn", left_chosen, right_chosen, precision=highest)
    new_momentum = 0.9 * momentum[0] + approx_slots
    new_master = master_weights[0] - 0.1 * new_momentum
    master_narrow = new_master.astype(jnp.bfloat16)
    weight_slots = lax.all_gather(master_narrow, "mp", axis=0, tiled=True)
    new_weights = jnp.take(weight_slots, slots, axis=0)
    new_vector_momentum = 0.9 * vector_momentum + vector_total
    new_vector_params = vector_params - 0.1 * new_vector_momentum
    return (
        new_feedback[None],
        new_momentum[None],
        new_master[None],
        new_weights,
        new_vector_momentum,
        new_vector_params,
    )


def solution(mesh):
    return jax.shard_map(
        per_device,
        mesh=mesh,
        in_specs=(
            P("replica", None, "mp", None),
            P("replica", None, "mp", None),
            P(),
            P(),
            P(),
            P("mp", None, "replica", None),
            P("mp", None, "replica", None),
            P("replica", "mp"),
            P("mp"),
            P("mp"),
        ),
        out_specs=(
            P("replica", None, "mp", None),
            P("mp", None, "replica", None),
            P("mp", None, "replica", None),
            P(None, "replica", None),
            P("mp"),
            P("mp"),
        ),
        check_vma=False,
    )
```

```python
import functools

import jax
import jax.numpy as jnp
from jax import lax
from jax.experimental import pallas as pl
from jax.experimental.pallas import tpu as pltpu
from jax.sharding import PartitionSpec as P

MESH_IDS = pl.DeviceIdType.MESH


def _exchange_kernel(n, axis, x_ref, o_ref, recv, send_sem, recv_sem):
    me = lax.axis_index(axis)
    here = [lax.axis_index("replica"), lax.axis_index("mp")]
    where = 0 if axis == "replica" else 1

    def device(peer):
        ids = list(here)
        ids[where] = peer
        return tuple(ids)

    barrier = pltpu.get_barrier_semaphore()
    for d in range(1, n):
        peer = lax.rem(me + d, n)
        pl.semaphore_signal(barrier, inc=1, device_id=device(peer), device_id_type=MESH_IDS)
    pl.semaphore_wait(barrier, n - 1)
    copies = []
    for d in range(1, n):
        peer = lax.rem(me + d, n)
        copy = pltpu.make_async_remote_copy(
            src_ref=x_ref.at[peer],
            dst_ref=recv.at[me],
            send_sem=send_sem.at[d],
            recv_sem=recv_sem.at[me],
            device_id=device(peer),
            device_id_type=MESH_IDS,
        )
        copy.start()
        copies.append(copy)
    recv[me] = x_ref[me]
    for d in range(1, n):
        source = lax.rem(me + n - d, n)
        pltpu.make_async_remote_copy(
            src_ref=x_ref.at[source],
            dst_ref=recv.at[source],
            send_sem=send_sem.at[d],
            recv_sem=recv_sem.at[source],
            device_id=device(source),
            device_id_type=MESH_IDS,
        ).wait_recv()
    for copy in copies:
        copy.wait_send()
    o_ref[...] = recv[...]


def exchange(x, axis, cid):
    n = x.shape[0]
    return pl.pallas_call(
        functools.partial(_exchange_kernel, n, axis),
        out_shape=jax.ShapeDtypeStruct(x.shape, x.dtype),
        in_specs=[pl.BlockSpec(memory_space=pltpu.VMEM)],
        out_specs=pl.BlockSpec(memory_space=pltpu.VMEM),
        scratch_shapes=[
            pltpu.VMEM(x.shape, x.dtype),
            pltpu.SemaphoreType.DMA((n,)),
            pltpu.SemaphoreType.DMA((n,)),
        ],
        compiler_params=pltpu.CompilerParams(
            collective_id=cid, has_side_effects=True, vmem_limit_bytes=48 * 1024 * 1024
        ),
    )(x)


def per_device(
    gradients,
    feedback,
    right_init,
    gram_root,
    owners,
    momentum,
    master_weights,
    vector_grads,
    vector_momentum,
    vector_params,
):
    highest = lax.Precision.HIGHEST
    compensated = (gradients[0].astype(jnp.float32) + feedback[0].astype(jnp.float32)).astype(
        jnp.bfloat16
    )
    owner_count = lax.axis_size("mp")
    capacity = momentum.shape[1]
    matrices = owners.shape[0]
    replica_rows = momentum.shape[2]
    mp_index = lax.axis_index("mp")
    replica_index = lax.axis_index("replica")
    same_owner = owners[:, None] == owners[None, :]
    earlier = jnp.arange(matrices)[:, None] < jnp.arange(matrices)[None, :]
    ranks = jnp.sum((same_owner & earlier).astype(jnp.int32), axis=0)
    slots = owners * capacity + ranks
    mine = slots[None, :] == (mp_index * capacity + jnp.arange(capacity))[:, None]
    has = jnp.any(mine, axis=1)
    chosen = jnp.argmax(mine, axis=1)
    left_terms = jnp.einsum(
        "kmn,knr->kmr", compensated, right_init, preferred_element_type=jnp.float32
    )
    replicas = lax.axis_size("replica")
    vector_len = vector_grads.shape[1]
    packed = jnp.concatenate([left_terms.reshape(-1), vector_grads[0]])
    lanes = 128
    rows = -(-packed.shape[0] // (8 * lanes)) * 8
    packed = jnp.pad(packed, (0, rows * lanes - packed.shape[0])).reshape(rows, lanes)
    packed = jnp.sum(exchange(jnp.broadcast_to(packed, (replicas, rows, lanes)), "replica", 0), axis=0)
    packed = packed.reshape(-1)
    left_sum = packed[: left_terms.size].reshape(left_terms.shape)
    vector_total = packed[left_terms.size : left_terms.size + vector_len]
    left_rows = jnp.einsum("kmr,krs->kms", left_sum, gram_root, precision=highest).astype(
        jnp.bfloat16
    )
    owners_count = lax.axis_size("mp")
    right_terms = jnp.einsum(
        "kmn,kms->ksn", compensated, left_rows, preferred_element_type=jnp.float32
    )
    right_slots = right_terms.reshape(owners_count, -1, right_terms.shape[2])
    right_part = jnp.sum(exchange(right_slots, "mp", 1), axis=0)
    part_shape = right_part.shape
    right_part = right_part.reshape(replicas, -1, lanes)
    right_chunk = jnp.sum(exchange(right_part, "replica", 2), axis=0)
    right_part = exchange(jnp.broadcast_to(right_chunk, right_part.shape), "replica", 3)
    right_part = right_part.reshape(part_shape).astype(jnp.bfloat16)
    right_new = exchange(
        jnp.broadcast_to(right_part, right_slots.shape), "mp", 4
    ).reshape(right_terms.shape)
    pairs = [
        (a * owners_count + b, b * owners_count + a)
        for a in range(replicas)
        for b in range(owners_count)
    ]
    left_block = lax.ppermute(left_rows, ("replica", "mp"), pairs)
    approx_rows = jnp.einsum(
        "kms,ksn->kmn", left_rows, right_new, preferred_element_type=jnp.float32
    )
    new_feedback = (compensated.astype(jnp.float32) - approx_rows).astype(jnp.bfloat16)
    scale = has.astype(jnp.float32)[:, None, None]
    left_chosen = left_block[chosen].astype(jnp.float32) * scale
    right_chosen = right_new[chosen].astype(jnp.float32) * scale
    approx_slots = jnp.einsum("cmr,crn->cmn", left_chosen, right_chosen, precision=highest)
    new_momentum = 0.9 * momentum[0] + approx_slots
    new_master = master_weights[0] - 0.1 * new_momentum
    master_narrow = new_master.astype(jnp.bfloat16)
    weight_slots = lax.all_gather(master_narrow, "mp", axis=0, tiled=True)
    new_weights = jnp.take(weight_slots, slots, axis=0)
    new_vector_momentum = 0.9 * vector_momentum + vector_total
    new_vector_params = vector_params - 0.1 * new_vector_momentum
    return (
        new_feedback[None],
        new_momentum[None],
        new_master[None],
        new_weights,
        new_vector_momentum,
        new_vector_params,
    )


def solution(mesh):
    return jax.shard_map(
        per_device,
        mesh=mesh,
        in_specs=(
            P("replica", None, "mp", None),
            P("replica", None, "mp", None),
            P(),
            P(),
            P(),
            P("mp", None, "replica", None),
            P("mp", None, "replica", None),
            P("replica", "mp"),
            P("mp"),
            P("mp"),
        ),
        out_specs=(
            P("replica", None, "mp", None),
            P("mp", None, "replica", None),
            P("mp", None, "replica", None),
            P(None, "replica", None),
            P("mp"),
            P("mp"),
        ),
        check_vma=False,
    )
```

```python
import functools

import jax
import jax.numpy as jnp
from jax import lax
from jax.experimental import pallas as pl
from jax.experimental.pallas import tpu as pltpu
from jax.sharding import PartitionSpec as P

MESH_IDS = pl.DeviceIdType.MESH


def _exchange_kernel(n, axis, x_ref, o_ref, recv, send_sem, recv_sem):
    me = lax.axis_index(axis)
    here = [lax.axis_index("replica"), lax.axis_index("mp")]
    where = 0 if axis == "replica" else 1

    def device(peer):
        ids = list(here)
        ids[where] = peer
        return tuple(ids)

    barrier = pltpu.get_barrier_semaphore()
    for d in range(1, n):
        peer = lax.rem(me + d, n)
        pl.semaphore_signal(barrier, inc=1, device_id=device(peer), device_id_type=MESH_IDS)
    pl.semaphore_wait(barrier, n - 1)
    copies = []
    for d in range(1, n):
        peer = lax.rem(me + d, n)
        copy = pltpu.make_async_remote_copy(
            src_ref=x_ref.at[peer],
            dst_ref=recv.at[me],
            send_sem=send_sem.at[d],
            recv_sem=recv_sem.at[me],
            device_id=device(peer),
            device_id_type=MESH_IDS,
        )
        copy.start()
        copies.append(copy)
    recv[me] = x_ref[me]
    for d in range(1, n):
        source = lax.rem(me + n - d, n)
        pltpu.make_async_remote_copy(
            src_ref=x_ref.at[source],
            dst_ref=recv.at[source],
            send_sem=send_sem.at[d],
            recv_sem=recv_sem.at[source],
            device_id=device(source),
            device_id_type=MESH_IDS,
        ).wait_recv()
    for copy in copies:
        copy.wait_send()
    o_ref[...] = recv[...]


def exchange(x, axis, cid):
    n = x.shape[0]
    return pl.pallas_call(
        functools.partial(_exchange_kernel, n, axis),
        out_shape=jax.ShapeDtypeStruct(x.shape, x.dtype),
        in_specs=[pl.BlockSpec(memory_space=pltpu.VMEM)],
        out_specs=pl.BlockSpec(memory_space=pltpu.VMEM),
        scratch_shapes=[
            pltpu.VMEM(x.shape, x.dtype),
            pltpu.SemaphoreType.DMA((n,)),
            pltpu.SemaphoreType.DMA((n,)),
        ],
        compiler_params=pltpu.CompilerParams(
            collective_id=cid, has_side_effects=True, vmem_limit_bytes=48 * 1024 * 1024
        ),
    )(x)


def per_device(
    gradients,
    feedback,
    right_init,
    gram_root,
    owners,
    momentum,
    master_weights,
    vector_grads,
    vector_momentum,
    vector_params,
):
    highest = lax.Precision.HIGHEST
    compensated = (gradients[0].astype(jnp.float32) + feedback[0].astype(jnp.float32)).astype(
        jnp.bfloat16
    )
    owner_count = lax.axis_size("mp")
    capacity = momentum.shape[1]
    matrices = owners.shape[0]
    replica_rows = momentum.shape[2]
    mp_index = lax.axis_index("mp")
    replica_index = lax.axis_index("replica")
    same_owner = owners[:, None] == owners[None, :]
    earlier = jnp.arange(matrices)[:, None] < jnp.arange(matrices)[None, :]
    ranks = jnp.sum((same_owner & earlier).astype(jnp.int32), axis=0)
    slots = owners * capacity + ranks
    mine = slots[None, :] == (mp_index * capacity + jnp.arange(capacity))[:, None]
    has = jnp.any(mine, axis=1)
    chosen = jnp.argmax(mine, axis=1)
    weight_base = master_weights[0] - 0.1 * (0.9 * momentum[0])
    weight_slots = lax.all_gather(weight_base.astype(jnp.bfloat16), "mp", axis=0, tiled=True)
    left_terms = jnp.einsum(
        "kmn,knr->kmr", compensated, right_init, preferred_element_type=jnp.float32
    )
    replicas = lax.axis_size("replica")
    vector_len = vector_grads.shape[1]
    packed = jnp.concatenate([left_terms.reshape(-1), vector_grads[0]])
    lanes = 128
    rows = -(-packed.shape[0] // (8 * lanes)) * 8
    packed = jnp.pad(packed, (0, rows * lanes - packed.shape[0])).reshape(rows, lanes)
    packed = jnp.sum(exchange(jnp.broadcast_to(packed, (replicas, rows, lanes)), "replica", 0), axis=0)
    packed = packed.reshape(-1)
    left_sum = packed[: left_terms.size].reshape(left_terms.shape)
    vector_total = packed[left_terms.size : left_terms.size + vector_len]
    left_rows = jnp.einsum("kmr,krs->kms", left_sum, gram_root, precision=highest).astype(
        jnp.bfloat16
    )
    owners_count = lax.axis_size("mp")
    right_terms = jnp.einsum(
        "kmn,kms->ksn", compensated, left_rows, preferred_element_type=jnp.float32
    )
    right_slots = right_terms.reshape(owners_count, -1, right_terms.shape[2])
    right_part = jnp.sum(exchange(right_slots, "mp", 1), axis=0)
    part_shape = right_part.shape
    right_part = right_part.reshape(replicas, -1, lanes)
    right_chunk = jnp.sum(exchange(right_part, "replica", 2), axis=0)
    right_part = exchange(jnp.broadcast_to(right_chunk, right_part.shape), "replica", 3)
    right_part = right_part.reshape(part_shape).astype(jnp.bfloat16)
    right_new = exchange(
        jnp.broadcast_to(right_part, right_slots.shape), "mp", 4
    ).reshape(right_terms.shape)
    pairs = [
        (a * owners_count + b, b * owners_count + a)
        for a in range(replicas)
        for b in range(owners_count)
    ]
    left_block = lax.ppermute(left_rows, ("replica", "mp"), pairs)
    approx_rows = jnp.einsum(
        "kms,ksn->kmn", left_rows, right_new, preferred_element_type=jnp.float32
    )
    new_feedback = (compensated.astype(jnp.float32) - approx_rows).astype(jnp.bfloat16)
    scale = has.astype(jnp.float32)[:, None, None]
    left_chosen = left_block[chosen].astype(jnp.float32) * scale
    right_chosen = right_new[chosen].astype(jnp.float32) * scale
    approx_slots = jnp.einsum("cmr,crn->cmn", left_chosen, right_chosen, precision=highest)
    new_momentum = 0.9 * momentum[0] + approx_slots
    new_master = master_weights[0] - 0.1 * new_momentum
    block_approx = jnp.einsum(
        "kms,ksn->kmn", left_block, right_new, preferred_element_type=jnp.float32
    )
    new_weights = (
        jnp.take(weight_slots, slots, axis=0).astype(jnp.float32) - 0.1 * block_approx
    ).astype(jnp.bfloat16)
    new_vector_momentum = 0.9 * vector_momentum + vector_total
    new_vector_params = vector_params - 0.1 * new_vector_momentum
    return (
        new_feedback[None],
        new_momentum[None],
        new_master[None],
        new_weights,
        new_vector_momentum,
        new_vector_params,
    )


def solution(mesh):
    return jax.shard_map(
        per_device,
        mesh=mesh,
        in_specs=(
            P("replica", None, "mp", None),
            P("replica", None, "mp", None),
            P(),
            P(),
            P(),
            P("mp", None, "replica", None),
            P("mp", None, "replica", None),
            P("replica", "mp"),
            P("mp"),
            P("mp"),
        ),
        out_specs=(
            P("replica", None, "mp", None),
            P("mp", None, "replica", None),
            P("mp", None, "replica", None),
            P(None, "replica", None),
            P("mp"),
            P("mp"),
        ),
        check_vma=False,
    )
```

```python
import functools

import jax
import jax.numpy as jnp
from jax import lax
from jax.experimental import pallas as pl
from jax.experimental.pallas import tpu as pltpu
from jax.sharding import PartitionSpec as P

MESH_IDS = pl.DeviceIdType.MESH


def _exchange_kernel(n, axis, x_ref, o_ref, recv, send_sem, recv_sem):
    me = lax.axis_index(axis)
    here = [lax.axis_index("replica"), lax.axis_index("mp")]
    where = 0 if axis == "replica" else 1

    def device(peer):
        ids = list(here)
        ids[where] = peer
        return tuple(ids)

    barrier = pltpu.get_barrier_semaphore()
    for d in range(1, n):
        peer = lax.rem(me + d, n)
        pl.semaphore_signal(barrier, inc=1, device_id=device(peer), device_id_type=MESH_IDS)
    pl.semaphore_wait(barrier, n - 1)
    copies = []
    for d in range(1, n):
        peer = lax.rem(me + d, n)
        copy = pltpu.make_async_remote_copy(
            src_ref=x_ref.at[peer],
            dst_ref=recv.at[me],
            send_sem=send_sem.at[d],
            recv_sem=recv_sem.at[me],
            device_id=device(peer),
            device_id_type=MESH_IDS,
        )
        copy.start()
        copies.append(copy)
    recv[me] = x_ref[me]
    for d in range(1, n):
        source = lax.rem(me + n - d, n)
        pltpu.make_async_remote_copy(
            src_ref=x_ref.at[source],
            dst_ref=recv.at[source],
            send_sem=send_sem.at[d],
            recv_sem=recv_sem.at[source],
            device_id=device(source),
            device_id_type=MESH_IDS,
        ).wait_recv()
    for copy in copies:
        copy.wait_send()
    o_ref[...] = recv[...]


def exchange(x, axis, cid):
    n = x.shape[0]
    return pl.pallas_call(
        functools.partial(_exchange_kernel, n, axis),
        out_shape=jax.ShapeDtypeStruct(x.shape, x.dtype),
        in_specs=[pl.BlockSpec(memory_space=pltpu.VMEM)],
        out_specs=pl.BlockSpec(memory_space=pltpu.VMEM),
        scratch_shapes=[
            pltpu.VMEM(x.shape, x.dtype),
            pltpu.SemaphoreType.DMA((n,)),
            pltpu.SemaphoreType.DMA((n,)),
        ],
        compiler_params=pltpu.CompilerParams(
            collective_id=cid, has_side_effects=True, vmem_limit_bytes=48 * 1024 * 1024
        ),
    )(x)


def per_device(
    gradients,
    feedback,
    right_init,
    gram_root,
    owners,
    momentum,
    master_weights,
    vector_grads,
    vector_momentum,
    vector_params,
):
    highest = lax.Precision.HIGHEST
    compensated = (gradients[0].astype(jnp.float32) + feedback[0].astype(jnp.float32)).astype(
        jnp.bfloat16
    )
    owner_count = lax.axis_size("mp")
    capacity = momentum.shape[1]
    matrices = owners.shape[0]
    replica_rows = momentum.shape[2]
    mp_index = lax.axis_index("mp")
    replica_index = lax.axis_index("replica")
    same_owner = owners[:, None] == owners[None, :]
    earlier = jnp.arange(matrices)[:, None] < jnp.arange(matrices)[None, :]
    ranks = jnp.sum((same_owner & earlier).astype(jnp.int32), axis=0)
    slots = owners * capacity + ranks
    mine = slots[None, :] == (mp_index * capacity + jnp.arange(capacity))[:, None]
    has = jnp.any(mine, axis=1)
    chosen = jnp.argmax(mine, axis=1)
    weight_base = master_weights[0] - 0.1 * (0.9 * momentum[0])
    weight_slots = lax.all_gather(weight_base.astype(jnp.bfloat16), "mp", axis=0, tiled=True)
    left_terms = jnp.einsum(
        "kmn,knr->kmr", compensated, right_init, preferred_element_type=jnp.float32
    )
    replicas = lax.axis_size("replica")
    vector_len = vector_grads.shape[1]
    packed = jnp.concatenate([left_terms.reshape(-1), vector_grads[0]])
    lanes = 128
    rows = -(-packed.shape[0] // (8 * lanes)) * 8
    packed = jnp.pad(packed, (0, rows * lanes - packed.shape[0])).reshape(rows, lanes)
    packed = jnp.sum(exchange(jnp.broadcast_to(packed, (replicas, rows, lanes)), "replica", 0), axis=0)
    packed = packed.reshape(-1)
    left_sum = packed[: left_terms.size].reshape(left_terms.shape)
    vector_total = packed[left_terms.size : left_terms.size + vector_len]
    left_rows = jnp.einsum("kmr,krs->kms", left_sum, gram_root, precision=highest).astype(
        jnp.bfloat16
    )
    owners_count = lax.axis_size("mp")
    right_terms = jnp.einsum(
        "kmn,kms->ksn", compensated, left_rows, preferred_element_type=jnp.float32
    )
    right_slots = right_terms.reshape(owners_count, -1, right_terms.shape[2])
    right_part = jnp.sum(
        exchange(right_slots.astype(jnp.bfloat16), "mp", 1).astype(jnp.float32), axis=0
    )
    part_shape = right_part.shape
    right_part = right_part.reshape(replicas, -1, lanes)
    right_chunk = jnp.sum(exchange(right_part, "replica", 2), axis=0)
    right_part = exchange(jnp.broadcast_to(right_chunk, right_part.shape), "replica", 3)
    right_part = right_part.reshape(part_shape).astype(jnp.bfloat16)
    right_new = exchange(
        jnp.broadcast_to(right_part, right_slots.shape), "mp", 4
    ).reshape(right_terms.shape)
    pairs = [
        (a * owners_count + b, b * owners_count + a)
        for a in range(replicas)
        for b in range(owners_count)
    ]
    left_block = lax.ppermute(left_rows, ("replica", "mp"), pairs)
    approx_rows = jnp.einsum(
        "kms,ksn->kmn", left_rows, right_new, preferred_element_type=jnp.float32
    )
    new_feedback = (compensated.astype(jnp.float32) - approx_rows).astype(jnp.bfloat16)
    scale = has.astype(jnp.float32)[:, None, None]
    left_chosen = left_block[chosen].astype(jnp.float32) * scale
    right_chosen = right_new[chosen].astype(jnp.float32) * scale
    approx_slots = jnp.einsum("cmr,crn->cmn", left_chosen, right_chosen, precision=highest)
    new_momentum = 0.9 * momentum[0] + approx_slots
    new_master = master_weights[0] - 0.1 * new_momentum
    block_approx = jnp.einsum(
        "kms,ksn->kmn", left_block, right_new, preferred_element_type=jnp.float32
    )
    new_weights = (
        jnp.take(weight_slots, slots, axis=0).astype(jnp.float32) - 0.1 * block_approx
    ).astype(jnp.bfloat16)
    new_vector_momentum = 0.9 * vector_momentum + vector_total
    new_vector_params = vector_params - 0.1 * new_vector_momentum
    return (
        new_feedback[None],
        new_momentum[None],
        new_master[None],
        new_weights,
        new_vector_momentum,
        new_vector_params,
    )


def solution(mesh):
    return jax.shard_map(
        per_device,
        mesh=mesh,
        in_specs=(
            P("replica", None, "mp", None),
            P("replica", None, "mp", None),
            P(),
            P(),
            P(),
            P("mp", None, "replica", None),
            P("mp", None, "replica", None),
            P("replica", "mp"),
            P("mp"),
            P("mp"),
        ),
        out_specs=(
            P("replica", None, "mp", None),
            P("mp", None, "replica", None),
            P("mp", None, "replica", None),
            P(None, "replica", None),
            P("mp"),
            P("mp"),
        ),
        check_vma=False,
    )
```

```python
import functools

import jax
import jax.numpy as jnp
from jax import lax
from jax.experimental import pallas as pl
from jax.experimental.pallas import tpu as pltpu
from jax.sharding import PartitionSpec as P

MESH_IDS = pl.DeviceIdType.MESH


def _exchange_kernel(n, axis, x_ref, o_ref, recv, send_sem, recv_sem):
    me = lax.axis_index(axis)
    here = [lax.axis_index("replica"), lax.axis_index("mp")]
    where = 0 if axis == "replica" else 1

    def device(peer):
        ids = list(here)
        ids[where] = peer
        return tuple(ids)

    barrier = pltpu.get_barrier_semaphore()
    for d in range(1, n):
        peer = lax.rem(me + d, n)
        pl.semaphore_signal(barrier, inc=1, device_id=device(peer), device_id_type=MESH_IDS)
    pl.semaphore_wait(barrier, n - 1)
    copies = []
    for d in range(1, n):
        peer = lax.rem(me + d, n)
        copy = pltpu.make_async_remote_copy(
            src_ref=x_ref.at[peer],
            dst_ref=recv.at[me],
            send_sem=send_sem.at[d],
            recv_sem=recv_sem.at[me],
            device_id=device(peer),
            device_id_type=MESH_IDS,
        )
        copy.start()
        copies.append(copy)
    recv[me] = x_ref[me]
    for d in range(1, n):
        source = lax.rem(me + n - d, n)
        pltpu.make_async_remote_copy(
            src_ref=x_ref.at[source],
            dst_ref=recv.at[source],
            send_sem=send_sem.at[d],
            recv_sem=recv_sem.at[source],
            device_id=device(source),
            device_id_type=MESH_IDS,
        ).wait_recv()
    for copy in copies:
        copy.wait_send()
    o_ref[...] = recv[...]


def exchange(x, axis, cid):
    n = x.shape[0]
    return pl.pallas_call(
        functools.partial(_exchange_kernel, n, axis),
        out_shape=jax.ShapeDtypeStruct(x.shape, x.dtype),
        in_specs=[pl.BlockSpec(memory_space=pltpu.VMEM)],
        out_specs=pl.BlockSpec(memory_space=pltpu.VMEM),
        scratch_shapes=[
            pltpu.VMEM(x.shape, x.dtype),
            pltpu.SemaphoreType.DMA((n,)),
            pltpu.SemaphoreType.DMA((n,)),
        ],
        compiler_params=pltpu.CompilerParams(
            collective_id=cid, has_side_effects=True, vmem_limit_bytes=48 * 1024 * 1024
        ),
    )(x)


def _allreduce_kernel(n, x_ref, o_ref, first, middle, second, send_sem, recv_sem):
    me = lax.axis_index("replica")
    mp = lax.axis_index("mp")
    barrier = pltpu.get_barrier_semaphore()
    for d in range(1, n):
        peer = lax.rem(me + d, n)
        pl.semaphore_signal(barrier, inc=1, device_id=(peer, mp), device_id_type=MESH_IDS)
    pl.semaphore_wait(barrier, n - 1)

    def round_trip(phase, source_of, landing):
        copies = []
        for d in range(1, n):
            peer = lax.rem(me + d, n)
            copy = pltpu.make_async_remote_copy(
                src_ref=source_of(peer),
                dst_ref=landing.at[me],
                send_sem=send_sem.at[phase, d],
                recv_sem=recv_sem.at[phase, me],
                device_id=(peer, mp),
                device_id_type=MESH_IDS,
            )
            copy.start()
            copies.append(copy)
        landing[me] = source_of(me)[...]
        for d in range(1, n):
            source = lax.rem(me + n - d, n)
            pltpu.make_async_remote_copy(
                src_ref=source_of(source),
                dst_ref=landing.at[source],
                send_sem=send_sem.at[phase, d],
                recv_sem=recv_sem.at[phase, source],
                device_id=(source, mp),
                device_id_type=MESH_IDS,
            ).wait_recv()
        for copy in copies:
            copy.wait_send()

    round_trip(0, lambda peer: x_ref.at[peer], first)
    total = first[0]
    for s in range(1, n):
        total = total + first[s]
    middle[...] = total
    round_trip(1, lambda peer: middle, second)
    o_ref[...] = second[...]


def allreduce_replica(x, cid):
    n = x.shape[0]
    return pl.pallas_call(
        functools.partial(_allreduce_kernel, n),
        out_shape=jax.ShapeDtypeStruct(x.shape, x.dtype),
        in_specs=[pl.BlockSpec(memory_space=pltpu.VMEM)],
        out_specs=pl.BlockSpec(memory_space=pltpu.VMEM),
        scratch_shapes=[
            pltpu.VMEM(x.shape, x.dtype),
            pltpu.VMEM(x.shape[1:], x.dtype),
            pltpu.VMEM(x.shape, x.dtype),
            pltpu.SemaphoreType.DMA((2, n)),
            pltpu.SemaphoreType.DMA((2, n)),
        ],
        compiler_params=pltpu.CompilerParams(collective_id=cid, has_side_effects=True),
    )(x)


def per_device(
    gradients,
    feedback,
    right_init,
    gram_root,
    owners,
    momentum,
    master_weights,
    vector_grads,
    vector_momentum,
    vector_params,
):
    highest = lax.Precision.HIGHEST
    compensated = (gradients[0].astype(jnp.float32) + feedback[0].astype(jnp.float32)).astype(
        jnp.bfloat16
    )
    owner_count = lax.axis_size("mp")
    capacity = momentum.shape[1]
    matrices = owners.shape[0]
    replica_rows = momentum.shape[2]
    mp_index = lax.axis_index("mp")
    replica_index = lax.axis_index("replica")
    same_owner = owners[:, None] == owners[None, :]
    earlier = jnp.arange(matrices)[:, None] < jnp.arange(matrices)[None, :]
    ranks = jnp.sum((same_owner & earlier).astype(jnp.int32), axis=0)
    slots = owners * capacity + ranks
    mine = slots[None, :] == (mp_index * capacity + jnp.arange(capacity))[:, None]
    has = jnp.any(mine, axis=1)
    chosen = jnp.argmax(mine, axis=1)
    weight_base = master_weights[0] - 0.1 * (0.9 * momentum[0])
    weight_slots = lax.all_gather(weight_base.astype(jnp.bfloat16), "mp", axis=0, tiled=True)
    left_terms = jnp.einsum(
        "kmn,knr->kmr", compensated, right_init, preferred_element_type=jnp.float32
    )
    replicas = lax.axis_size("replica")
    vector_len = vector_grads.shape[1]
    packed = jnp.concatenate([left_terms.reshape(-1), vector_grads[0]])
    lanes = 128
    rows = -(-packed.shape[0] // (replicas * 8 * lanes)) * 8
    packed = jnp.pad(packed, (0, replicas * rows * lanes - packed.shape[0]))
    packed = allreduce_replica(packed.reshape(replicas, rows, lanes), 0).reshape(-1)
    left_sum = packed[: left_terms.size].reshape(left_terms.shape)
    vector_total = packed[left_terms.size : left_terms.size + vector_len]
    left_rows = jnp.einsum("kmr,krs->kms", left_sum, gram_root, precision=highest).astype(
        jnp.bfloat16
    )
    owners_count = lax.axis_size("mp")
    right_terms = jnp.einsum(
        "kmn,kms->ksn", compensated, left_rows, preferred_element_type=jnp.float32
    )
    right_slots = right_terms.reshape(owners_count, -1, right_terms.shape[2])
    right_part = jnp.sum(
        exchange(right_slots.astype(jnp.bfloat16), "mp", 1).astype(jnp.float32), axis=0
    )
    part_shape = right_part.shape
    right_part = right_part.reshape(replicas, -1, lanes)
    right_part = allreduce_replica(right_part, 2)
    right_part = right_part.reshape(part_shape).astype(jnp.bfloat16)
    right_new = exchange(
        jnp.broadcast_to(right_part, right_slots.shape), "mp", 4
    ).reshape(right_terms.shape)
    pairs = [
        (a * owners_count + b, b * owners_count + a)
        for a in range(replicas)
        for b in range(owners_count)
    ]
    left_block = lax.ppermute(left_rows, ("replica", "mp"), pairs)
    approx_rows = jnp.einsum(
        "kms,ksn->kmn", left_rows, right_new, preferred_element_type=jnp.float32
    )
    new_feedback = (compensated.astype(jnp.float32) - approx_rows).astype(jnp.bfloat16)
    scale = has.astype(jnp.float32)[:, None, None]
    left_chosen = left_block[chosen].astype(jnp.float32) * scale
    right_chosen = right_new[chosen].astype(jnp.float32) * scale
    approx_slots = jnp.einsum("cmr,crn->cmn", left_chosen, right_chosen, precision=highest)
    new_momentum = 0.9 * momentum[0] + approx_slots
    new_master = master_weights[0] - 0.1 * new_momentum
    block_approx = jnp.einsum(
        "kms,ksn->kmn", left_block, right_new, preferred_element_type=jnp.float32
    )
    new_weights = (
        jnp.take(weight_slots, slots, axis=0).astype(jnp.float32) - 0.1 * block_approx
    ).astype(jnp.bfloat16)
    new_vector_momentum = 0.9 * vector_momentum + vector_total
    new_vector_params = vector_params - 0.1 * new_vector_momentum
    return (
        new_feedback[None],
        new_momentum[None],
        new_master[None],
        new_weights,
        new_vector_momentum,
        new_vector_params,
    )


def solution(mesh):
    return jax.shard_map(
        per_device,
        mesh=mesh,
        in_specs=(
            P("replica", None, "mp", None),
            P("replica", None, "mp", None),
            P(),
            P(),
            P(),
            P("mp", None, "replica", None),
            P("mp", None, "replica", None),
            P("replica", "mp"),
            P("mp"),
            P("mp"),
        ),
        out_specs=(
            P("replica", None, "mp", None),
            P("mp", None, "replica", None),
            P("mp", None, "replica", None),
            P(None, "replica", None),
            P("mp"),
            P("mp"),
        ),
        check_vma=False,
    )
```

```python
import functools

import jax
import jax.numpy as jnp
from jax import lax
from jax.experimental import pallas as pl
from jax.experimental.pallas import tpu as pltpu
from jax.sharding import PartitionSpec as P

MESH_IDS = pl.DeviceIdType.MESH


def _exchange_kernel(n, axis, x_ref, o_ref, recv, send_sem, recv_sem):
    me = lax.axis_index(axis)
    here = [lax.axis_index("replica"), lax.axis_index("mp")]
    where = 0 if axis == "replica" else 1

    def device(peer):
        ids = list(here)
        ids[where] = peer
        return tuple(ids)

    barrier = pltpu.get_barrier_semaphore()
    for d in range(1, n):
        peer = lax.rem(me + d, n)
        pl.semaphore_signal(barrier, inc=1, device_id=device(peer), device_id_type=MESH_IDS)
    pl.semaphore_wait(barrier, n - 1)
    copies = []
    for d in range(1, n):
        peer = lax.rem(me + d, n)
        copy = pltpu.make_async_remote_copy(
            src_ref=x_ref.at[peer],
            dst_ref=recv.at[me],
            send_sem=send_sem.at[d],
            recv_sem=recv_sem.at[me],
            device_id=device(peer),
            device_id_type=MESH_IDS,
        )
        copy.start()
        copies.append(copy)
    recv[me] = x_ref[me]
    for d in range(1, n):
        source = lax.rem(me + n - d, n)
        pltpu.make_async_remote_copy(
            src_ref=x_ref.at[source],
            dst_ref=recv.at[source],
            send_sem=send_sem.at[d],
            recv_sem=recv_sem.at[source],
            device_id=device(source),
            device_id_type=MESH_IDS,
        ).wait_recv()
    for copy in copies:
        copy.wait_send()
    o_ref[...] = recv[...]


def exchange(x, axis, cid):
    n = x.shape[0]
    return pl.pallas_call(
        functools.partial(_exchange_kernel, n, axis),
        out_shape=jax.ShapeDtypeStruct(x.shape, x.dtype),
        in_specs=[pl.BlockSpec(memory_space=pltpu.VMEM)],
        out_specs=pl.BlockSpec(memory_space=pltpu.VMEM),
        scratch_shapes=[
            pltpu.VMEM(x.shape, x.dtype),
            pltpu.SemaphoreType.DMA((n,)),
            pltpu.SemaphoreType.DMA((n,)),
        ],
        compiler_params=pltpu.CompilerParams(
            collective_id=cid, has_side_effects=True, vmem_limit_bytes=48 * 1024 * 1024
        ),
    )(x)


def _allreduce_kernel(n, x_ref, o_ref, first, middle, second, send_sem, recv_sem):
    me = lax.axis_index("replica")
    mp = lax.axis_index("mp")
    barrier = pltpu.get_barrier_semaphore()
    for d in range(1, n):
        peer = lax.rem(me + d, n)
        pl.semaphore_signal(barrier, inc=1, device_id=(peer, mp), device_id_type=MESH_IDS)
    pl.semaphore_wait(barrier, n - 1)

    def round_trip(phase, source_of, landing):
        copies = []
        for d in range(1, n):
            peer = lax.rem(me + d, n)
            copy = pltpu.make_async_remote_copy(
                src_ref=source_of(peer),
                dst_ref=landing.at[me],
                send_sem=send_sem.at[phase, d],
                recv_sem=recv_sem.at[phase, me],
                device_id=(peer, mp),
                device_id_type=MESH_IDS,
            )
            copy.start()
            copies.append(copy)
        landing[me] = source_of(me)[...]
        for d in range(1, n):
            source = lax.rem(me + n - d, n)
            pltpu.make_async_remote_copy(
                src_ref=source_of(source),
                dst_ref=landing.at[source],
                send_sem=send_sem.at[phase, d],
                recv_sem=recv_sem.at[phase, source],
                device_id=(source, mp),
                device_id_type=MESH_IDS,
            ).wait_recv()
        for copy in copies:
            copy.wait_send()

    round_trip(0, lambda peer: x_ref.at[peer], first)
    total = first[0]
    for s in range(1, n):
        total = total + first[s]
    middle[...] = total
    round_trip(1, lambda peer: middle, second)
    o_ref[...] = second[...]


def allreduce_replica(x, cid):
    n = x.shape[0]
    return pl.pallas_call(
        functools.partial(_allreduce_kernel, n),
        out_shape=jax.ShapeDtypeStruct(x.shape, x.dtype),
        in_specs=[pl.BlockSpec(memory_space=pltpu.VMEM)],
        out_specs=pl.BlockSpec(memory_space=pltpu.VMEM),
        scratch_shapes=[
            pltpu.VMEM(x.shape, x.dtype),
            pltpu.VMEM(x.shape[1:], x.dtype),
            pltpu.VMEM(x.shape, x.dtype),
            pltpu.SemaphoreType.DMA((2, n)),
            pltpu.SemaphoreType.DMA((2, n)),
        ],
        compiler_params=pltpu.CompilerParams(collective_id=cid, has_side_effects=True),
    )(x)


def _weights_kernel(slots_ref, base_ref, left_ref, right_ref, o_ref):
    del slots_ref
    approx = jnp.dot(left_ref[0], right_ref[0], preferred_element_type=jnp.float32)
    o_ref[0] = (base_ref[0].astype(jnp.float32) - 0.1 * approx).astype(o_ref.dtype)


def weights_of(slots, base, left, right):
    matrices, rows, _ = left.shape
    columns = right.shape[2]
    return pl.pallas_call(
        _weights_kernel,
        out_shape=jax.ShapeDtypeStruct((matrices, rows, columns), base.dtype),
        grid_spec=pltpu.PrefetchScalarGridSpec(
            num_scalar_prefetch=1,
            grid=(matrices,),
            in_specs=[
                pl.BlockSpec((1, rows, columns), lambda k, slot: (slot[k], 0, 0)),
                pl.BlockSpec((1, rows, left.shape[2]), lambda k, slot: (k, 0, 0)),
                pl.BlockSpec((1, right.shape[1], columns), lambda k, slot: (k, 0, 0)),
            ],
            out_specs=pl.BlockSpec((1, rows, columns), lambda k, slot: (k, 0, 0)),
        ),
    )(slots, base, left, right)


def per_device(
    gradients,
    feedback,
    right_init,
    gram_root,
    owners,
    momentum,
    master_weights,
    vector_grads,
    vector_momentum,
    vector_params,
):
    highest = lax.Precision.HIGHEST
    compensated = (gradients[0].astype(jnp.float32) + feedback[0].astype(jnp.float32)).astype(
        jnp.bfloat16
    )
    owner_count = lax.axis_size("mp")
    capacity = momentum.shape[1]
    matrices = owners.shape[0]
    replica_rows = momentum.shape[2]
    mp_index = lax.axis_index("mp")
    replica_index = lax.axis_index("replica")
    same_owner = owners[:, None] == owners[None, :]
    earlier = jnp.arange(matrices)[:, None] < jnp.arange(matrices)[None, :]
    ranks = jnp.sum((same_owner & earlier).astype(jnp.int32), axis=0)
    slots = owners * capacity + ranks
    mine = slots[None, :] == (mp_index * capacity + jnp.arange(capacity))[:, None]
    has = jnp.any(mine, axis=1)
    chosen = jnp.argmax(mine, axis=1)
    weight_base = master_weights[0] - 0.1 * (0.9 * momentum[0])
    weight_slots = lax.all_gather(weight_base.astype(jnp.bfloat16), "mp", axis=0, tiled=True)
    left_terms = jnp.einsum(
        "kmn,knr->kmr", compensated, right_init, preferred_element_type=jnp.float32
    )
    replicas = lax.axis_size("replica")
    vector_len = vector_grads.shape[1]
    packed = jnp.concatenate([left_terms.reshape(-1), vector_grads[0]])
    lanes = 128
    rows = -(-packed.shape[0] // (replicas * 8 * lanes)) * 8
    packed = jnp.pad(packed, (0, replicas * rows * lanes - packed.shape[0]))
    packed = allreduce_replica(packed.reshape(replicas, rows, lanes), 0).reshape(-1)
    left_sum = packed[: left_terms.size].reshape(left_terms.shape)
    vector_total = packed[left_terms.size : left_terms.size + vector_len]
    left_rows = jnp.einsum("kmr,krs->kms", left_sum, gram_root, precision=highest).astype(
        jnp.bfloat16
    )
    owners_count = lax.axis_size("mp")
    right_terms = jnp.einsum(
        "kmn,kms->ksn", compensated, left_rows, preferred_element_type=jnp.float32
    )
    right_slots = right_terms.reshape(owners_count, -1, right_terms.shape[2])
    right_part = jnp.sum(
        exchange(right_slots.astype(jnp.bfloat16), "mp", 1).astype(jnp.float32), axis=0
    )
    part_shape = right_part.shape
    right_part = right_part.reshape(replicas, -1, lanes)
    right_part = allreduce_replica(right_part, 2)
    right_part = right_part.reshape(part_shape).astype(jnp.bfloat16)
    right_new = exchange(
        jnp.broadcast_to(right_part, right_slots.shape), "mp", 4
    ).reshape(right_terms.shape)
    pairs = [
        (a * owners_count + b, b * owners_count + a)
        for a in range(replicas)
        for b in range(owners_count)
    ]
    left_block = lax.ppermute(left_rows, ("replica", "mp"), pairs)
    approx_rows = jnp.einsum(
        "kms,ksn->kmn", left_rows, right_new, preferred_element_type=jnp.float32
    )
    new_feedback = (compensated.astype(jnp.float32) - approx_rows).astype(jnp.bfloat16)
    scale = has.astype(jnp.float32)[:, None, None]
    left_chosen = left_block[chosen].astype(jnp.float32) * scale
    right_chosen = right_new[chosen].astype(jnp.float32) * scale
    approx_slots = jnp.einsum("cmr,crn->cmn", left_chosen, right_chosen, precision=highest)
    new_momentum = 0.9 * momentum[0] + approx_slots
    new_master = master_weights[0] - 0.1 * new_momentum
    new_weights = weights_of(slots, weight_slots, left_block, right_new)
    new_vector_momentum = 0.9 * vector_momentum + vector_total
    new_vector_params = vector_params - 0.1 * new_vector_momentum
    return (
        new_feedback[None],
        new_momentum[None],
        new_master[None],
        new_weights,
        new_vector_momentum,
        new_vector_params,
    )


def solution(mesh):
    return jax.shard_map(
        per_device,
        mesh=mesh,
        in_specs=(
            P("replica", None, "mp", None),
            P("replica", None, "mp", None),
            P(),
            P(),
            P(),
            P("mp", None, "replica", None),
            P("mp", None, "replica", None),
            P("replica", "mp"),
            P("mp"),
            P("mp"),
        ),
        out_specs=(
            P("replica", None, "mp", None),
            P("mp", None, "replica", None),
            P("mp", None, "replica", None),
            P(None, "replica", None),
            P("mp"),
            P("mp"),
        ),
        check_vma=False,
    )
```

```python
import functools

import jax
import jax.numpy as jnp
from jax import lax
from jax.experimental import pallas as pl
from jax.experimental.pallas import tpu as pltpu
from jax.sharding import PartitionSpec as P

MESH_IDS = pl.DeviceIdType.MESH


def _exchange_kernel(n, axis, stride, x_ref, o_ref, recv, send_sem, recv_sem):
    rank = lax.axis_index(axis)
    me = lax.rem(lax.div(rank, stride), n)
    first = rank - me * stride
    here = [lax.axis_index("replica"), lax.axis_index("mp")]
    where = 0 if axis == "replica" else 1

    def device(peer):
        ids = list(here)
        ids[where] = first + peer * stride
        return tuple(ids)

    barrier = pltpu.get_barrier_semaphore()
    for d in range(1, n):
        peer = lax.rem(me + d, n)
        pl.semaphore_signal(barrier, inc=1, device_id=device(peer), device_id_type=MESH_IDS)
    pl.semaphore_wait(barrier, n - 1)
    copies = []
    for d in range(1, n):
        peer = lax.rem(me + d, n)
        copy = pltpu.make_async_remote_copy(
            src_ref=x_ref.at[peer],
            dst_ref=recv.at[me],
            send_sem=send_sem.at[d],
            recv_sem=recv_sem.at[me],
            device_id=device(peer),
            device_id_type=MESH_IDS,
        )
        copy.start()
        copies.append(copy)
    recv[me] = x_ref[me]
    for d in range(1, n):
        source = lax.rem(me + n - d, n)
        pltpu.make_async_remote_copy(
            src_ref=x_ref.at[source],
            dst_ref=recv.at[source],
            send_sem=send_sem.at[d],
            recv_sem=recv_sem.at[source],
            device_id=device(source),
            device_id_type=MESH_IDS,
        ).wait_recv()
    for copy in copies:
        copy.wait_send()
    o_ref[...] = recv[...]


def exchange(x, axis, cid, stride=1):
    n = x.shape[0]
    return pl.pallas_call(
        functools.partial(_exchange_kernel, n, axis, stride),
        out_shape=jax.ShapeDtypeStruct(x.shape, x.dtype),
        in_specs=[pl.BlockSpec(memory_space=pltpu.VMEM)],
        out_specs=pl.BlockSpec(memory_space=pltpu.VMEM),
        scratch_shapes=[
            pltpu.VMEM(x.shape, x.dtype),
            pltpu.SemaphoreType.DMA((n,)),
            pltpu.SemaphoreType.DMA((n,)),
        ],
        compiler_params=pltpu.CompilerParams(
            collective_id=cid, has_side_effects=True, vmem_limit_bytes=48 * 1024 * 1024
        ),
    )(x)


def _allreduce_kernel(n, stride, x_ref, o_ref, first, middle, second, send_sem, recv_sem):
    rank = lax.axis_index("replica")
    me = lax.rem(lax.div(rank, stride), n)
    base = rank - me * stride
    mp = lax.axis_index("mp")

    def device(peer):
        return (base + peer * stride, mp)

    barrier = pltpu.get_barrier_semaphore()
    for d in range(1, n):
        peer = lax.rem(me + d, n)
        pl.semaphore_signal(barrier, inc=1, device_id=device(peer), device_id_type=MESH_IDS)
    pl.semaphore_wait(barrier, n - 1)

    def round_trip(phase, source_of, landing):
        copies = []
        for d in range(1, n):
            peer = lax.rem(me + d, n)
            copy = pltpu.make_async_remote_copy(
                src_ref=source_of(peer),
                dst_ref=landing.at[me],
                send_sem=send_sem.at[phase, d],
                recv_sem=recv_sem.at[phase, me],
                device_id=device(peer),
                device_id_type=MESH_IDS,
            )
            copy.start()
            copies.append(copy)
        landing[me] = source_of(me)[...]
        for d in range(1, n):
            source = lax.rem(me + n - d, n)
            pltpu.make_async_remote_copy(
                src_ref=source_of(source),
                dst_ref=landing.at[source],
                send_sem=send_sem.at[phase, d],
                recv_sem=recv_sem.at[phase, source],
                device_id=device(source),
                device_id_type=MESH_IDS,
            ).wait_recv()
        for copy in copies:
            copy.wait_send()

    round_trip(0, lambda peer: x_ref.at[peer], first)
    total = first[0]
    for s in range(1, n):
        total = total + first[s]
    middle[...] = total
    round_trip(1, lambda peer: middle, second)
    o_ref[...] = second[...]


def allreduce_replica(x, cid, stride=1):
    n = x.shape[0]
    return pl.pallas_call(
        functools.partial(_allreduce_kernel, n, stride),
        out_shape=jax.ShapeDtypeStruct(x.shape, x.dtype),
        in_specs=[pl.BlockSpec(memory_space=pltpu.VMEM)],
        out_specs=pl.BlockSpec(memory_space=pltpu.VMEM),
        scratch_shapes=[
            pltpu.VMEM(x.shape, x.dtype),
            pltpu.VMEM(x.shape[1:], x.dtype),
            pltpu.VMEM(x.shape, x.dtype),
            pltpu.SemaphoreType.DMA((2, n)),
            pltpu.SemaphoreType.DMA((2, n)),
        ],
        compiler_params=pltpu.CompilerParams(collective_id=cid, has_side_effects=True),
    )(x)


def per_device(
    gradients,
    feedback,
    right_init,
    gram_root,
    owners,
    momentum,
    master_weights,
    vector_grads,
    vector_momentum,
    vector_params,
):
    highest = lax.Precision.HIGHEST
    compensated = (gradients[0].astype(jnp.float32) + feedback[0].astype(jnp.float32)).astype(
        jnp.bfloat16
    )
    owner_count = lax.axis_size("mp")
    capacity = momentum.shape[1]
    matrices = owners.shape[0]
    replica_rows = momentum.shape[2]
    mp_index = lax.axis_index("mp")
    replica_index = lax.axis_index("replica")
    same_owner = owners[:, None] == owners[None, :]
    earlier = jnp.arange(matrices)[:, None] < jnp.arange(matrices)[None, :]
    ranks = jnp.sum((same_owner & earlier).astype(jnp.int32), axis=0)
    slots = owners * capacity + ranks
    mine = slots[None, :] == (mp_index * capacity + jnp.arange(capacity))[:, None]
    has = jnp.any(mine, axis=1)
    chosen = jnp.argmax(mine, axis=1)
    weight_base = master_weights[0] - 0.1 * (0.9 * momentum[0])
    weight_slots = lax.all_gather(weight_base.astype(jnp.bfloat16), "mp", axis=0, tiled=True)
    left_terms = jnp.einsum(
        "kmn,knr->kmr", compensated, right_init, preferred_element_type=jnp.float32
    )
    replicas = lax.axis_size("replica")
    vector_len = vector_grads.shape[1]
    packed = jnp.concatenate([left_terms.reshape(-1), vector_grads[0]])
    lanes = 128
    rows = -(-packed.shape[0] // (replicas * 8 * lanes)) * 8
    packed = jnp.pad(packed, (0, replicas * rows * lanes - packed.shape[0]))
    packed = allreduce_replica(packed.reshape(replicas, rows, lanes), 0).reshape(-1)
    left_sum = packed[: left_terms.size].reshape(left_terms.shape)
    vector_total = packed[left_terms.size : left_terms.size + vector_len]
    left_rows = jnp.einsum("kmr,krs->kms", left_sum, gram_root, precision=highest).astype(
        jnp.bfloat16
    )
    owners_count = lax.axis_size("mp")
    cores = 2
    chips = replicas // cores
    pieces = owners_count // (matrices // cores)
    width = compensated.shape[2] // pieces
    right_terms = jnp.einsum(
        "kmjn,kms->kjsn",
        compensated.reshape(matrices, -1, pieces, width),
        left_rows,
        preferred_element_type=jnp.float32,
    )
    right_terms = right_terms.reshape(cores, owners_count, -1, width)
    right_half = jnp.sum(exchange(right_terms, "replica", 1), axis=0)
    right_part = jnp.sum(
        exchange(right_half.astype(jnp.bfloat16), "mp", 2).astype(jnp.float32), axis=0
    )
    part_shape = right_part.shape
    right_part = allreduce_replica(right_part.reshape(chips, -1, lanes), 3, cores)
    right_part = right_part.reshape(part_shape).astype(jnp.bfloat16)
    right_half = exchange(jnp.broadcast_to(right_part, right_half.shape), "mp", 4)
    right_new = exchange(jnp.broadcast_to(right_half, right_terms.shape), "replica", 5)
    right_new = right_new.reshape(matrices, pieces, -1, width).transpose(0, 2, 1, 3)
    right_new = right_new.reshape(matrices, -1, compensated.shape[2])
    pairs = [
        (a * owners_count + b, b * owners_count + a)
        for a in range(replicas)
        for b in range(owners_count)
    ]
    left_block = lax.ppermute(left_rows, ("replica", "mp"), pairs)
    approx_rows = jnp.einsum(
        "kms,ksn->kmn", left_rows, right_new, preferred_element_type=jnp.float32
    )
    new_feedback = (compensated.astype(jnp.float32) - approx_rows).astype(jnp.bfloat16)
    scale = has.astype(jnp.float32)[:, None, None]
    left_chosen = left_block[chosen].astype(jnp.float32) * scale
    right_chosen = right_new[chosen].astype(jnp.float32) * scale
    approx_slots = jnp.einsum("cmr,crn->cmn", left_chosen, right_chosen, precision=highest)
    new_momentum = 0.9 * momentum[0] + approx_slots
    new_master = master_weights[0] - 0.1 * new_momentum
    block_approx = jnp.einsum(
        "kms,ksn->kmn", left_block, right_new, preferred_element_type=jnp.float32
    )
    new_weights = (
        jnp.take(weight_slots, slots, axis=0).astype(jnp.float32) - 0.1 * block_approx
    ).astype(jnp.bfloat16)
    new_vector_momentum = 0.9 * vector_momentum + vector_total
    new_vector_params = vector_params - 0.1 * new_vector_momentum
    return (
        new_feedback[None],
        new_momentum[None],
        new_master[None],
        new_weights,
        new_vector_momentum,
        new_vector_params,
    )


def solution(mesh):
    return jax.shard_map(
        per_device,
        mesh=mesh,
        in_specs=(
            P("replica", None, "mp", None),
            P("replica", None, "mp", None),
            P(),
            P(),
            P(),
            P("mp", None, "replica", None),
            P("mp", None, "replica", None),
            P("replica", "mp"),
            P("mp"),
            P("mp"),
        ),
        out_specs=(
            P("replica", None, "mp", None),
            P("mp", None, "replica", None),
            P("mp", None, "replica", None),
            P(None, "replica", None),
            P("mp"),
            P("mp"),
        ),
        check_vma=False,
    )
```

```python
import functools

import jax
import jax.numpy as jnp
from jax import lax
from jax.experimental import pallas as pl
from jax.experimental.pallas import tpu as pltpu
from jax.sharding import PartitionSpec as P

MESH_IDS = pl.DeviceIdType.MESH


def _exchange_kernel(n, axis, stride, x_ref, o_ref, recv, send_sem, recv_sem):
    rank = lax.axis_index(axis)
    me = lax.rem(lax.div(rank, stride), n)
    first = rank - me * stride
    here = [lax.axis_index("replica"), lax.axis_index("mp")]
    where = 0 if axis == "replica" else 1

    def device(peer):
        ids = list(here)
        ids[where] = first + peer * stride
        return tuple(ids)

    barrier = pltpu.get_barrier_semaphore()
    for d in range(1, n):
        peer = lax.rem(me + d, n)
        pl.semaphore_signal(barrier, inc=1, device_id=device(peer), device_id_type=MESH_IDS)
    pl.semaphore_wait(barrier, n - 1)
    copies = []
    for d in range(1, n):
        peer = lax.rem(me + d, n)
        copy = pltpu.make_async_remote_copy(
            src_ref=x_ref.at[peer],
            dst_ref=recv.at[me],
            send_sem=send_sem.at[d],
            recv_sem=recv_sem.at[me],
            device_id=device(peer),
            device_id_type=MESH_IDS,
        )
        copy.start()
        copies.append(copy)
    recv[me] = x_ref[me]
    for d in range(1, n):
        source = lax.rem(me + n - d, n)
        pltpu.make_async_remote_copy(
            src_ref=x_ref.at[source],
            dst_ref=recv.at[source],
            send_sem=send_sem.at[d],
            recv_sem=recv_sem.at[source],
            device_id=device(source),
            device_id_type=MESH_IDS,
        ).wait_recv()
    for copy in copies:
        copy.wait_send()
    o_ref[...] = recv[...]


def exchange(x, axis, cid, stride=1):
    n = x.shape[0]
    return pl.pallas_call(
        functools.partial(_exchange_kernel, n, axis, stride),
        out_shape=jax.ShapeDtypeStruct(x.shape, x.dtype),
        in_specs=[pl.BlockSpec(memory_space=pltpu.VMEM)],
        out_specs=pl.BlockSpec(memory_space=pltpu.VMEM),
        scratch_shapes=[
            pltpu.VMEM(x.shape, x.dtype),
            pltpu.SemaphoreType.DMA((n,)),
            pltpu.SemaphoreType.DMA((n,)),
        ],
        compiler_params=pltpu.CompilerParams(
            collective_id=cid, has_side_effects=True, vmem_limit_bytes=48 * 1024 * 1024
        ),
    )(x)


def _allreduce_kernel(n, stride, x_ref, o_ref, first, middle, second, send_sem, recv_sem):
    rank = lax.axis_index("replica")
    me = lax.rem(lax.div(rank, stride), n)
    base = rank - me * stride
    mp = lax.axis_index("mp")

    def device(peer):
        return (base + peer * stride, mp)

    barrier = pltpu.get_barrier_semaphore()
    for d in range(1, n):
        peer = lax.rem(me + d, n)
        pl.semaphore_signal(barrier, inc=1, device_id=device(peer), device_id_type=MESH_IDS)
    pl.semaphore_wait(barrier, n - 1)

    def round_trip(phase, source_of, landing):
        copies = []
        for d in range(1, n):
            peer = lax.rem(me + d, n)
            copy = pltpu.make_async_remote_copy(
                src_ref=source_of(peer),
                dst_ref=landing.at[me],
                send_sem=send_sem.at[phase, d],
                recv_sem=recv_sem.at[phase, me],
                device_id=device(peer),
                device_id_type=MESH_IDS,
            )
            copy.start()
            copies.append(copy)
        landing[me] = source_of(me)[...]
        for d in range(1, n):
            source = lax.rem(me + n - d, n)
            pltpu.make_async_remote_copy(
                src_ref=source_of(source),
                dst_ref=landing.at[source],
                send_sem=send_sem.at[phase, d],
                recv_sem=recv_sem.at[phase, source],
                device_id=device(source),
                device_id_type=MESH_IDS,
            ).wait_recv()
        for copy in copies:
            copy.wait_send()

    round_trip(0, lambda peer: x_ref.at[peer], first)
    total = first[0]
    for s in range(1, n):
        total = total + first[s]
    middle[...] = total
    round_trip(1, lambda peer: middle, second)
    o_ref[...] = second[...]


def allreduce_replica(x, cid, stride=1):
    n = x.shape[0]
    return pl.pallas_call(
        functools.partial(_allreduce_kernel, n, stride),
        out_shape=jax.ShapeDtypeStruct(x.shape, x.dtype),
        in_specs=[pl.BlockSpec(memory_space=pltpu.VMEM)],
        out_specs=pl.BlockSpec(memory_space=pltpu.VMEM),
        scratch_shapes=[
            pltpu.VMEM(x.shape, x.dtype),
            pltpu.VMEM(x.shape[1:], x.dtype),
            pltpu.VMEM(x.shape, x.dtype),
            pltpu.SemaphoreType.DMA((2, n)),
            pltpu.SemaphoreType.DMA((2, n)),
        ],
        compiler_params=pltpu.CompilerParams(collective_id=cid, has_side_effects=True),
    )(x)


def per_device(
    gradients,
    feedback,
    right_init,
    gram_root,
    owners,
    momentum,
    master_weights,
    vector_grads,
    vector_momentum,
    vector_params,
):
    highest = lax.Precision.HIGHEST
    compensated = (gradients[0].astype(jnp.float32) + feedback[0].astype(jnp.float32)).astype(
        jnp.bfloat16
    )
    owner_count = lax.axis_size("mp")
    capacity = momentum.shape[1]
    matrices = owners.shape[0]
    replica_rows = momentum.shape[2]
    mp_index = lax.axis_index("mp")
    replica_index = lax.axis_index("replica")
    same_owner = owners[:, None] == owners[None, :]
    earlier = jnp.arange(matrices)[:, None] < jnp.arange(matrices)[None, :]
    ranks = jnp.sum((same_owner & earlier).astype(jnp.int32), axis=0)
    slots = owners * capacity + ranks
    mine = slots[None, :] == (mp_index * capacity + jnp.arange(capacity))[:, None]
    has = jnp.any(mine, axis=1)
    chosen = jnp.argmax(mine, axis=1)
    weight_base = master_weights[0] - 0.1 * (0.9 * momentum[0])
    weight_slots = lax.all_gather(weight_base.astype(jnp.bfloat16), "mp", axis=0, tiled=True)
    left_terms = jnp.einsum(
        "kmn,knr->kmr", compensated, right_init, preferred_element_type=jnp.float32
    )
    replicas = lax.axis_size("replica")
    vector_len = vector_grads.shape[1]
    packed = jnp.concatenate([left_terms.reshape(-1), vector_grads[0]])
    lanes = 128
    rows = -(-packed.shape[0] // (replicas * 8 * lanes)) * 8
    packed = jnp.pad(packed, (0, replicas * rows * lanes - packed.shape[0]))
    packed = allreduce_replica(packed.reshape(replicas, rows, lanes), 0).reshape(-1)
    left_sum = packed[: left_terms.size].reshape(left_terms.shape)
    vector_total = packed[left_terms.size : left_terms.size + vector_len]
    left_rows = jnp.einsum("kmr,krs->kms", left_sum, gram_root, precision=highest).astype(
        jnp.bfloat16
    )
    owners_count = lax.axis_size("mp")
    cores = 2
    chips = replicas // cores
    pieces = owners_count // (matrices // cores)
    width = compensated.shape[2] // pieces
    right_terms = jnp.einsum(
        "kmn,kms->ksn", compensated, left_rows, preferred_element_type=jnp.float32
    )
    right_terms = right_terms.reshape(matrices, -1, pieces, width).transpose(0, 2, 1, 3)
    right_terms = right_terms.astype(jnp.bfloat16).reshape(cores, owners_count, -1, width)
    right_half = jnp.sum(exchange(right_terms, "replica", 1).astype(jnp.float32), axis=0)
    right_part = jnp.sum(
        exchange(right_half.astype(jnp.bfloat16), "mp", 2).astype(jnp.float32), axis=0
    )
    part_shape = right_part.shape
    right_part = allreduce_replica(right_part.reshape(chips, -1, lanes), 3, cores)
    right_part = right_part.reshape(part_shape).astype(jnp.bfloat16)
    right_half = exchange(jnp.broadcast_to(right_part, right_half.shape), "mp", 4)
    right_new = exchange(jnp.broadcast_to(right_half, right_terms.shape), "replica", 5)
    right_new = right_new.reshape(matrices, pieces, -1, width).transpose(0, 2, 1, 3)
    right_new = right_new.reshape(matrices, -1, compensated.shape[2])
    pairs = [
        (a * owners_count + b, b * owners_count + a)
        for a in range(replicas)
        for b in range(owners_count)
    ]
    left_block = lax.ppermute(left_rows, ("replica", "mp"), pairs)
    approx_rows = jnp.einsum(
        "kms,ksn->kmn", left_rows, right_new, preferred_element_type=jnp.float32
    )
    new_feedback = (compensated.astype(jnp.float32) - approx_rows).astype(jnp.bfloat16)
    scale = has.astype(jnp.float32)[:, None, None]
    left_chosen = left_block[chosen].astype(jnp.float32) * scale
    right_chosen = right_new[chosen].astype(jnp.float32) * scale
    approx_slots = jnp.einsum("cmr,crn->cmn", left_chosen, right_chosen, precision=highest)
    new_momentum = 0.9 * momentum[0] + approx_slots
    new_master = master_weights[0] - 0.1 * new_momentum
    block_approx = jnp.einsum(
        "kms,ksn->kmn", left_block, right_new, preferred_element_type=jnp.float32
    )
    new_weights = (
        jnp.take(weight_slots, slots, axis=0).astype(jnp.float32) - 0.1 * block_approx
    ).astype(jnp.bfloat16)
    new_vector_momentum = 0.9 * vector_momentum + vector_total
    new_vector_params = vector_params - 0.1 * new_vector_momentum
    return (
        new_feedback[None],
        new_momentum[None],
        new_master[None],
        new_weights,
        new_vector_momentum,
        new_vector_params,
    )


def solution(mesh):
    return jax.shard_map(
        per_device,
        mesh=mesh,
        in_specs=(
            P("replica", None, "mp", None),
            P("replica", None, "mp", None),
            P(),
            P(),
            P(),
            P("mp", None, "replica", None),
            P("mp", None, "replica", None),
            P("replica", "mp"),
            P("mp"),
            P("mp"),
        ),
        out_specs=(
            P("replica", None, "mp", None),
            P("mp", None, "replica", None),
            P("mp", None, "replica", None),
            P(None, "replica", None),
            P("mp"),
            P("mp"),
        ),
        check_vma=False,
    )
```

```python
import functools

import jax
import jax.numpy as jnp
from jax import lax
from jax.experimental import pallas as pl
from jax.experimental.pallas import tpu as pltpu
from jax.sharding import PartitionSpec as P

MESH_IDS = pl.DeviceIdType.MESH


def _exchange_kernel(n, axis, stride, total, x_ref, o_ref, recv, send_sem, recv_sem):
    rank = lax.axis_index(axis)
    me = lax.rem(lax.div(rank, stride), n)
    first = rank - me * stride
    here = [lax.axis_index("replica"), lax.axis_index("mp")]
    where = 0 if axis == "replica" else 1

    def device(peer):
        ids = list(here)
        ids[where] = first + peer * stride
        return tuple(ids)

    barrier = pltpu.get_barrier_semaphore()
    for d in range(1, n):
        peer = lax.rem(me + d, n)
        pl.semaphore_signal(barrier, inc=1, device_id=device(peer), device_id_type=MESH_IDS)
    pl.semaphore_wait(barrier, n - 1)
    copies = []
    for d in range(1, n):
        peer = lax.rem(me + d, n)
        copy = pltpu.make_async_remote_copy(
            src_ref=x_ref.at[peer],
            dst_ref=recv.at[me],
            send_sem=send_sem.at[d],
            recv_sem=recv_sem.at[me],
            device_id=device(peer),
            device_id_type=MESH_IDS,
        )
        copy.start()
        copies.append(copy)
    recv[me] = x_ref[me]
    for d in range(1, n):
        source = lax.rem(me + n - d, n)
        pltpu.make_async_remote_copy(
            src_ref=x_ref.at[source],
            dst_ref=recv.at[source],
            send_sem=send_sem.at[d],
            recv_sem=recv_sem.at[source],
            device_id=device(source),
            device_id_type=MESH_IDS,
        ).wait_recv()
    for copy in copies:
        copy.wait_send()
    if total is None:
        o_ref[...] = recv[...]
    else:
        acc = recv[0].astype(jnp.float32)
        for s in range(1, n):
            acc = acc + recv[s].astype(jnp.float32)
        o_ref[...] = acc.astype(o_ref.dtype)


def exchange(x, axis, cid, stride=1, total=None):
    n = x.shape[0]
    out = jax.ShapeDtypeStruct(x.shape, x.dtype) if total is None else jax.ShapeDtypeStruct(
        x.shape[1:], total
    )
    return pl.pallas_call(
        functools.partial(_exchange_kernel, n, axis, stride, total),
        out_shape=out,
        in_specs=[pl.BlockSpec(memory_space=pltpu.VMEM)],
        out_specs=pl.BlockSpec(memory_space=pltpu.VMEM),
        scratch_shapes=[
            pltpu.VMEM(x.shape, x.dtype),
            pltpu.SemaphoreType.DMA((n,)),
            pltpu.SemaphoreType.DMA((n,)),
        ],
        compiler_params=pltpu.CompilerParams(
            collective_id=cid, has_side_effects=True, vmem_limit_bytes=48 * 1024 * 1024
        ),
    )(x)


def _allreduce_kernel(n, stride, x_ref, o_ref, first, middle, second, send_sem, recv_sem):
    rank = lax.axis_index("replica")
    me = lax.rem(lax.div(rank, stride), n)
    base = rank - me * stride
    mp = lax.axis_index("mp")

    def device(peer):
        return (base + peer * stride, mp)

    barrier = pltpu.get_barrier_semaphore()
    for d in range(1, n):
        peer = lax.rem(me + d, n)
        pl.semaphore_signal(barrier, inc=1, device_id=device(peer), device_id_type=MESH_IDS)
    pl.semaphore_wait(barrier, n - 1)

    def round_trip(phase, source_of, landing):
        copies = []
        for d in range(1, n):
            peer = lax.rem(me + d, n)
            copy = pltpu.make_async_remote_copy(
                src_ref=source_of(peer),
                dst_ref=landing.at[me],
                send_sem=send_sem.at[phase, d],
                recv_sem=recv_sem.at[phase, me],
                device_id=device(peer),
                device_id_type=MESH_IDS,
            )
            copy.start()
            copies.append(copy)
        landing[me] = source_of(me)[...]
        for d in range(1, n):
            source = lax.rem(me + n - d, n)
            pltpu.make_async_remote_copy(
                src_ref=source_of(source),
                dst_ref=landing.at[source],
                send_sem=send_sem.at[phase, d],
                recv_sem=recv_sem.at[phase, source],
                device_id=device(source),
                device_id_type=MESH_IDS,
            ).wait_recv()
        for copy in copies:
            copy.wait_send()

    round_trip(0, lambda peer: x_ref.at[peer], first)
    total = first[0]
    for s in range(1, n):
        total = total + first[s]
    middle[...] = total
    round_trip(1, lambda peer: middle, second)
    o_ref[...] = second[...]


def allreduce_replica(x, cid, stride=1):
    n = x.shape[0]
    return pl.pallas_call(
        functools.partial(_allreduce_kernel, n, stride),
        out_shape=jax.ShapeDtypeStruct(x.shape, x.dtype),
        in_specs=[pl.BlockSpec(memory_space=pltpu.VMEM)],
        out_specs=pl.BlockSpec(memory_space=pltpu.VMEM),
        scratch_shapes=[
            pltpu.VMEM(x.shape, x.dtype),
            pltpu.VMEM(x.shape[1:], x.dtype),
            pltpu.VMEM(x.shape, x.dtype),
            pltpu.SemaphoreType.DMA((2, n)),
            pltpu.SemaphoreType.DMA((2, n)),
        ],
        compiler_params=pltpu.CompilerParams(collective_id=cid, has_side_effects=True),
    )(x)


def per_device(
    gradients,
    feedback,
    right_init,
    gram_root,
    owners,
    momentum,
    master_weights,
    vector_grads,
    vector_momentum,
    vector_params,
):
    highest = lax.Precision.HIGHEST
    compensated = (gradients[0].astype(jnp.float32) + feedback[0].astype(jnp.float32)).astype(
        jnp.bfloat16
    )
    owner_count = lax.axis_size("mp")
    capacity = momentum.shape[1]
    matrices = owners.shape[0]
    replica_rows = momentum.shape[2]
    mp_index = lax.axis_index("mp")
    replica_index = lax.axis_index("replica")
    same_owner = owners[:, None] == owners[None, :]
    earlier = jnp.arange(matrices)[:, None] < jnp.arange(matrices)[None, :]
    ranks = jnp.sum((same_owner & earlier).astype(jnp.int32), axis=0)
    slots = owners * capacity + ranks
    mine = slots[None, :] == (mp_index * capacity + jnp.arange(capacity))[:, None]
    has = jnp.any(mine, axis=1)
    chosen = jnp.argmax(mine, axis=1)
    weight_base = master_weights[0] - 0.1 * (0.9 * momentum[0])
    weight_slots = lax.all_gather(weight_base.astype(jnp.bfloat16), "mp", axis=0, tiled=True)
    left_terms = jnp.einsum(
        "kmn,knr->kmr", compensated, right_init, preferred_element_type=jnp.float32
    )
    replicas = lax.axis_size("replica")
    vector_len = vector_grads.shape[1]
    packed = jnp.concatenate([left_terms.reshape(-1), vector_grads[0]])
    lanes = 128
    rows = -(-packed.shape[0] // (replicas * 8 * lanes)) * 8
    packed = jnp.pad(packed, (0, replicas * rows * lanes - packed.shape[0]))
    packed = allreduce_replica(packed.reshape(replicas, rows, lanes), 0).reshape(-1)
    left_sum = packed[: left_terms.size].reshape(left_terms.shape)
    vector_total = packed[left_terms.size : left_terms.size + vector_len]
    left_rows = jnp.einsum("kmr,krs->kms", left_sum, gram_root, precision=highest).astype(
        jnp.bfloat16
    )
    owners_count = lax.axis_size("mp")
    cores = 2
    chips = replicas // cores
    pieces = owners_count // (matrices // cores)
    width = compensated.shape[2] // pieces
    right_terms = jnp.einsum(
        "kmn,kms->ksn", compensated, left_rows, preferred_element_type=jnp.float32
    )
    right_terms = right_terms.reshape(matrices, -1, pieces, width).transpose(0, 2, 1, 3)
    right_terms = right_terms.astype(jnp.bfloat16).reshape(cores, owners_count, -1, width)
    right_half = exchange(right_terms, "replica", 1, total=jnp.bfloat16)
    right_part = exchange(right_half, "mp", 2, total=jnp.float32)
    part_shape = right_part.shape
    right_part = allreduce_replica(right_part.reshape(chips, -1, lanes), 3, cores)
    right_part = right_part.reshape(part_shape).astype(jnp.bfloat16)
    right_half = exchange(jnp.broadcast_to(right_part, right_half.shape), "mp", 4)
    right_new = exchange(jnp.broadcast_to(right_half, right_terms.shape), "replica", 5)
    right_new = right_new.reshape(matrices, pieces, -1, width).transpose(0, 2, 1, 3)
    right_new = right_new.reshape(matrices, -1, compensated.shape[2])
    pairs = [
        (a * owners_count + b, b * owners_count + a)
        for a in range(replicas)
        for b in range(owners_count)
    ]
    left_block = lax.ppermute(left_rows, ("replica", "mp"), pairs)
    approx_rows = jnp.einsum(
        "kms,ksn->kmn", left_rows, right_new, preferred_element_type=jnp.float32
    )
    new_feedback = (compensated.astype(jnp.float32) - approx_rows).astype(jnp.bfloat16)
    scale = has.astype(jnp.float32)[:, None, None]
    left_chosen = left_block[chosen].astype(jnp.float32) * scale
    right_chosen = right_new[chosen].astype(jnp.float32) * scale
    approx_slots = jnp.einsum("cmr,crn->cmn", left_chosen, right_chosen, precision=highest)
    new_momentum = 0.9 * momentum[0] + approx_slots
    new_master = master_weights[0] - 0.1 * new_momentum
    block_approx = jnp.einsum(
        "kms,ksn->kmn", left_block, right_new, preferred_element_type=jnp.float32
    )
    new_weights = (
        jnp.take(weight_slots, slots, axis=0).astype(jnp.float32) - 0.1 * block_approx
    ).astype(jnp.bfloat16)
    new_vector_momentum = 0.9 * vector_momentum + vector_total
    new_vector_params = vector_params - 0.1 * new_vector_momentum
    return (
        new_feedback[None],
        new_momentum[None],
        new_master[None],
        new_weights,
        new_vector_momentum,
        new_vector_params,
    )


def solution(mesh):
    return jax.shard_map(
        per_device,
        mesh=mesh,
        in_specs=(
            P("replica", None, "mp", None),
            P("replica", None, "mp", None),
            P(),
            P(),
            P(),
            P("mp", None, "replica", None),
            P("mp", None, "replica", None),
            P("replica", "mp"),
            P("mp"),
            P("mp"),
        ),
        out_specs=(
            P("replica", None, "mp", None),
            P("mp", None, "replica", None),
            P("mp", None, "replica", None),
            P(None, "replica", None),
            P("mp"),
            P("mp"),
        ),
        check_vma=False,
    )
```

```python
import functools

import jax
import jax.numpy as jnp
from jax import lax
from jax.experimental import pallas as pl
from jax.experimental.pallas import tpu as pltpu
from jax.sharding import PartitionSpec as P

MESH_IDS = pl.DeviceIdType.MESH


def _exchange_kernel(n, axis, stride, total, x_ref, o_ref, recv, send_sem, recv_sem):
    rank = lax.axis_index(axis)
    me = lax.rem(lax.div(rank, stride), n)
    first = rank - me * stride
    here = [lax.axis_index("replica"), lax.axis_index("mp")]
    where = 0 if axis == "replica" else 1

    def device(peer):
        ids = list(here)
        ids[where] = first + peer * stride
        return tuple(ids)

    barrier = pltpu.get_barrier_semaphore()
    for d in range(1, n):
        peer = lax.rem(me + d, n)
        pl.semaphore_signal(barrier, inc=1, device_id=device(peer), device_id_type=MESH_IDS)
    pl.semaphore_wait(barrier, n - 1)
    copies = []
    for d in range(1, n):
        peer = lax.rem(me + d, n)
        copy = pltpu.make_async_remote_copy(
            src_ref=x_ref.at[peer],
            dst_ref=recv.at[me],
            send_sem=send_sem.at[d],
            recv_sem=recv_sem.at[me],
            device_id=device(peer),
            device_id_type=MESH_IDS,
        )
        copy.start()
        copies.append(copy)
    recv[me] = x_ref[me]
    for d in range(1, n):
        source = lax.rem(me + n - d, n)
        pltpu.make_async_remote_copy(
            src_ref=x_ref.at[source],
            dst_ref=recv.at[source],
            send_sem=send_sem.at[d],
            recv_sem=recv_sem.at[source],
            device_id=device(source),
            device_id_type=MESH_IDS,
        ).wait_recv()
    for copy in copies:
        copy.wait_send()
    if total is None:
        o_ref[...] = recv[...]
    else:
        acc = recv[0].astype(jnp.float32)
        for s in range(1, n):
            acc = acc + recv[s].astype(jnp.float32)
        o_ref[...] = acc.astype(o_ref.dtype)


def exchange(x, axis, cid, stride=1, total=None):
    n = x.shape[0]
    out = jax.ShapeDtypeStruct(x.shape, x.dtype) if total is None else jax.ShapeDtypeStruct(
        x.shape[1:], total
    )
    return pl.pallas_call(
        functools.partial(_exchange_kernel, n, axis, stride, total),
        out_shape=out,
        in_specs=[pl.BlockSpec(memory_space=pltpu.VMEM)],
        out_specs=pl.BlockSpec(memory_space=pltpu.VMEM),
        scratch_shapes=[
            pltpu.VMEM(x.shape, x.dtype),
            pltpu.SemaphoreType.DMA((n,)),
            pltpu.SemaphoreType.DMA((n,)),
        ],
        compiler_params=pltpu.CompilerParams(
            collective_id=cid, has_side_effects=True, vmem_limit_bytes=48 * 1024 * 1024
        ),
    )(x)


def _allreduce_kernel(n, stride, x_ref, o_ref, first, middle, second, send_sem, recv_sem):
    rank = lax.axis_index("replica")
    me = lax.rem(lax.div(rank, stride), n)
    base = rank - me * stride
    mp = lax.axis_index("mp")

    def device(peer):
        return (base + peer * stride, mp)

    barrier = pltpu.get_barrier_semaphore()
    for d in range(1, n):
        peer = lax.rem(me + d, n)
        pl.semaphore_signal(barrier, inc=1, device_id=device(peer), device_id_type=MESH_IDS)
    pl.semaphore_wait(barrier, n - 1)

    def round_trip(phase, source_of, landing):
        copies = []
        for d in range(1, n):
            peer = lax.rem(me + d, n)
            copy = pltpu.make_async_remote_copy(
                src_ref=source_of(peer),
                dst_ref=landing.at[me],
                send_sem=send_sem.at[phase, d],
                recv_sem=recv_sem.at[phase, me],
                device_id=device(peer),
                device_id_type=MESH_IDS,
            )
            copy.start()
            copies.append(copy)
        landing[me] = source_of(me)[...]
        for d in range(1, n):
            source = lax.rem(me + n - d, n)
            pltpu.make_async_remote_copy(
                src_ref=source_of(source),
                dst_ref=landing.at[source],
                send_sem=send_sem.at[phase, d],
                recv_sem=recv_sem.at[phase, source],
                device_id=device(source),
                device_id_type=MESH_IDS,
            ).wait_recv()
        for copy in copies:
            copy.wait_send()

    round_trip(0, lambda peer: x_ref.at[peer], first)
    total = first[0]
    for s in range(1, n):
        total = total + first[s]
    middle[...] = total
    round_trip(1, lambda peer: middle, second)
    o_ref[...] = second[...]


def allreduce_replica(x, cid, stride=1):
    n = x.shape[0]
    return pl.pallas_call(
        functools.partial(_allreduce_kernel, n, stride),
        out_shape=jax.ShapeDtypeStruct(x.shape, x.dtype),
        in_specs=[pl.BlockSpec(memory_space=pltpu.VMEM)],
        out_specs=pl.BlockSpec(memory_space=pltpu.VMEM),
        scratch_shapes=[
            pltpu.VMEM(x.shape, x.dtype),
            pltpu.VMEM(x.shape[1:], x.dtype),
            pltpu.VMEM(x.shape, x.dtype),
            pltpu.SemaphoreType.DMA((2, n)),
            pltpu.SemaphoreType.DMA((2, n)),
        ],
        compiler_params=pltpu.CompilerParams(collective_id=cid, has_side_effects=True),
    )(x)


def _weights_kernel(slots_ref, base_hbm, left_ref, right_ref, o_ref, bases, sems):
    matrices = left_ref.shape[0]
    copies = []
    for k in range(matrices):
        copy = pltpu.make_async_copy(base_hbm.at[slots_ref[k]], bases.at[k], sems.at[k])
        copy.start()
        copies.append(copy)
    for k in range(matrices):
        copies[k].wait()
        approx = jnp.dot(left_ref[k], right_ref[k], preferred_element_type=jnp.float32)
        o_ref[k] = (bases[k].astype(jnp.float32) - 0.1 * approx).astype(o_ref.dtype)


def weights_of(slots, base, left, right):
    matrices, rows, _ = left.shape
    shape = (matrices, rows, right.shape[2])
    return pl.pallas_call(
        _weights_kernel,
        out_shape=jax.ShapeDtypeStruct(shape, base.dtype),
        in_specs=[
            pl.BlockSpec(memory_space=pltpu.SMEM),
            pl.BlockSpec(memory_space=pl.ANY),
            pl.BlockSpec(memory_space=pltpu.VMEM),
            pl.BlockSpec(memory_space=pltpu.VMEM),
        ],
        out_specs=pl.BlockSpec(memory_space=pltpu.VMEM),
        scratch_shapes=[
            pltpu.VMEM(shape, base.dtype),
            pltpu.SemaphoreType.DMA((matrices,)),
        ],
        compiler_params=pltpu.CompilerParams(vmem_limit_bytes=32 * 1024 * 1024),
    )(slots, base, left, right)


def per_device(
    gradients,
    feedback,
    right_init,
    gram_root,
    owners,
    momentum,
    master_weights,
    vector_grads,
    vector_momentum,
    vector_params,
):
    highest = lax.Precision.HIGHEST
    compensated = (gradients[0].astype(jnp.float32) + feedback[0].astype(jnp.float32)).astype(
        jnp.bfloat16
    )
    owner_count = lax.axis_size("mp")
    capacity = momentum.shape[1]
    matrices = owners.shape[0]
    replica_rows = momentum.shape[2]
    mp_index = lax.axis_index("mp")
    replica_index = lax.axis_index("replica")
    same_owner = owners[:, None] == owners[None, :]
    earlier = jnp.arange(matrices)[:, None] < jnp.arange(matrices)[None, :]
    ranks = jnp.sum((same_owner & earlier).astype(jnp.int32), axis=0)
    slots = owners * capacity + ranks
    mine = slots[None, :] == (mp_index * capacity + jnp.arange(capacity))[:, None]
    has = jnp.any(mine, axis=1)
    chosen = jnp.argmax(mine, axis=1)
    weight_base = master_weights[0] - 0.1 * (0.9 * momentum[0])
    weight_slots = lax.all_gather(weight_base.astype(jnp.bfloat16), "mp", axis=0, tiled=True)
    left_terms = jnp.einsum(
        "kmn,knr->kmr", compensated, right_init, preferred_element_type=jnp.float32
    )
    replicas = lax.axis_size("replica")
    vector_len = vector_grads.shape[1]
    packed = jnp.concatenate([left_terms.reshape(-1), vector_grads[0]])
    lanes = 128
    rows = -(-packed.shape[0] // (replicas * 8 * lanes)) * 8
    packed = jnp.pad(packed, (0, replicas * rows * lanes - packed.shape[0]))
    packed = allreduce_replica(packed.reshape(replicas, rows, lanes), 0).reshape(-1)
    left_sum = packed[: left_terms.size].reshape(left_terms.shape)
    vector_total = packed[left_terms.size : left_terms.size + vector_len]
    left_rows = jnp.einsum("kmr,krs->kms", left_sum, gram_root, precision=highest).astype(
        jnp.bfloat16
    )
    owners_count = lax.axis_size("mp")
    cores = 2
    chips = replicas // cores
    pieces = owners_count // (matrices // cores)
    width = compensated.shape[2] // pieces
    right_terms = jnp.einsum(
        "kmn,kms->ksn", compensated, left_rows, preferred_element_type=jnp.float32
    )
    right_terms = right_terms.reshape(matrices, -1, pieces, width).transpose(0, 2, 1, 3)
    right_terms = right_terms.astype(jnp.bfloat16).reshape(cores, owners_count, -1, width)
    right_half = exchange(right_terms, "replica", 1, total=jnp.bfloat16)
    right_part = exchange(right_half, "mp", 2, total=jnp.float32)
    part_shape = right_part.shape
    right_part = allreduce_replica(right_part.reshape(chips, -1, lanes), 3, cores)
    right_part = right_part.reshape(part_shape).astype(jnp.bfloat16)
    right_half = exchange(jnp.broadcast_to(right_part, right_half.shape), "mp", 4)
    right_new = exchange(jnp.broadcast_to(right_half, right_terms.shape), "replica", 5)
    right_new = right_new.reshape(matrices, pieces, -1, width).transpose(0, 2, 1, 3)
    right_new = right_new.reshape(matrices, -1, compensated.shape[2])
    pairs = [
        (a * owners_count + b, b * owners_count + a)
        for a in range(replicas)
        for b in range(owners_count)
    ]
    left_block = lax.ppermute(left_rows, ("replica", "mp"), pairs)
    approx_rows = jnp.einsum(
        "kms,ksn->kmn", left_rows, right_new, preferred_element_type=jnp.float32
    )
    new_feedback = (compensated.astype(jnp.float32) - approx_rows).astype(jnp.bfloat16)
    scale = has.astype(jnp.float32)[:, None, None]
    left_chosen = left_block[chosen].astype(jnp.float32) * scale
    right_chosen = right_new[chosen].astype(jnp.float32) * scale
    approx_slots = jnp.einsum("cmr,crn->cmn", left_chosen, right_chosen, precision=highest)
    new_momentum = 0.9 * momentum[0] + approx_slots
    new_master = master_weights[0] - 0.1 * new_momentum
    new_weights = weights_of(slots, weight_slots, left_block, right_new)
    new_vector_momentum = 0.9 * vector_momentum + vector_total
    new_vector_params = vector_params - 0.1 * new_vector_momentum
    return (
        new_feedback[None],
        new_momentum[None],
        new_master[None],
        new_weights,
        new_vector_momentum,
        new_vector_params,
    )


def solution(mesh):
    return jax.shard_map(
        per_device,
        mesh=mesh,
        in_specs=(
            P("replica", None, "mp", None),
            P("replica", None, "mp", None),
            P(),
            P(),
            P(),
            P("mp", None, "replica", None),
            P("mp", None, "replica", None),
            P("replica", "mp"),
            P("mp"),
            P("mp"),
        ),
        out_specs=(
            P("replica", None, "mp", None),
            P("mp", None, "replica", None),
            P("mp", None, "replica", None),
            P(None, "replica", None),
            P("mp"),
            P("mp"),
        ),
        check_vma=False,
    )
```

```python
import functools

import jax
import jax.numpy as jnp
from jax import lax
from jax.experimental import pallas as pl
from jax.experimental.pallas import tpu as pltpu
from jax.sharding import PartitionSpec as P

MESH_IDS = pl.DeviceIdType.MESH


def _exchange_kernel(n, axis, stride, total, x_ref, o_ref, recv, send_sem, recv_sem):
    rank = lax.axis_index(axis)
    me = lax.rem(lax.div(rank, stride), n)
    first = rank - me * stride
    here = [lax.axis_index("replica"), lax.axis_index("mp")]
    where = 0 if axis == "replica" else 1

    def device(peer):
        ids = list(here)
        ids[where] = first + peer * stride
        return tuple(ids)

    barrier = pltpu.get_barrier_semaphore()
    for d in range(1, n):
        peer = lax.rem(me + d, n)
        pl.semaphore_signal(barrier, inc=1, device_id=device(peer), device_id_type=MESH_IDS)
    pl.semaphore_wait(barrier, n - 1)
    copies = []
    for d in range(1, n):
        peer = lax.rem(me + d, n)
        copy = pltpu.make_async_remote_copy(
            src_ref=x_ref.at[peer],
            dst_ref=recv.at[me],
            send_sem=send_sem.at[d],
            recv_sem=recv_sem.at[me],
            device_id=device(peer),
            device_id_type=MESH_IDS,
        )
        copy.start()
        copies.append(copy)
    recv[me] = x_ref[me]
    for d in range(1, n):
        source = lax.rem(me + n - d, n)
        pltpu.make_async_remote_copy(
            src_ref=x_ref.at[source],
            dst_ref=recv.at[source],
            send_sem=send_sem.at[d],
            recv_sem=recv_sem.at[source],
            device_id=device(source),
            device_id_type=MESH_IDS,
        ).wait_recv()
    for copy in copies:
        copy.wait_send()
    if total is None:
        o_ref[...] = recv[...]
    else:
        acc = recv[0].astype(jnp.float32)
        for s in range(1, n):
            acc = acc + recv[s].astype(jnp.float32)
        o_ref[...] = acc.astype(o_ref.dtype)


def exchange(x, axis, cid, stride=1, total=None):
    n = x.shape[0]
    out = jax.ShapeDtypeStruct(x.shape, x.dtype) if total is None else jax.ShapeDtypeStruct(
        x.shape[1:], total
    )
    return pl.pallas_call(
        functools.partial(_exchange_kernel, n, axis, stride, total),
        out_shape=out,
        in_specs=[pl.BlockSpec(memory_space=pltpu.VMEM)],
        out_specs=pl.BlockSpec(memory_space=pltpu.VMEM),
        scratch_shapes=[
            pltpu.VMEM(x.shape, x.dtype),
            pltpu.SemaphoreType.DMA((n,)),
            pltpu.SemaphoreType.DMA((n,)),
        ],
        compiler_params=pltpu.CompilerParams(
            collective_id=cid, has_side_effects=True, vmem_limit_bytes=48 * 1024 * 1024
        ),
    )(x)


def _allreduce_kernel(n, stride, x_ref, o_ref, first, middle, second, send_sem, recv_sem):
    rank = lax.axis_index("replica")
    me = lax.rem(lax.div(rank, stride), n)
    base = rank - me * stride
    mp = lax.axis_index("mp")

    def device(peer):
        return (base + peer * stride, mp)

    barrier = pltpu.get_barrier_semaphore()
    for d in range(1, n):
        peer = lax.rem(me + d, n)
        pl.semaphore_signal(barrier, inc=1, device_id=device(peer), device_id_type=MESH_IDS)
    pl.semaphore_wait(barrier, n - 1)

    def round_trip(phase, source_of, landing):
        copies = []
        for d in range(1, n):
            peer = lax.rem(me + d, n)
            copy = pltpu.make_async_remote_copy(
                src_ref=source_of(peer),
                dst_ref=landing.at[me],
                send_sem=send_sem.at[phase, d],
                recv_sem=recv_sem.at[phase, me],
                device_id=device(peer),
                device_id_type=MESH_IDS,
            )
            copy.start()
            copies.append(copy)
        landing[me] = source_of(me)[...]
        for d in range(1, n):
            source = lax.rem(me + n - d, n)
            pltpu.make_async_remote_copy(
                src_ref=source_of(source),
                dst_ref=landing.at[source],
                send_sem=send_sem.at[phase, d],
                recv_sem=recv_sem.at[phase, source],
                device_id=device(source),
                device_id_type=MESH_IDS,
            ).wait_recv()
        for copy in copies:
            copy.wait_send()

    round_trip(0, lambda peer: x_ref.at[peer], first)
    total = first[0]
    for s in range(1, n):
        total = total + first[s]
    middle[...] = total
    round_trip(1, lambda peer: middle, second)
    o_ref[...] = second[...]


def allreduce_replica(x, cid, stride=1):
    n = x.shape[0]
    return pl.pallas_call(
        functools.partial(_allreduce_kernel, n, stride),
        out_shape=jax.ShapeDtypeStruct(x.shape, x.dtype),
        in_specs=[pl.BlockSpec(memory_space=pltpu.VMEM)],
        out_specs=pl.BlockSpec(memory_space=pltpu.VMEM),
        scratch_shapes=[
            pltpu.VMEM(x.shape, x.dtype),
            pltpu.VMEM(x.shape[1:], x.dtype),
            pltpu.VMEM(x.shape, x.dtype),
            pltpu.SemaphoreType.DMA((2, n)),
            pltpu.SemaphoreType.DMA((2, n)),
        ],
        compiler_params=pltpu.CompilerParams(collective_id=cid, has_side_effects=True),
    )(x)


def per_device(
    gradients,
    feedback,
    right_init,
    gram_root,
    owners,
    momentum,
    master_weights,
    vector_grads,
    vector_momentum,
    vector_params,
):
    highest = lax.Precision.HIGHEST
    compensated = (gradients[0].astype(jnp.float32) + feedback[0].astype(jnp.float32)).astype(
        jnp.bfloat16
    )
    owner_count = lax.axis_size("mp")
    capacity = momentum.shape[1]
    matrices = owners.shape[0]
    replica_rows = momentum.shape[2]
    mp_index = lax.axis_index("mp")
    replica_index = lax.axis_index("replica")
    same_owner = owners[:, None] == owners[None, :]
    earlier = jnp.arange(matrices)[:, None] < jnp.arange(matrices)[None, :]
    ranks = jnp.sum((same_owner & earlier).astype(jnp.int32), axis=0)
    slots = owners * capacity + ranks
    mine = slots[None, :] == (mp_index * capacity + jnp.arange(capacity))[:, None]
    has = jnp.any(mine, axis=1)
    chosen = jnp.argmax(mine, axis=1)
    weight_base = master_weights[0] - 0.1 * (0.9 * momentum[0])
    weight_slots = lax.all_gather(weight_base.astype(jnp.bfloat16), "mp", axis=0, tiled=True)
    left_terms = jnp.einsum(
        "kmn,knr->kmr", compensated, right_init, preferred_element_type=jnp.float32
    )
    replicas = lax.axis_size("replica")
    vector_len = vector_grads.shape[1]
    packed = jnp.concatenate([left_terms.reshape(-1), vector_grads[0]])
    lanes = 128
    rows = -(-packed.shape[0] // (replicas * 8 * lanes)) * 8
    packed = jnp.pad(packed, (0, replicas * rows * lanes - packed.shape[0]))
    packed = allreduce_replica(packed.reshape(replicas, rows, lanes), 0).reshape(-1)
    left_sum = packed[: left_terms.size].reshape(left_terms.shape)
    vector_total = packed[left_terms.size : left_terms.size + vector_len]
    left_rows = jnp.einsum("kmr,krs->kms", left_sum, gram_root, precision=highest).astype(
        jnp.bfloat16
    )
    owners_count = lax.axis_size("mp")
    cores = 2
    chips = replicas // cores
    pieces = owners_count // (matrices // cores)
    width = compensated.shape[2] // pieces
    right_terms = jnp.einsum(
        "kmn,kms->ksn", compensated, left_rows, preferred_element_type=jnp.float32
    )
    right_terms = right_terms.reshape(matrices, -1, pieces, width).transpose(0, 2, 1, 3)
    right_terms = right_terms.astype(jnp.bfloat16).reshape(cores, owners_count, -1, width)
    right_half = exchange(right_terms, "replica", 1, total=jnp.bfloat16)
    right_part = exchange(right_half, "mp", 2, total=jnp.float32)
    part_shape = right_part.shape
    right_part = allreduce_replica(right_part.reshape(chips, -1, lanes), 3, cores)
    right_part = right_part.reshape(part_shape).astype(jnp.bfloat16)
    right_half = exchange(jnp.broadcast_to(right_part, right_half.shape), "mp", 4)
    right_new = exchange(jnp.broadcast_to(right_half, right_terms.shape), "replica", 5)
    right_new = right_new.reshape(matrices, pieces, -1, width).transpose(0, 2, 1, 3)
    right_new = right_new.reshape(matrices, -1, compensated.shape[2])
    pairs = [
        (a * owners_count + b, b * owners_count + a)
        for a in range(replicas)
        for b in range(owners_count)
    ]
    left_block = lax.ppermute(left_rows, ("replica", "mp"), pairs)
    approx_rows = jnp.einsum(
        "kms,ksn->kmn", left_rows, right_new, preferred_element_type=jnp.float32
    )
    new_feedback = (compensated.astype(jnp.float32) - approx_rows).astype(jnp.bfloat16)
    scale = has.astype(jnp.float32)[:, None, None]
    left_chosen = left_block[chosen].astype(jnp.float32) * scale
    right_chosen = right_new[chosen].astype(jnp.float32) * scale
    approx_slots = jnp.einsum("cmr,crn->cmn", left_chosen, right_chosen, precision=highest)
    new_momentum = 0.9 * momentum[0] + approx_slots
    new_master = master_weights[0] - 0.1 * new_momentum
    block_approx = jnp.einsum(
        "kms,ksn->kmn", left_block, right_new, preferred_element_type=jnp.float32
    )
    new_weights = (
        jnp.stack(
            [
                lax.dynamic_index_in_dim(weight_slots, slots[k], 0, keepdims=False)
                for k in range(matrices)
            ]
        ).astype(jnp.float32)
        - 0.1 * block_approx
    ).astype(jnp.bfloat16)
    new_vector_momentum = 0.9 * vector_momentum + vector_total
    new_vector_params = vector_params - 0.1 * new_vector_momentum
    return (
        new_feedback[None],
        new_momentum[None],
        new_master[None],
        new_weights,
        new_vector_momentum,
        new_vector_params,
    )


def solution(mesh):
    return jax.shard_map(
        per_device,
        mesh=mesh,
        in_specs=(
            P("replica", None, "mp", None),
            P("replica", None, "mp", None),
            P(),
            P(),
            P(),
            P("mp", None, "replica", None),
            P("mp", None, "replica", None),
            P("replica", "mp"),
            P("mp"),
            P("mp"),
        ),
        out_specs=(
            P("replica", None, "mp", None),
            P("mp", None, "replica", None),
            P("mp", None, "replica", None),
            P(None, "replica", None),
            P("mp"),
            P("mp"),
        ),
        check_vma=False,
    )
```

```python
import functools

import jax
import jax.numpy as jnp
from jax import lax
from jax.experimental import pallas as pl
from jax.experimental.pallas import tpu as pltpu
from jax.sharding import PartitionSpec as P

MESH_IDS = pl.DeviceIdType.MESH


def _exchange_kernel(n, axis, stride, total, x_ref, o_ref, recv, send_sem, recv_sem):
    rank = lax.axis_index(axis)
    me = lax.rem(lax.div(rank, stride), n)
    first = rank - me * stride
    here = [lax.axis_index("replica"), lax.axis_index("mp")]
    where = 0 if axis == "replica" else 1

    def device(peer):
        ids = list(here)
        ids[where] = first + peer * stride
        return tuple(ids)

    barrier = pltpu.get_barrier_semaphore()
    for d in range(1, n):
        peer = lax.rem(me + d, n)
        pl.semaphore_signal(barrier, inc=1, device_id=device(peer), device_id_type=MESH_IDS)
    pl.semaphore_wait(barrier, n - 1)
    copies = []
    for d in range(1, n):
        peer = lax.rem(me + d, n)
        copy = pltpu.make_async_remote_copy(
            src_ref=x_ref.at[peer],
            dst_ref=recv.at[me],
            send_sem=send_sem.at[d],
            recv_sem=recv_sem.at[me],
            device_id=device(peer),
            device_id_type=MESH_IDS,
        )
        copy.start()
        copies.append(copy)
    recv[me] = x_ref[me]
    for d in range(1, n):
        source = lax.rem(me + n - d, n)
        pltpu.make_async_remote_copy(
            src_ref=x_ref.at[source],
            dst_ref=recv.at[source],
            send_sem=send_sem.at[d],
            recv_sem=recv_sem.at[source],
            device_id=device(source),
            device_id_type=MESH_IDS,
        ).wait_recv()
    for copy in copies:
        copy.wait_send()
    if total is None:
        o_ref[...] = recv[...]
    else:
        acc = recv[0].astype(jnp.float32)
        for s in range(1, n):
            acc = acc + recv[s].astype(jnp.float32)
        o_ref[...] = acc.astype(o_ref.dtype)


def exchange(x, axis, cid, stride=1, total=None):
    n = x.shape[0]
    out = jax.ShapeDtypeStruct(x.shape, x.dtype) if total is None else jax.ShapeDtypeStruct(
        x.shape[1:], total
    )
    return pl.pallas_call(
        functools.partial(_exchange_kernel, n, axis, stride, total),
        out_shape=out,
        in_specs=[pl.BlockSpec(memory_space=pltpu.VMEM)],
        out_specs=pl.BlockSpec(memory_space=pltpu.VMEM),
        scratch_shapes=[
            pltpu.VMEM(x.shape, x.dtype),
            pltpu.SemaphoreType.DMA((n,)),
            pltpu.SemaphoreType.DMA((n,)),
        ],
        compiler_params=pltpu.CompilerParams(
            collective_id=cid, has_side_effects=True, vmem_limit_bytes=48 * 1024 * 1024
        ),
    )(x)


def _allreduce_kernel(n, stride, x_ref, o_ref, first, middle, second, send_sem, recv_sem):
    rank = lax.axis_index("replica")
    me = lax.rem(lax.div(rank, stride), n)
    base = rank - me * stride
    mp = lax.axis_index("mp")

    def device(peer):
        return (base + peer * stride, mp)

    barrier = pltpu.get_barrier_semaphore()
    for d in range(1, n):
        peer = lax.rem(me + d, n)
        pl.semaphore_signal(barrier, inc=1, device_id=device(peer), device_id_type=MESH_IDS)
    pl.semaphore_wait(barrier, n - 1)

    def round_trip(phase, source_of, landing):
        copies = []
        for d in range(1, n):
            peer = lax.rem(me + d, n)
            copy = pltpu.make_async_remote_copy(
                src_ref=source_of(peer),
                dst_ref=landing.at[me],
                send_sem=send_sem.at[phase, d],
                recv_sem=recv_sem.at[phase, me],
                device_id=device(peer),
                device_id_type=MESH_IDS,
            )
            copy.start()
            copies.append(copy)
        landing[me] = source_of(me)[...]
        for d in range(1, n):
            source = lax.rem(me + n - d, n)
            pltpu.make_async_remote_copy(
                src_ref=source_of(source),
                dst_ref=landing.at[source],
                send_sem=send_sem.at[phase, d],
                recv_sem=recv_sem.at[phase, source],
                device_id=device(source),
                device_id_type=MESH_IDS,
            ).wait_recv()
        for copy in copies:
            copy.wait_send()

    round_trip(0, lambda peer: x_ref.at[peer], first)
    total = first[0]
    for s in range(1, n):
        total = total + first[s]
    middle[...] = total
    round_trip(1, lambda peer: middle, second)
    o_ref[...] = second[...]


def allreduce_replica(x, cid, stride=1):
    n = x.shape[0]
    return pl.pallas_call(
        functools.partial(_allreduce_kernel, n, stride),
        out_shape=jax.ShapeDtypeStruct(x.shape, x.dtype),
        in_specs=[pl.BlockSpec(memory_space=pltpu.VMEM)],
        out_specs=pl.BlockSpec(memory_space=pltpu.VMEM),
        scratch_shapes=[
            pltpu.VMEM(x.shape, x.dtype),
            pltpu.VMEM(x.shape[1:], x.dtype),
            pltpu.VMEM(x.shape, x.dtype),
            pltpu.SemaphoreType.DMA((2, n)),
            pltpu.SemaphoreType.DMA((2, n)),
        ],
        compiler_params=pltpu.CompilerParams(collective_id=cid, has_side_effects=True),
    )(x)


def _reduce_kernel(n, chips, x_ref, o_ref, recv, acc, first, middle, second, mp_sem, z_sem):
    rank = lax.axis_index("replica")
    me = lax.axis_index("mp")
    spot = lax.rem(lax.div(rank, 2), chips)
    base = rank - spot * 2
    rows, cols = first.shape[1], first.shape[2]

    def chip(peer):
        return (base + peer * 2, me)

    def piece(p):
        r = pl.multiple_of(lax.div(p, 2) * rows, rows)
        c = pl.multiple_of(lax.rem(p, 2) * cols, cols)
        return acc.at[pl.ds(r, rows), pl.ds(c, cols)]

    barrier = pltpu.get_barrier_semaphore()
    for d in range(1, n):
        peer = lax.rem(me + d, n)
        pl.semaphore_signal(barrier, inc=1, device_id=(rank, peer), device_id_type=MESH_IDS)
    for d in range(1, chips):
        peer = lax.rem(spot + d, chips)
        pl.semaphore_signal(barrier, inc=1, device_id=chip(peer), device_id_type=MESH_IDS)
    pl.semaphore_wait(barrier, n - 1 + chips - 1)
    copies = []
    for d in range(1, n):
        peer = lax.rem(me + d, n)
        copy = pltpu.make_async_remote_copy(
            src_ref=x_ref.at[peer],
            dst_ref=recv.at[me],
            send_sem=mp_sem.at[0, d],
            recv_sem=mp_sem.at[1, me],
            device_id=(rank, peer),
            device_id_type=MESH_IDS,
        )
        copy.start()
        copies.append(copy)
    recv[me] = x_ref[me]
    for d in range(1, n):
        source = lax.rem(me + n - d, n)
        pltpu.make_async_remote_copy(
            src_ref=x_ref.at[source],
            dst_ref=recv.at[source],
            send_sem=mp_sem.at[0, d],
            recv_sem=mp_sem.at[1, source],
            device_id=(rank, source),
            device_id_type=MESH_IDS,
        ).wait_recv()
    for copy in copies:
        copy.wait_send()
    total = recv[0].astype(jnp.float32)
    for s in range(1, n):
        total = total + recv[s].astype(jnp.float32)
    acc[...] = total

    def round_trip(phase, source_of, landing):
        sent = []
        for d in range(1, chips):
            peer = lax.rem(spot + d, chips)
            copy = pltpu.make_async_remote_copy(
                src_ref=source_of(peer),
                dst_ref=landing.at[spot],
                send_sem=z_sem.at[phase, 0, d],
                recv_sem=z_sem.at[phase, 1, spot],
                device_id=chip(peer),
                device_id_type=MESH_IDS,
            )
            copy.start()
            sent.append(copy)
        landing[spot] = source_of(spot)[...]
        for d in range(1, chips):
            source = lax.rem(spot + chips - d, chips)
            pltpu.make_async_remote_copy(
                src_ref=source_of(source),
                dst_ref=landing.at[source],
                send_sem=z_sem.at[phase, 0, d],
                recv_sem=z_sem.at[phase, 1, source],
                device_id=chip(source),
                device_id_type=MESH_IDS,
            ).wait_recv()
        for copy in sent:
            copy.wait_send()

    round_trip(0, piece, first)
    part = first[0]
    for s in range(1, chips):
        part = part + first[s]
    middle[...] = part
    round_trip(1, lambda peer: middle, second)
    o_ref[...] = second[...]


def reduce_right(x, chips, cid):
    n = x.shape[0]
    rows, cols = x.shape[1] // (chips // 2), x.shape[2] // 2
    return pl.pallas_call(
        functools.partial(_reduce_kernel, n, chips),
        out_shape=jax.ShapeDtypeStruct((chips, rows, cols), jnp.float32),
        in_specs=[pl.BlockSpec(memory_space=pltpu.VMEM)],
        out_specs=pl.BlockSpec(memory_space=pltpu.VMEM),
        scratch_shapes=[
            pltpu.VMEM(x.shape, x.dtype),
            pltpu.VMEM(x.shape[1:], jnp.float32),
            pltpu.VMEM((chips, rows, cols), jnp.float32),
            pltpu.VMEM((rows, cols), jnp.float32),
            pltpu.VMEM((chips, rows, cols), jnp.float32),
            pltpu.SemaphoreType.DMA((2, n)),
            pltpu.SemaphoreType.DMA((2, 2, chips)),
        ],
        compiler_params=pltpu.CompilerParams(
            collective_id=cid, has_side_effects=True, vmem_limit_bytes=48 * 1024 * 1024
        ),
    )(x)


def per_device(
    gradients,
    feedback,
    right_init,
    gram_root,
    owners,
    momentum,
    master_weights,
    vector_grads,
    vector_momentum,
    vector_params,
):
    highest = lax.Precision.HIGHEST
    compensated = (gradients[0].astype(jnp.float32) + feedback[0].astype(jnp.float32)).astype(
        jnp.bfloat16
    )
    owner_count = lax.axis_size("mp")
    capacity = momentum.shape[1]
    matrices = owners.shape[0]
    replica_rows = momentum.shape[2]
    mp_index = lax.axis_index("mp")
    replica_index = lax.axis_index("replica")
    same_owner = owners[:, None] == owners[None, :]
    earlier = jnp.arange(matrices)[:, None] < jnp.arange(matrices)[None, :]
    ranks = jnp.sum((same_owner & earlier).astype(jnp.int32), axis=0)
    slots = owners * capacity + ranks
    mine = slots[None, :] == (mp_index * capacity + jnp.arange(capacity))[:, None]
    has = jnp.any(mine, axis=1)
    chosen = jnp.argmax(mine, axis=1)
    weight_base = master_weights[0] - 0.1 * (0.9 * momentum[0])
    weight_slots = lax.all_gather(weight_base.astype(jnp.bfloat16), "mp", axis=0, tiled=True)
    left_terms = jnp.einsum(
        "kmn,knr->kmr", compensated, right_init, preferred_element_type=jnp.float32
    )
    replicas = lax.axis_size("replica")
    vector_len = vector_grads.shape[1]
    packed = jnp.concatenate([left_terms.reshape(-1), vector_grads[0]])
    lanes = 128
    rows = -(-packed.shape[0] // (replicas * 8 * lanes)) * 8
    packed = jnp.pad(packed, (0, replicas * rows * lanes - packed.shape[0]))
    packed = allreduce_replica(packed.reshape(replicas, rows, lanes), 0).reshape(-1)
    left_sum = packed[: left_terms.size].reshape(left_terms.shape)
    vector_total = packed[left_terms.size : left_terms.size + vector_len]
    left_rows = jnp.einsum("kmr,krs->kms", left_sum, gram_root, precision=highest).astype(
        jnp.bfloat16
    )
    owners_count = lax.axis_size("mp")
    cores = 2
    chips = replicas // cores
    pieces = owners_count // (matrices // cores)
    width = compensated.shape[2] // pieces
    right_terms = jnp.einsum(
        "kmn,kms->ksn", compensated, left_rows, preferred_element_type=jnp.float32
    )
    right_terms = right_terms.reshape(matrices, -1, pieces, width).transpose(0, 2, 1, 3)
    right_terms = right_terms.astype(jnp.bfloat16).reshape(cores, owners_count, -1, width)
    right_half = exchange(right_terms, "replica", 1, total=jnp.bfloat16)
    right_part = reduce_right(right_half, chips, 2)
    right_part = right_part.reshape(chips // 2, 2, *right_part.shape[1:]).transpose(0, 2, 1, 3)
    right_part = right_part.reshape(right_half.shape[1:]).astype(jnp.bfloat16)
    right_half = exchange(jnp.broadcast_to(right_part, right_half.shape), "mp", 4)
    right_new = exchange(jnp.broadcast_to(right_half, right_terms.shape), "replica", 5)
    right_new = right_new.reshape(matrices, pieces, -1, width).transpose(0, 2, 1, 3)
    right_new = right_new.reshape(matrices, -1, compensated.shape[2])
    pairs = [
        (a * owners_count + b, b * owners_count + a)
        for a in range(replicas)
        for b in range(owners_count)
    ]
    left_block = lax.ppermute(left_rows, ("replica", "mp"), pairs)
    approx_rows = jnp.einsum(
        "kms,ksn->kmn", left_rows, right_new, preferred_element_type=jnp.float32
    )
    new_feedback = (compensated.astype(jnp.float32) - approx_rows).astype(jnp.bfloat16)
    scale = has.astype(jnp.float32)[:, None, None]
    left_chosen = left_block[chosen].astype(jnp.float32) * scale
    right_chosen = right_new[chosen].astype(jnp.float32) * scale
    approx_slots = jnp.einsum("cmr,crn->cmn", left_chosen, right_chosen, precision=highest)
    new_momentum = 0.9 * momentum[0] + approx_slots
    new_master = master_weights[0] - 0.1 * new_momentum
    block_approx = jnp.einsum(
        "kms,ksn->kmn", left_block, right_new, preferred_element_type=jnp.float32
    )
    new_weights = (
        jnp.take(weight_slots, slots, axis=0).astype(jnp.float32) - 0.1 * block_approx
    ).astype(jnp.bfloat16)
    new_vector_momentum = 0.9 * vector_momentum + vector_total
    new_vector_params = vector_params - 0.1 * new_vector_momentum
    return (
        new_feedback[None],
        new_momentum[None],
        new_master[None],
        new_weights,
        new_vector_momentum,
        new_vector_params,
    )


def solution(mesh):
    return jax.shard_map(
        per_device,
        mesh=mesh,
        in_specs=(
            P("replica", None, "mp", None),
            P("replica", None, "mp", None),
            P(),
            P(),
            P(),
            P("mp", None, "replica", None),
            P("mp", None, "replica", None),
            P("replica", "mp"),
            P("mp"),
            P("mp"),
        ),
        out_specs=(
            P("replica", None, "mp", None),
            P("mp", None, "replica", None),
            P("mp", None, "replica", None),
            P(None, "replica", None),
            P("mp"),
            P("mp"),
        ),
        check_vma=False,
    )
```

```python
import functools

import jax
import jax.numpy as jnp
from jax import lax
from jax.experimental import pallas as pl
from jax.experimental.pallas import tpu as pltpu
from jax.sharding import PartitionSpec as P

MESH_IDS = pl.DeviceIdType.MESH


def _exchange_kernel(n, axis, stride, total, x_ref, o_ref, recv, send_sem, recv_sem):
    rank = lax.axis_index(axis)
    me = lax.rem(lax.div(rank, stride), n)
    first = rank - me * stride
    here = [lax.axis_index("replica"), lax.axis_index("mp")]
    where = 0 if axis == "replica" else 1

    def device(peer):
        ids = list(here)
        ids[where] = first + peer * stride
        return tuple(ids)

    barrier = pltpu.get_barrier_semaphore()
    for d in range(1, n):
        peer = lax.rem(me + d, n)
        pl.semaphore_signal(barrier, inc=1, device_id=device(peer), device_id_type=MESH_IDS)
    pl.semaphore_wait(barrier, n - 1)
    copies = []
    for d in range(1, n):
        peer = lax.rem(me + d, n)
        copy = pltpu.make_async_remote_copy(
            src_ref=x_ref.at[peer],
            dst_ref=recv.at[me],
            send_sem=send_sem.at[d],
            recv_sem=recv_sem.at[me],
            device_id=device(peer),
            device_id_type=MESH_IDS,
        )
        copy.start()
        copies.append(copy)
    recv[me] = x_ref[me]
    for d in range(1, n):
        source = lax.rem(me + n - d, n)
        pltpu.make_async_remote_copy(
            src_ref=x_ref.at[source],
            dst_ref=recv.at[source],
            send_sem=send_sem.at[d],
            recv_sem=recv_sem.at[source],
            device_id=device(source),
            device_id_type=MESH_IDS,
        ).wait_recv()
    for copy in copies:
        copy.wait_send()
    if total is None:
        o_ref[...] = recv[...]
    else:
        acc = recv[0].astype(jnp.float32)
        for s in range(1, n):
            acc = acc + recv[s].astype(jnp.float32)
        o_ref[...] = acc.astype(o_ref.dtype)


def exchange(x, axis, cid, stride=1, total=None):
    n = x.shape[0]
    out = jax.ShapeDtypeStruct(x.shape, x.dtype) if total is None else jax.ShapeDtypeStruct(
        x.shape[1:], total
    )
    return pl.pallas_call(
        functools.partial(_exchange_kernel, n, axis, stride, total),
        out_shape=out,
        in_specs=[pl.BlockSpec(memory_space=pltpu.VMEM)],
        out_specs=pl.BlockSpec(memory_space=pltpu.VMEM),
        scratch_shapes=[
            pltpu.VMEM(x.shape, x.dtype),
            pltpu.SemaphoreType.DMA((n,)),
            pltpu.SemaphoreType.DMA((n,)),
        ],
        compiler_params=pltpu.CompilerParams(
            collective_id=cid, has_side_effects=True, vmem_limit_bytes=48 * 1024 * 1024
        ),
    )(x)


def _allreduce_kernel(n, stride, x_ref, o_ref, first, middle, second, send_sem, recv_sem):
    rank = lax.axis_index("replica")
    me = lax.rem(lax.div(rank, stride), n)
    base = rank - me * stride
    mp = lax.axis_index("mp")

    def device(peer):
        return (base + peer * stride, mp)

    barrier = pltpu.get_barrier_semaphore()
    for d in range(1, n):
        peer = lax.rem(me + d, n)
        pl.semaphore_signal(barrier, inc=1, device_id=device(peer), device_id_type=MESH_IDS)
    pl.semaphore_wait(barrier, n - 1)

    def round_trip(phase, source_of, landing):
        copies = []
        for d in range(1, n):
            peer = lax.rem(me + d, n)
            copy = pltpu.make_async_remote_copy(
                src_ref=source_of(peer),
                dst_ref=landing.at[me],
                send_sem=send_sem.at[phase, d],
                recv_sem=recv_sem.at[phase, me],
                device_id=device(peer),
                device_id_type=MESH_IDS,
            )
            copy.start()
            copies.append(copy)
        landing[me] = source_of(me)[...]
        for d in range(1, n):
            source = lax.rem(me + n - d, n)
            pltpu.make_async_remote_copy(
                src_ref=source_of(source),
                dst_ref=landing.at[source],
                send_sem=send_sem.at[phase, d],
                recv_sem=recv_sem.at[phase, source],
                device_id=device(source),
                device_id_type=MESH_IDS,
            ).wait_recv()
        for copy in copies:
            copy.wait_send()

    round_trip(0, lambda peer: x_ref.at[peer], first)
    total = first[0]
    for s in range(1, n):
        total = total + first[s]
    middle[...] = total
    round_trip(1, lambda peer: middle, second)
    o_ref[...] = second[...]


def allreduce_replica(x, cid, stride=1):
    n = x.shape[0]
    return pl.pallas_call(
        functools.partial(_allreduce_kernel, n, stride),
        out_shape=jax.ShapeDtypeStruct(x.shape, x.dtype),
        in_specs=[pl.BlockSpec(memory_space=pltpu.VMEM)],
        out_specs=pl.BlockSpec(memory_space=pltpu.VMEM),
        scratch_shapes=[
            pltpu.VMEM(x.shape, x.dtype),
            pltpu.VMEM(x.shape[1:], x.dtype),
            pltpu.VMEM(x.shape, x.dtype),
            pltpu.SemaphoreType.DMA((2, n)),
            pltpu.SemaphoreType.DMA((2, n)),
        ],
        compiler_params=pltpu.CompilerParams(collective_id=cid, has_side_effects=True),
    )(x)


def _reduce_kernel(n, chips, x_ref, o_ref, recv, acc, first, middle, second, mp_sem, z_sem):
    rank = lax.axis_index("replica")
    me = lax.axis_index("mp")
    spot = lax.rem(lax.div(rank, 2), chips)
    base = rank - spot * 2
    rows, cols = first.shape[1], first.shape[2]

    def chip(peer):
        return (base + peer * 2, me)

    def piece(p):
        r = pl.multiple_of(lax.div(p, 2) * rows, rows)
        c = pl.multiple_of(lax.rem(p, 2) * cols, cols)
        return acc.at[pl.ds(r, rows), pl.ds(c, cols)]

    barrier = pltpu.get_barrier_semaphore()
    for d in range(1, n):
        peer = lax.rem(me + d, n)
        pl.semaphore_signal(barrier, inc=1, device_id=(rank, peer), device_id_type=MESH_IDS)
    for d in range(1, chips):
        peer = lax.rem(spot + d, chips)
        pl.semaphore_signal(barrier, inc=1, device_id=chip(peer), device_id_type=MESH_IDS)
    pl.semaphore_wait(barrier, n - 1 + chips - 1)
    copies = []
    for d in range(1, n):
        peer = lax.rem(me + d, n)
        copy = pltpu.make_async_remote_copy(
            src_ref=x_ref.at[peer],
            dst_ref=recv.at[me],
            send_sem=mp_sem.at[0, d],
            recv_sem=mp_sem.at[1, me],
            device_id=(rank, peer),
            device_id_type=MESH_IDS,
        )
        copy.start()
        copies.append(copy)
    recv[me] = x_ref[me]
    for d in range(1, n):
        source = lax.rem(me + n - d, n)
        pltpu.make_async_remote_copy(
            src_ref=x_ref.at[source],
            dst_ref=recv.at[source],
            send_sem=mp_sem.at[0, d],
            recv_sem=mp_sem.at[1, source],
            device_id=(rank, source),
            device_id_type=MESH_IDS,
        ).wait_recv()
    for copy in copies:
        copy.wait_send()
    total = recv[0].astype(jnp.float32)
    for s in range(1, n):
        total = total + recv[s].astype(jnp.float32)
    acc[...] = total

    def round_trip(phase, source_of, landing):
        sent = []
        for d in range(1, chips):
            peer = lax.rem(spot + d, chips)
            copy = pltpu.make_async_remote_copy(
                src_ref=source_of(peer),
                dst_ref=landing.at[spot],
                send_sem=z_sem.at[phase, 0, d],
                recv_sem=z_sem.at[phase, 1, spot],
                device_id=chip(peer),
                device_id_type=MESH_IDS,
            )
            copy.start()
            sent.append(copy)
        landing[spot] = source_of(spot)[...]
        for d in range(1, chips):
            source = lax.rem(spot + chips - d, chips)
            pltpu.make_async_remote_copy(
                src_ref=source_of(source),
                dst_ref=landing.at[source],
                send_sem=z_sem.at[phase, 0, d],
                recv_sem=z_sem.at[phase, 1, source],
                device_id=chip(source),
                device_id_type=MESH_IDS,
            ).wait_recv()
        for copy in sent:
            copy.wait_send()

    round_trip(0, piece, first)
    part = first[0]
    for s in range(1, chips):
        part = part + first[s]
    middle[...] = part
    round_trip(1, lambda peer: middle, second)
    o_ref[...] = second[...]


def reduce_right(x, chips, cid):
    n = x.shape[0]
    rows, cols = x.shape[1] // (chips // 2), x.shape[2] // 2
    return pl.pallas_call(
        functools.partial(_reduce_kernel, n, chips),
        out_shape=jax.ShapeDtypeStruct((chips, rows, cols), jnp.float32),
        in_specs=[pl.BlockSpec(memory_space=pltpu.VMEM)],
        out_specs=pl.BlockSpec(memory_space=pltpu.VMEM),
        scratch_shapes=[
            pltpu.VMEM(x.shape, x.dtype),
            pltpu.VMEM(x.shape[1:], jnp.float32),
            pltpu.VMEM((chips, rows, cols), jnp.float32),
            pltpu.VMEM((rows, cols), jnp.float32),
            pltpu.VMEM((chips, rows, cols), jnp.float32),
            pltpu.SemaphoreType.DMA((2, n)),
            pltpu.SemaphoreType.DMA((2, 2, chips)),
        ],
        compiler_params=pltpu.CompilerParams(
            collective_id=cid, has_side_effects=True, vmem_limit_bytes=48 * 1024 * 1024
        ),
    )(x)


def _gather_kernel(n, x_ref, o_ref, half, full, sems):
    rank = lax.axis_index("replica")
    me = lax.axis_index("mp")
    core = lax.rem(rank, 2)
    partner = rank + 1 - 2 * core
    barrier = pltpu.get_barrier_semaphore()
    for d in range(1, n):
        peer = lax.rem(me + d, n)
        pl.semaphore_signal(barrier, inc=1, device_id=(rank, peer), device_id_type=MESH_IDS)
    pl.semaphore_signal(barrier, inc=1, device_id=(partner, me), device_id_type=MESH_IDS)
    pl.semaphore_wait(barrier, n)
    copies = []
    for d in range(1, n):
        peer = lax.rem(me + d, n)
        copy = pltpu.make_async_remote_copy(
            src_ref=x_ref,
            dst_ref=half.at[me],
            send_sem=sems.at[0, d],
            recv_sem=sems.at[1, me],
            device_id=(rank, peer),
            device_id_type=MESH_IDS,
        )
        copy.start()
        copies.append(copy)
    half[me] = x_ref[...]
    for d in range(1, n):
        source = lax.rem(me + n - d, n)
        pltpu.make_async_remote_copy(
            src_ref=x_ref,
            dst_ref=half.at[source],
            send_sem=sems.at[0, d],
            recv_sem=sems.at[1, source],
            device_id=(rank, source),
            device_id_type=MESH_IDS,
        ).wait_recv()
    for copy in copies:
        copy.wait_send()
    swap = pltpu.make_async_remote_copy(
        src_ref=half,
        dst_ref=full.at[core],
        send_sem=sems.at[2, 0],
        recv_sem=sems.at[2, 1],
        device_id=(partner, me),
        device_id_type=MESH_IDS,
    )
    swap.start()
    full[core] = half[...]
    swap.wait()
    o_ref[...] = full[...]


def gather_right(x, n, cid):
    return pl.pallas_call(
        functools.partial(_gather_kernel, n),
        out_shape=jax.ShapeDtypeStruct((2, n) + x.shape, x.dtype),
        in_specs=[pl.BlockSpec(memory_space=pltpu.VMEM)],
        out_specs=pl.BlockSpec(memory_space=pltpu.VMEM),
        scratch_shapes=[
            pltpu.VMEM((n,) + x.shape, x.dtype),
            pltpu.VMEM((2, n) + x.shape, x.dtype),
            pltpu.SemaphoreType.DMA((3, n)),
        ],
        compiler_params=pltpu.CompilerParams(
            collective_id=cid, has_side_effects=True, vmem_limit_bytes=48 * 1024 * 1024
        ),
    )(x)


def per_device(
    gradients,
    feedback,
    right_init,
    gram_root,
    owners,
    momentum,
    master_weights,
    vector_grads,
    vector_momentum,
    vector_params,
):
    highest = lax.Precision.HIGHEST
    compensated = (gradients[0].astype(jnp.float32) + feedback[0].astype(jnp.float32)).astype(
        jnp.bfloat16
    )
    owner_count = lax.axis_size("mp")
    capacity = momentum.shape[1]
    matrices = owners.shape[0]
    replica_rows = momentum.shape[2]
    mp_index = lax.axis_index("mp")
    replica_index = lax.axis_index("replica")
    same_owner = owners[:, None] == owners[None, :]
    earlier = jnp.arange(matrices)[:, None] < jnp.arange(matrices)[None, :]
    ranks = jnp.sum((same_owner & earlier).astype(jnp.int32), axis=0)
    slots = owners * capacity + ranks
    mine = slots[None, :] == (mp_index * capacity + jnp.arange(capacity))[:, None]
    has = jnp.any(mine, axis=1)
    chosen = jnp.argmax(mine, axis=1)
    weight_base = master_weights[0] - 0.1 * (0.9 * momentum[0])
    weight_slots = lax.all_gather(weight_base.astype(jnp.bfloat16), "mp", axis=0, tiled=True)
    left_terms = jnp.einsum(
        "kmn,knr->kmr", compensated, right_init, preferred_element_type=jnp.float32
    )
    replicas = lax.axis_size("replica")
    vector_len = vector_grads.shape[1]
    packed = jnp.concatenate([left_terms.reshape(-1), vector_grads[0]])
    lanes = 128
    rows = -(-packed.shape[0] // (replicas * 8 * lanes)) * 8
    packed = jnp.pad(packed, (0, replicas * rows * lanes - packed.shape[0]))
    packed = allreduce_replica(packed.reshape(replicas, rows, lanes), 0).reshape(-1)
    left_sum = packed[: left_terms.size].reshape(left_terms.shape)
    vector_total = packed[left_terms.size : left_terms.size + vector_len]
    left_rows = jnp.einsum("kmr,krs->kms", left_sum, gram_root, precision=highest).astype(
        jnp.bfloat16
    )
    owners_count = lax.axis_size("mp")
    cores = 2
    chips = replicas // cores
    pieces = owners_count // (matrices // cores)
    width = compensated.shape[2] // pieces
    right_terms = jnp.einsum(
        "kmn,kms->ksn", compensated, left_rows, preferred_element_type=jnp.float32
    )
    right_terms = right_terms.reshape(matrices, -1, pieces, width).transpose(0, 2, 1, 3)
    right_terms = right_terms.astype(jnp.bfloat16).reshape(cores, owners_count, -1, width)
    right_half = exchange(right_terms, "replica", 1, total=jnp.bfloat16)
    right_part = reduce_right(right_half, chips, 2)
    right_part = right_part.reshape(chips // 2, 2, *right_part.shape[1:]).transpose(0, 2, 1, 3)
    right_part = right_part.reshape(right_half.shape[1:]).astype(jnp.bfloat16)
    right_new = gather_right(right_part, owners_count, 4)
    right_new = right_new.reshape(matrices, pieces, -1, width).transpose(0, 2, 1, 3)
    right_new = right_new.reshape(matrices, -1, compensated.shape[2])
    pairs = [
        (a * owners_count + b, b * owners_count + a)
        for a in range(replicas)
        for b in range(owners_count)
    ]
    left_block = lax.ppermute(left_rows, ("replica", "mp"), pairs)
    approx_rows = jnp.einsum(
        "kms,ksn->kmn", left_rows, right_new, preferred_element_type=jnp.float32
    )
    new_feedback = (compensated.astype(jnp.float32) - approx_rows).astype(jnp.bfloat16)
    scale = has.astype(jnp.float32)[:, None, None]
    left_chosen = left_block[chosen].astype(jnp.float32) * scale
    right_chosen = right_new[chosen].astype(jnp.float32) * scale
    approx_slots = jnp.einsum("cmr,crn->cmn", left_chosen, right_chosen, precision=highest)
    new_momentum = 0.9 * momentum[0] + approx_slots
    new_master = master_weights[0] - 0.1 * new_momentum
    block_approx = jnp.einsum(
        "kms,ksn->kmn", left_block, right_new, preferred_element_type=jnp.float32
    )
    new_weights = (
        jnp.take(weight_slots, slots, axis=0).astype(jnp.float32) - 0.1 * block_approx
    ).astype(jnp.bfloat16)
    new_vector_momentum = 0.9 * vector_momentum + vector_total
    new_vector_params = vector_params - 0.1 * new_vector_momentum
    return (
        new_feedback[None],
        new_momentum[None],
        new_master[None],
        new_weights,
        new_vector_momentum,
        new_vector_params,
    )


def solution(mesh):
    return jax.shard_map(
        per_device,
        mesh=mesh,
        in_specs=(
            P("replica", None, "mp", None),
            P("replica", None, "mp", None),
            P(),
            P(),
            P(),
            P("mp", None, "replica", None),
            P("mp", None, "replica", None),
            P("replica", "mp"),
            P("mp"),
            P("mp"),
        ),
        out_specs=(
            P("replica", None, "mp", None),
            P("mp", None, "replica", None),
            P("mp", None, "replica", None),
            P(None, "replica", None),
            P("mp"),
            P("mp"),
        ),
        check_vma=False,
    )
```

```python
import functools

import jax
import jax.numpy as jnp
from jax import lax
from jax.experimental import pallas as pl
from jax.experimental.pallas import tpu as pltpu
from jax.sharding import PartitionSpec as P

MESH_IDS = pl.DeviceIdType.MESH


def _exchange_kernel(n, axis, stride, total, x_ref, o_ref, recv, send_sem, recv_sem):
    rank = lax.axis_index(axis)
    me = lax.rem(lax.div(rank, stride), n)
    first = rank - me * stride
    here = [lax.axis_index("replica"), lax.axis_index("mp")]
    where = 0 if axis == "replica" else 1

    def device(peer):
        ids = list(here)
        ids[where] = first + peer * stride
        return tuple(ids)

    barrier = pltpu.get_barrier_semaphore()
    for d in range(1, n):
        peer = lax.rem(me + d, n)
        pl.semaphore_signal(barrier, inc=1, device_id=device(peer), device_id_type=MESH_IDS)
    pl.semaphore_wait(barrier, n - 1)
    copies = []
    for d in range(1, n):
        peer = lax.rem(me + d, n)
        copy = pltpu.make_async_remote_copy(
            src_ref=x_ref.at[peer],
            dst_ref=recv.at[me],
            send_sem=send_sem.at[d],
            recv_sem=recv_sem.at[me],
            device_id=device(peer),
            device_id_type=MESH_IDS,
        )
        copy.start()
        copies.append(copy)
    recv[me] = x_ref[me]
    for d in range(1, n):
        source = lax.rem(me + n - d, n)
        pltpu.make_async_remote_copy(
            src_ref=x_ref.at[source],
            dst_ref=recv.at[source],
            send_sem=send_sem.at[d],
            recv_sem=recv_sem.at[source],
            device_id=device(source),
            device_id_type=MESH_IDS,
        ).wait_recv()
    for copy in copies:
        copy.wait_send()
    if total is None:
        o_ref[...] = recv[...]
    else:
        acc = recv[0].astype(jnp.float32)
        for s in range(1, n):
            acc = acc + recv[s].astype(jnp.float32)
        o_ref[...] = acc.astype(o_ref.dtype)


def exchange(x, axis, cid, stride=1, total=None):
    n = x.shape[0]
    out = jax.ShapeDtypeStruct(x.shape, x.dtype) if total is None else jax.ShapeDtypeStruct(
        x.shape[1:], total
    )
    return pl.pallas_call(
        functools.partial(_exchange_kernel, n, axis, stride, total),
        out_shape=out,
        in_specs=[pl.BlockSpec(memory_space=pltpu.VMEM)],
        out_specs=pl.BlockSpec(memory_space=pltpu.VMEM),
        scratch_shapes=[
            pltpu.VMEM(x.shape, x.dtype),
            pltpu.SemaphoreType.DMA((n,)),
            pltpu.SemaphoreType.DMA((n,)),
        ],
        compiler_params=pltpu.CompilerParams(
            collective_id=cid, has_side_effects=True, vmem_limit_bytes=48 * 1024 * 1024
        ),
    )(x)


def _allreduce_kernel(n, stride, x_ref, o_ref, first, middle, second, send_sem, recv_sem):
    rank = lax.axis_index("replica")
    me = lax.rem(lax.div(rank, stride), n)
    base = rank - me * stride
    mp = lax.axis_index("mp")

    def device(peer):
        return (base + peer * stride, mp)

    barrier = pltpu.get_barrier_semaphore()
    for d in range(1, n):
        peer = lax.rem(me + d, n)
        pl.semaphore_signal(barrier, inc=1, device_id=device(peer), device_id_type=MESH_IDS)
    pl.semaphore_wait(barrier, n - 1)

    def round_trip(phase, source_of, landing):
        copies = []
        for d in range(1, n):
            peer = lax.rem(me + d, n)
            copy = pltpu.make_async_remote_copy(
                src_ref=source_of(peer),
                dst_ref=landing.at[me],
                send_sem=send_sem.at[phase, d],
                recv_sem=recv_sem.at[phase, me],
                device_id=device(peer),
                device_id_type=MESH_IDS,
            )
            copy.start()
            copies.append(copy)
        landing[me] = source_of(me)[...]
        for d in range(1, n):
            source = lax.rem(me + n - d, n)
            pltpu.make_async_remote_copy(
                src_ref=source_of(source),
                dst_ref=landing.at[source],
                send_sem=send_sem.at[phase, d],
                recv_sem=recv_sem.at[phase, source],
                device_id=device(source),
                device_id_type=MESH_IDS,
            ).wait_recv()
        for copy in copies:
            copy.wait_send()

    round_trip(0, lambda peer: x_ref.at[peer], first)
    total = first[0]
    for s in range(1, n):
        total = total + first[s]
    middle[...] = total
    round_trip(1, lambda peer: middle, second)
    o_ref[...] = second[...]


def allreduce_replica(x, cid, stride=1):
    n = x.shape[0]
    return pl.pallas_call(
        functools.partial(_allreduce_kernel, n, stride),
        out_shape=jax.ShapeDtypeStruct(x.shape, x.dtype),
        in_specs=[pl.BlockSpec(memory_space=pltpu.VMEM)],
        out_specs=pl.BlockSpec(memory_space=pltpu.VMEM),
        scratch_shapes=[
            pltpu.VMEM(x.shape, x.dtype),
            pltpu.VMEM(x.shape[1:], x.dtype),
            pltpu.VMEM(x.shape, x.dtype),
            pltpu.SemaphoreType.DMA((2, n)),
            pltpu.SemaphoreType.DMA((2, n)),
        ],
        compiler_params=pltpu.CompilerParams(collective_id=cid, has_side_effects=True),
    )(x)


def _reduce_kernel(
    n, chips, x_ref, o_ref, pair, mine, recv, acc, first, middle, second, mp_sem, z_sem
):
    rank = lax.axis_index("replica")
    me = lax.axis_index("mp")
    core = lax.rem(rank, 2)
    partner = rank + 1 - 2 * core
    spot = lax.rem(lax.div(rank, 2), chips)
    base = rank - spot * 2
    rows, cols = first.shape[1], first.shape[2]

    def chip(peer):
        return (base + peer * 2, me)

    def piece(p):
        r = pl.multiple_of(lax.div(p, 2) * rows, rows)
        c = pl.multiple_of(lax.rem(p, 2) * cols, cols)
        return acc.at[pl.ds(r, rows), pl.ds(c, cols)]

    barrier = pltpu.get_barrier_semaphore()
    for d in range(1, n):
        peer = lax.rem(me + d, n)
        pl.semaphore_signal(barrier, inc=1, device_id=(rank, peer), device_id_type=MESH_IDS)
    for d in range(1, chips):
        peer = lax.rem(spot + d, chips)
        pl.semaphore_signal(barrier, inc=1, device_id=chip(peer), device_id_type=MESH_IDS)
    pl.semaphore_signal(barrier, inc=1, device_id=(partner, me), device_id_type=MESH_IDS)
    pl.semaphore_wait(barrier, n - 1 + chips - 1 + 1)
    swap = pltpu.make_async_remote_copy(
        src_ref=x_ref.at[1 - core],
        dst_ref=pair,
        send_sem=z_sem.at[2, 0, 0],
        recv_sem=z_sem.at[2, 1, 0],
        device_id=(partner, me),
        device_id_type=MESH_IDS,
    )
    swap.start()
    swap.wait()
    mine[...] = (x_ref[core].astype(jnp.float32) + pair[...].astype(jnp.float32)).astype(
        mine.dtype
    )
    copies = []
    for d in range(1, n):
        peer = lax.rem(me + d, n)
        copy = pltpu.make_async_remote_copy(
            src_ref=mine.at[peer],
            dst_ref=recv.at[me],
            send_sem=mp_sem.at[0, d],
            recv_sem=mp_sem.at[1, me],
            device_id=(rank, peer),
            device_id_type=MESH_IDS,
        )
        copy.start()
        copies.append(copy)
    recv[me] = mine[me]
    for d in range(1, n):
        source = lax.rem(me + n - d, n)
        pltpu.make_async_remote_copy(
            src_ref=mine.at[source],
            dst_ref=recv.at[source],
            send_sem=mp_sem.at[0, d],
            recv_sem=mp_sem.at[1, source],
            device_id=(rank, source),
            device_id_type=MESH_IDS,
        ).wait_recv()
    for copy in copies:
        copy.wait_send()
    total = recv[0].astype(jnp.float32)
    for s in range(1, n):
        total = total + recv[s].astype(jnp.float32)
    acc[...] = total

    def round_trip(phase, source_of, landing):
        sent = []
        for d in range(1, chips):
            peer = lax.rem(spot + d, chips)
            copy = pltpu.make_async_remote_copy(
                src_ref=source_of(peer),
                dst_ref=landing.at[spot],
                send_sem=z_sem.at[phase, 0, d],
                recv_sem=z_sem.at[phase, 1, spot],
                device_id=chip(peer),
                device_id_type=MESH_IDS,
            )
            copy.start()
            sent.append(copy)
        landing[spot] = source_of(spot)[...]
        for d in range(1, chips):
            source = lax.rem(spot + chips - d, chips)
            pltpu.make_async_remote_copy(
                src_ref=source_of(source),
                dst_ref=landing.at[source],
                send_sem=z_sem.at[phase, 0, d],
                recv_sem=z_sem.at[phase, 1, source],
                device_id=chip(source),
                device_id_type=MESH_IDS,
            ).wait_recv()
        for copy in sent:
            copy.wait_send()

    round_trip(0, piece, first)
    part = first[0]
    for s in range(1, chips):
        part = part + first[s]
    middle[...] = part
    round_trip(1, lambda peer: middle, second)
    o_ref[...] = second[...]


def reduce_right(x, chips, cid):
    n = x.shape[1]
    rows, cols = x.shape[2] // (chips // 2), x.shape[3] // 2
    return pl.pallas_call(
        functools.partial(_reduce_kernel, n, chips),
        out_shape=jax.ShapeDtypeStruct((chips, rows, cols), jnp.float32),
        in_specs=[pl.BlockSpec(memory_space=pltpu.VMEM)],
        out_specs=pl.BlockSpec(memory_space=pltpu.VMEM),
        scratch_shapes=[
            pltpu.VMEM(x.shape[1:], x.dtype),
            pltpu.VMEM(x.shape[1:], x.dtype),
            pltpu.VMEM(x.shape[1:], x.dtype),
            pltpu.VMEM(x.shape[2:], jnp.float32),
            pltpu.VMEM((chips, rows, cols), jnp.float32),
            pltpu.VMEM((rows, cols), jnp.float32),
            pltpu.VMEM((chips, rows, cols), jnp.float32),
            pltpu.SemaphoreType.DMA((2, n)),
            pltpu.SemaphoreType.DMA((3, 2, chips)),
        ],
        compiler_params=pltpu.CompilerParams(
            collective_id=cid, has_side_effects=True, vmem_limit_bytes=48 * 1024 * 1024
        ),
    )(x)


def _gather_kernel(n, x_ref, o_ref, half, full, sems):
    rank = lax.axis_index("replica")
    me = lax.axis_index("mp")
    core = lax.rem(rank, 2)
    partner = rank + 1 - 2 * core
    barrier = pltpu.get_barrier_semaphore()
    for d in range(1, n):
        peer = lax.rem(me + d, n)
        pl.semaphore_signal(barrier, inc=1, device_id=(rank, peer), device_id_type=MESH_IDS)
    pl.semaphore_signal(barrier, inc=1, device_id=(partner, me), device_id_type=MESH_IDS)
    pl.semaphore_wait(barrier, n)
    copies = []
    for d in range(1, n):
        peer = lax.rem(me + d, n)
        copy = pltpu.make_async_remote_copy(
            src_ref=x_ref,
            dst_ref=half.at[me],
            send_sem=sems.at[0, d],
            recv_sem=sems.at[1, me],
            device_id=(rank, peer),
            device_id_type=MESH_IDS,
        )
        copy.start()
        copies.append(copy)
    half[me] = x_ref[...]
    for d in range(1, n):
        source = lax.rem(me + n - d, n)
        pltpu.make_async_remote_copy(
            src_ref=x_ref,
            dst_ref=half.at[source],
            send_sem=sems.at[0, d],
            recv_sem=sems.at[1, source],
            device_id=(rank, source),
            device_id_type=MESH_IDS,
        ).wait_recv()
    for copy in copies:
        copy.wait_send()
    swap = pltpu.make_async_remote_copy(
        src_ref=half,
        dst_ref=full.at[core],
        send_sem=sems.at[2, 0],
        recv_sem=sems.at[2, 1],
        device_id=(partner, me),
        device_id_type=MESH_IDS,
    )
    swap.start()
    full[core] = half[...]
    swap.wait()
    o_ref[...] = full[...]


def gather_right(x, n, cid):
    return pl.pallas_call(
        functools.partial(_gather_kernel, n),
        out_shape=jax.ShapeDtypeStruct((2, n) + x.shape, x.dtype),
        in_specs=[pl.BlockSpec(memory_space=pltpu.VMEM)],
        out_specs=pl.BlockSpec(memory_space=pltpu.VMEM),
        scratch_shapes=[
            pltpu.VMEM((n,) + x.shape, x.dtype),
            pltpu.VMEM((2, n) + x.shape, x.dtype),
            pltpu.SemaphoreType.DMA((3, n)),
        ],
        compiler_params=pltpu.CompilerParams(
            collective_id=cid, has_side_effects=True, vmem_limit_bytes=48 * 1024 * 1024
        ),
    )(x)


def per_device(
    gradients,
    feedback,
    right_init,
    gram_root,
    owners,
    momentum,
    master_weights,
    vector_grads,
    vector_momentum,
    vector_params,
):
    highest = lax.Precision.HIGHEST
    compensated = (gradients[0].astype(jnp.float32) + feedback[0].astype(jnp.float32)).astype(
        jnp.bfloat16
    )
    owner_count = lax.axis_size("mp")
    capacity = momentum.shape[1]
    matrices = owners.shape[0]
    replica_rows = momentum.shape[2]
    mp_index = lax.axis_index("mp")
    replica_index = lax.axis_index("replica")
    same_owner = owners[:, None] == owners[None, :]
    earlier = jnp.arange(matrices)[:, None] < jnp.arange(matrices)[None, :]
    ranks = jnp.sum((same_owner & earlier).astype(jnp.int32), axis=0)
    slots = owners * capacity + ranks
    mine = slots[None, :] == (mp_index * capacity + jnp.arange(capacity))[:, None]
    has = jnp.any(mine, axis=1)
    chosen = jnp.argmax(mine, axis=1)
    weight_base = master_weights[0] - 0.1 * (0.9 * momentum[0])
    weight_slots = lax.all_gather(weight_base.astype(jnp.bfloat16), "mp", axis=0, tiled=True)
    left_terms = jnp.einsum(
        "kmn,knr->kmr", compensated, right_init, preferred_element_type=jnp.float32
    )
    replicas = lax.axis_size("replica")
    vector_len = vector_grads.shape[1]
    packed = jnp.concatenate([left_terms.reshape(-1), vector_grads[0]])
    lanes = 128
    rows = -(-packed.shape[0] // (replicas * 8 * lanes)) * 8
    packed = jnp.pad(packed, (0, replicas * rows * lanes - packed.shape[0]))
    packed = allreduce_replica(packed.reshape(replicas, rows, lanes), 0).reshape(-1)
    left_sum = packed[: left_terms.size].reshape(left_terms.shape)
    vector_total = packed[left_terms.size : left_terms.size + vector_len]
    left_rows = jnp.einsum("kmr,krs->kms", left_sum, gram_root, precision=highest).astype(
        jnp.bfloat16
    )
    owners_count = lax.axis_size("mp")
    cores = 2
    chips = replicas // cores
    pieces = owners_count // (matrices // cores)
    width = compensated.shape[2] // pieces
    right_terms = jnp.einsum(
        "kmn,kms->ksn", compensated, left_rows, preferred_element_type=jnp.float32
    )
    right_terms = right_terms.reshape(matrices, -1, pieces, width).transpose(0, 2, 1, 3)
    right_terms = right_terms.astype(jnp.bfloat16).reshape(cores, owners_count, -1, width)
    right_part = reduce_right(right_terms, chips, 2)
    right_part = right_part.reshape(chips // 2, 2, *right_part.shape[1:]).transpose(0, 2, 1, 3)
    right_part = right_part.reshape(right_terms.shape[2:]).astype(jnp.bfloat16)
    right_new = gather_right(right_part, owners_count, 4)
    right_new = right_new.reshape(matrices, pieces, -1, width).transpose(0, 2, 1, 3)
    right_new = right_new.reshape(matrices, -1, compensated.shape[2])
    pairs = [
        (a * owners_count + b, b * owners_count + a)
        for a in range(replicas)
        for b in range(owners_count)
    ]
    left_block = lax.ppermute(left_rows, ("replica", "mp"), pairs)
    approx_rows = jnp.einsum(
        "kms,ksn->kmn", left_rows, right_new, preferred_element_type=jnp.float32
    )
    new_feedback = (compensated.astype(jnp.float32) - approx_rows).astype(jnp.bfloat16)
    scale = has.astype(jnp.float32)[:, None, None]
    left_chosen = left_block[chosen].astype(jnp.float32) * scale
    right_chosen = right_new[chosen].astype(jnp.float32) * scale
    approx_slots = jnp.einsum("cmr,crn->cmn", left_chosen, right_chosen, precision=highest)
    new_momentum = 0.9 * momentum[0] + approx_slots
    new_master = master_weights[0] - 0.1 * new_momentum
    block_approx = jnp.einsum(
        "kms,ksn->kmn", left_block, right_new, preferred_element_type=jnp.float32
    )
    new_weights = (
        jnp.take(weight_slots, slots, axis=0).astype(jnp.float32) - 0.1 * block_approx
    ).astype(jnp.bfloat16)
    new_vector_momentum = 0.9 * vector_momentum + vector_total
    new_vector_params = vector_params - 0.1 * new_vector_momentum
    return (
        new_feedback[None],
        new_momentum[None],
        new_master[None],
        new_weights,
        new_vector_momentum,
        new_vector_params,
    )


def solution(mesh):
    return jax.shard_map(
        per_device,
        mesh=mesh,
        in_specs=(
            P("replica", None, "mp", None),
            P("replica", None, "mp", None),
            P(),
            P(),
            P(),
            P("mp", None, "replica", None),
            P("mp", None, "replica", None),
            P("replica", "mp"),
            P("mp"),
            P("mp"),
        ),
        out_specs=(
            P("replica", None, "mp", None),
            P("mp", None, "replica", None),
            P("mp", None, "replica", None),
            P(None, "replica", None),
            P("mp"),
            P("mp"),
        ),
        check_vma=False,
    )
```

```python
import functools

import jax
import jax.numpy as jnp
from jax import lax
from jax.experimental import pallas as pl
from jax.experimental.pallas import tpu as pltpu
from jax.sharding import PartitionSpec as P

MESH_IDS = pl.DeviceIdType.MESH


def _exchange_kernel(n, axis, stride, total, x_ref, o_ref, recv, send_sem, recv_sem):
    rank = lax.axis_index(axis)
    me = lax.rem(lax.div(rank, stride), n)
    first = rank - me * stride
    here = [lax.axis_index("replica"), lax.axis_index("mp")]
    where = 0 if axis == "replica" else 1

    def device(peer):
        ids = list(here)
        ids[where] = first + peer * stride
        return tuple(ids)

    barrier = pltpu.get_barrier_semaphore()
    for d in range(1, n):
        peer = lax.rem(me + d, n)
        pl.semaphore_signal(barrier, inc=1, device_id=device(peer), device_id_type=MESH_IDS)
    pl.semaphore_wait(barrier, n - 1)
    copies = []
    for d in range(1, n):
        peer = lax.rem(me + d, n)
        copy = pltpu.make_async_remote_copy(
            src_ref=x_ref.at[peer],
            dst_ref=recv.at[me],
            send_sem=send_sem.at[d],
            recv_sem=recv_sem.at[me],
            device_id=device(peer),
            device_id_type=MESH_IDS,
        )
        copy.start()
        copies.append(copy)
    recv[me] = x_ref[me]
    for d in range(1, n):
        source = lax.rem(me + n - d, n)
        pltpu.make_async_remote_copy(
            src_ref=x_ref.at[source],
            dst_ref=recv.at[source],
            send_sem=send_sem.at[d],
            recv_sem=recv_sem.at[source],
            device_id=device(source),
            device_id_type=MESH_IDS,
        ).wait_recv()
    for copy in copies:
        copy.wait_send()
    if total is None:
        o_ref[...] = recv[...]
    else:
        acc = recv[0].astype(jnp.float32)
        for s in range(1, n):
            acc = acc + recv[s].astype(jnp.float32)
        o_ref[...] = acc.astype(o_ref.dtype)


def exchange(x, axis, cid, stride=1, total=None):
    n = x.shape[0]
    out = jax.ShapeDtypeStruct(x.shape, x.dtype) if total is None else jax.ShapeDtypeStruct(
        x.shape[1:], total
    )
    return pl.pallas_call(
        functools.partial(_exchange_kernel, n, axis, stride, total),
        out_shape=out,
        in_specs=[pl.BlockSpec(memory_space=pltpu.VMEM)],
        out_specs=pl.BlockSpec(memory_space=pltpu.VMEM),
        scratch_shapes=[
            pltpu.VMEM(x.shape, x.dtype),
            pltpu.SemaphoreType.DMA((n,)),
            pltpu.SemaphoreType.DMA((n,)),
        ],
        compiler_params=pltpu.CompilerParams(
            collective_id=cid, has_side_effects=True, vmem_limit_bytes=48 * 1024 * 1024
        ),
    )(x)


def _allreduce_kernel(n, stride, x_ref, o_ref, first, middle, second, send_sem, recv_sem):
    rank = lax.axis_index("replica")
    me = lax.rem(lax.div(rank, stride), n)
    base = rank - me * stride
    mp = lax.axis_index("mp")

    def device(peer):
        return (base + peer * stride, mp)

    barrier = pltpu.get_barrier_semaphore()
    for d in range(1, n):
        peer = lax.rem(me + d, n)
        pl.semaphore_signal(barrier, inc=1, device_id=device(peer), device_id_type=MESH_IDS)
    pl.semaphore_wait(barrier, n - 1)

    def round_trip(phase, source_of, landing):
        copies = []
        for d in range(1, n):
            peer = lax.rem(me + d, n)
            copy = pltpu.make_async_remote_copy(
                src_ref=source_of(peer),
                dst_ref=landing.at[me],
                send_sem=send_sem.at[phase, d],
                recv_sem=recv_sem.at[phase, me],
                device_id=device(peer),
                device_id_type=MESH_IDS,
            )
            copy.start()
            copies.append(copy)
        landing[me] = source_of(me)[...]
        for d in range(1, n):
            source = lax.rem(me + n - d, n)
            pltpu.make_async_remote_copy(
                src_ref=source_of(source),
                dst_ref=landing.at[source],
                send_sem=send_sem.at[phase, d],
                recv_sem=recv_sem.at[phase, source],
                device_id=device(source),
                device_id_type=MESH_IDS,
            ).wait_recv()
        for copy in copies:
            copy.wait_send()

    round_trip(0, lambda peer: x_ref.at[peer], first)
    total = first[0]
    for s in range(1, n):
        total = total + first[s]
    middle[...] = total
    round_trip(1, lambda peer: middle, second)
    o_ref[...] = second[...]


def allreduce_replica(x, cid, stride=1):
    n = x.shape[0]
    return pl.pallas_call(
        functools.partial(_allreduce_kernel, n, stride),
        out_shape=jax.ShapeDtypeStruct(x.shape, x.dtype),
        in_specs=[pl.BlockSpec(memory_space=pltpu.VMEM)],
        out_specs=pl.BlockSpec(memory_space=pltpu.VMEM),
        scratch_shapes=[
            pltpu.VMEM(x.shape, x.dtype),
            pltpu.VMEM(x.shape[1:], x.dtype),
            pltpu.VMEM(x.shape, x.dtype),
            pltpu.SemaphoreType.DMA((2, n)),
            pltpu.SemaphoreType.DMA((2, n)),
        ],
        compiler_params=pltpu.CompilerParams(collective_id=cid, has_side_effects=True),
    )(x)


def _reduce_kernel(
    n, chips, x_ref, o_ref, pair, mine, recv, acc, first, middle, second, mp_sem, z_sem
):
    rank = lax.axis_index("replica")
    me = lax.axis_index("mp")
    core = lax.rem(rank, 2)
    partner = rank + 1 - 2 * core
    spot = lax.rem(lax.div(rank, 2), chips)
    base = rank - spot * 2
    rows, cols = first.shape[1], first.shape[2]

    def chip(peer):
        return (base + peer * 2, me)

    def piece(p):
        r = pl.multiple_of(lax.div(p, 2) * rows, rows)
        c = pl.multiple_of(lax.rem(p, 2) * cols, cols)
        return acc.at[pl.ds(r, rows), pl.ds(c, cols)]

    barrier = pltpu.get_barrier_semaphore()
    for d in range(1, n):
        peer = lax.rem(me + d, n)
        pl.semaphore_signal(barrier, inc=1, device_id=(rank, peer), device_id_type=MESH_IDS)
    for d in range(1, chips):
        peer = lax.rem(spot + d, chips)
        pl.semaphore_signal(barrier, inc=1, device_id=chip(peer), device_id_type=MESH_IDS)
    pl.semaphore_signal(barrier, inc=1, device_id=(partner, me), device_id_type=MESH_IDS)
    pl.semaphore_wait(barrier, n - 1 + chips - 1 + 1)
    swap = pltpu.make_async_remote_copy(
        src_ref=x_ref.at[1 - core],
        dst_ref=pair,
        send_sem=z_sem.at[2, 0, 0],
        recv_sem=z_sem.at[2, 1, 0],
        device_id=(partner, me),
        device_id_type=MESH_IDS,
    )
    swap.start()
    swap.wait()
    mine[...] = (x_ref[core].astype(jnp.float32) + pair[...].astype(jnp.float32)).astype(
        mine.dtype
    )
    copies = []
    for d in range(1, n):
        peer = lax.rem(me + d, n)
        copy = pltpu.make_async_remote_copy(
            src_ref=mine.at[peer],
            dst_ref=recv.at[me],
            send_sem=mp_sem.at[0, d],
            recv_sem=mp_sem.at[1, me],
            device_id=(rank, peer),
            device_id_type=MESH_IDS,
        )
        copy.start()
        copies.append(copy)
    recv[me] = mine[me]
    for d in range(1, n):
        source = lax.rem(me + n - d, n)
        pltpu.make_async_remote_copy(
            src_ref=mine.at[source],
            dst_ref=recv.at[source],
            send_sem=mp_sem.at[0, d],
            recv_sem=mp_sem.at[1, source],
            device_id=(rank, source),
            device_id_type=MESH_IDS,
        ).wait_recv()
    for copy in copies:
        copy.wait_send()
    total = recv[0].astype(jnp.float32)
    for s in range(1, n):
        total = total + recv[s].astype(jnp.float32)
    acc[...] = total

    def round_trip(phase, source_of, landing):
        sent = []
        for d in range(1, chips):
            peer = lax.rem(spot + d, chips)
            copy = pltpu.make_async_remote_copy(
                src_ref=source_of(peer),
                dst_ref=landing.at[spot],
                send_sem=z_sem.at[phase, 0, d],
                recv_sem=z_sem.at[phase, 1, spot],
                device_id=chip(peer),
                device_id_type=MESH_IDS,
            )
            copy.start()
            sent.append(copy)
        landing[spot] = source_of(spot)[...]
        for d in range(1, chips):
            source = lax.rem(spot + chips - d, chips)
            pltpu.make_async_remote_copy(
                src_ref=source_of(source),
                dst_ref=landing.at[source],
                send_sem=z_sem.at[phase, 0, d],
                recv_sem=z_sem.at[phase, 1, source],
                device_id=chip(source),
                device_id_type=MESH_IDS,
            ).wait_recv()
        for copy in sent:
            copy.wait_send()

    round_trip(0, piece, first)
    part = first[0]
    for s in range(1, chips):
        part = part + first[s]
    middle[...] = part
    round_trip(1, lambda peer: middle, second)
    for p in range(chips):
        r, c = (p // 2) * rows, (p % 2) * cols
        o_ref[r : r + rows, c : c + cols] = second[p]


def reduce_right(x, chips, cid):
    n = x.shape[1]
    rows, cols = x.shape[2] // (chips // 2), x.shape[3] // 2
    return pl.pallas_call(
        functools.partial(_reduce_kernel, n, chips),
        out_shape=jax.ShapeDtypeStruct(x.shape[2:], jnp.float32),
        in_specs=[pl.BlockSpec(memory_space=pltpu.VMEM)],
        out_specs=pl.BlockSpec(memory_space=pltpu.VMEM),
        scratch_shapes=[
            pltpu.VMEM(x.shape[1:], x.dtype),
            pltpu.VMEM(x.shape[1:], x.dtype),
            pltpu.VMEM(x.shape[1:], x.dtype),
            pltpu.VMEM(x.shape[2:], jnp.float32),
            pltpu.VMEM((chips, rows, cols), jnp.float32),
            pltpu.VMEM((rows, cols), jnp.float32),
            pltpu.VMEM((chips, rows, cols), jnp.float32),
            pltpu.SemaphoreType.DMA((2, n)),
            pltpu.SemaphoreType.DMA((3, 2, chips)),
        ],
        compiler_params=pltpu.CompilerParams(
            collective_id=cid, has_side_effects=True, vmem_limit_bytes=48 * 1024 * 1024
        ),
    )(x)


def _gather_kernel(n, x_ref, o_ref, half, full, sems):
    rank = lax.axis_index("replica")
    me = lax.axis_index("mp")
    core = lax.rem(rank, 2)
    partner = rank + 1 - 2 * core
    barrier = pltpu.get_barrier_semaphore()
    for d in range(1, n):
        peer = lax.rem(me + d, n)
        pl.semaphore_signal(barrier, inc=1, device_id=(rank, peer), device_id_type=MESH_IDS)
    pl.semaphore_signal(barrier, inc=1, device_id=(partner, me), device_id_type=MESH_IDS)
    pl.semaphore_wait(barrier, n)
    copies = []
    for d in range(1, n):
        peer = lax.rem(me + d, n)
        copy = pltpu.make_async_remote_copy(
            src_ref=x_ref,
            dst_ref=half.at[me],
            send_sem=sems.at[0, d],
            recv_sem=sems.at[1, me],
            device_id=(rank, peer),
            device_id_type=MESH_IDS,
        )
        copy.start()
        copies.append(copy)
    half[me] = x_ref[...]
    for d in range(1, n):
        source = lax.rem(me + n - d, n)
        pltpu.make_async_remote_copy(
            src_ref=x_ref,
            dst_ref=half.at[source],
            send_sem=sems.at[0, d],
            recv_sem=sems.at[1, source],
            device_id=(rank, source),
            device_id_type=MESH_IDS,
        ).wait_recv()
    for copy in copies:
        copy.wait_send()
    swap = pltpu.make_async_remote_copy(
        src_ref=half,
        dst_ref=full.at[core],
        send_sem=sems.at[2, 0],
        recv_sem=sems.at[2, 1],
        device_id=(partner, me),
        device_id_type=MESH_IDS,
    )
    swap.start()
    full[core] = half[...]
    swap.wait()
    o_ref[...] = full[...]


def gather_right(x, n, cid):
    return pl.pallas_call(
        functools.partial(_gather_kernel, n),
        out_shape=jax.ShapeDtypeStruct((2, n) + x.shape, x.dtype),
        in_specs=[pl.BlockSpec(memory_space=pltpu.VMEM)],
        out_specs=pl.BlockSpec(memory_space=pltpu.VMEM),
        scratch_shapes=[
            pltpu.VMEM((n,) + x.shape, x.dtype),
            pltpu.VMEM((2, n) + x.shape, x.dtype),
            pltpu.SemaphoreType.DMA((3, n)),
        ],
        compiler_params=pltpu.CompilerParams(
            collective_id=cid, has_side_effects=True, vmem_limit_bytes=48 * 1024 * 1024
        ),
    )(x)


def per_device(
    gradients,
    feedback,
    right_init,
    gram_root,
    owners,
    momentum,
    master_weights,
    vector_grads,
    vector_momentum,
    vector_params,
):
    highest = lax.Precision.HIGHEST
    compensated = (gradients[0].astype(jnp.float32) + feedback[0].astype(jnp.float32)).astype(
        jnp.bfloat16
    )
    owner_count = lax.axis_size("mp")
    capacity = momentum.shape[1]
    matrices = owners.shape[0]
    replica_rows = momentum.shape[2]
    mp_index = lax.axis_index("mp")
    replica_index = lax.axis_index("replica")
    same_owner = owners[:, None] == owners[None, :]
    earlier = jnp.arange(matrices)[:, None] < jnp.arange(matrices)[None, :]
    ranks = jnp.sum((same_owner & earlier).astype(jnp.int32), axis=0)
    slots = owners * capacity + ranks
    mine = slots[None, :] == (mp_index * capacity + jnp.arange(capacity))[:, None]
    has = jnp.any(mine, axis=1)
    chosen = jnp.argmax(mine, axis=1)
    weight_base = master_weights[0] - 0.1 * (0.9 * momentum[0])
    weight_slots = lax.all_gather(weight_base.astype(jnp.bfloat16), "mp", axis=0, tiled=True)
    left_terms = jnp.einsum(
        "kmn,knr->kmr", compensated, right_init, preferred_element_type=jnp.float32
    )
    replicas = lax.axis_size("replica")
    vector_len = vector_grads.shape[1]
    packed = jnp.concatenate([left_terms.reshape(-1), vector_grads[0]])
    lanes = 128
    rows = -(-packed.shape[0] // (replicas * 8 * lanes)) * 8
    packed = jnp.pad(packed, (0, replicas * rows * lanes - packed.shape[0]))
    packed = allreduce_replica(packed.reshape(replicas, rows, lanes), 0).reshape(-1)
    left_sum = packed[: left_terms.size].reshape(left_terms.shape)
    vector_total = packed[left_terms.size : left_terms.size + vector_len]
    left_rows = jnp.einsum("kmr,krs->kms", left_sum, gram_root, precision=highest).astype(
        jnp.bfloat16
    )
    owners_count = lax.axis_size("mp")
    cores = 2
    chips = replicas // cores
    pieces = owners_count // (matrices // cores)
    width = compensated.shape[2] // pieces
    right_terms = jnp.einsum(
        "kmn,kms->ksn", compensated, left_rows, preferred_element_type=jnp.float32
    )
    right_terms = right_terms.reshape(matrices, -1, pieces, width).transpose(0, 2, 1, 3)
    right_terms = right_terms.astype(jnp.bfloat16).reshape(cores, owners_count, -1, width)
    right_part = reduce_right(right_terms, chips, 2).astype(jnp.bfloat16)
    right_new = gather_right(right_part, owners_count, 4)
    right_new = right_new.reshape(matrices, pieces, -1, width).transpose(0, 2, 1, 3)
    right_new = right_new.reshape(matrices, -1, compensated.shape[2])
    pairs = [
        (a * owners_count + b, b * owners_count + a)
        for a in range(replicas)
        for b in range(owners_count)
    ]
    left_block = lax.ppermute(left_rows, ("replica", "mp"), pairs)
    approx_rows = jnp.einsum(
        "kms,ksn->kmn", left_rows, right_new, preferred_element_type=jnp.float32
    )
    new_feedback = (compensated.astype(jnp.float32) - approx_rows).astype(jnp.bfloat16)
    scale = has.astype(jnp.float32)[:, None, None]
    left_chosen = left_block[chosen].astype(jnp.float32) * scale
    right_chosen = right_new[chosen].astype(jnp.float32) * scale
    approx_slots = jnp.einsum("cmr,crn->cmn", left_chosen, right_chosen, precision=highest)
    new_momentum = 0.9 * momentum[0] + approx_slots
    new_master = master_weights[0] - 0.1 * new_momentum
    block_approx = jnp.einsum(
        "kms,ksn->kmn", left_block, right_new, preferred_element_type=jnp.float32
    )
    new_weights = (
        jnp.take(weight_slots, slots, axis=0).astype(jnp.float32) - 0.1 * block_approx
    ).astype(jnp.bfloat16)
    new_vector_momentum = 0.9 * vector_momentum + vector_total
    new_vector_params = vector_params - 0.1 * new_vector_momentum
    return (
        new_feedback[None],
        new_momentum[None],
        new_master[None],
        new_weights,
        new_vector_momentum,
        new_vector_params,
    )


def solution(mesh):
    return jax.shard_map(
        per_device,
        mesh=mesh,
        in_specs=(
            P("replica", None, "mp", None),
            P("replica", None, "mp", None),
            P(),
            P(),
            P(),
            P("mp", None, "replica", None),
            P("mp", None, "replica", None),
            P("replica", "mp"),
            P("mp"),
            P("mp"),
        ),
        out_specs=(
            P("replica", None, "mp", None),
            P("mp", None, "replica", None),
            P("mp", None, "replica", None),
            P(None, "replica", None),
            P("mp"),
            P("mp"),
        ),
        check_vma=False,
    )
```

```python
import functools

import jax
import jax.numpy as jnp
from jax import lax
from jax.experimental import pallas as pl
from jax.experimental.pallas import tpu as pltpu
from jax.sharding import PartitionSpec as P

MESH_IDS = pl.DeviceIdType.MESH


def _exchange_kernel(n, axis, stride, total, x_ref, o_ref, recv, send_sem, recv_sem):
    rank = lax.axis_index(axis)
    me = lax.rem(lax.div(rank, stride), n)
    first = rank - me * stride
    here = [lax.axis_index("replica"), lax.axis_index("mp")]
    where = 0 if axis == "replica" else 1

    def device(peer):
        ids = list(here)
        ids[where] = first + peer * stride
        return tuple(ids)

    barrier = pltpu.get_barrier_semaphore()
    for d in range(1, n):
        peer = lax.rem(me + d, n)
        pl.semaphore_signal(barrier, inc=1, device_id=device(peer), device_id_type=MESH_IDS)
    pl.semaphore_wait(barrier, n - 1)
    copies = []
    for d in range(1, n):
        peer = lax.rem(me + d, n)
        copy = pltpu.make_async_remote_copy(
            src_ref=x_ref.at[peer],
            dst_ref=recv.at[me],
            send_sem=send_sem.at[d],
            recv_sem=recv_sem.at[me],
            device_id=device(peer),
            device_id_type=MESH_IDS,
        )
        copy.start()
        copies.append(copy)
    recv[me] = x_ref[me]
    for d in range(1, n):
        source = lax.rem(me + n - d, n)
        pltpu.make_async_remote_copy(
            src_ref=x_ref.at[source],
            dst_ref=recv.at[source],
            send_sem=send_sem.at[d],
            recv_sem=recv_sem.at[source],
            device_id=device(source),
            device_id_type=MESH_IDS,
        ).wait_recv()
    for copy in copies:
        copy.wait_send()
    if total is None:
        o_ref[...] = recv[...]
    else:
        acc = recv[0].astype(jnp.float32)
        for s in range(1, n):
            acc = acc + recv[s].astype(jnp.float32)
        o_ref[...] = acc.astype(o_ref.dtype)


def exchange(x, axis, cid, stride=1, total=None):
    n = x.shape[0]
    out = jax.ShapeDtypeStruct(x.shape, x.dtype) if total is None else jax.ShapeDtypeStruct(
        x.shape[1:], total
    )
    return pl.pallas_call(
        functools.partial(_exchange_kernel, n, axis, stride, total),
        out_shape=out,
        in_specs=[pl.BlockSpec(memory_space=pltpu.VMEM)],
        out_specs=pl.BlockSpec(memory_space=pltpu.VMEM),
        scratch_shapes=[
            pltpu.VMEM(x.shape, x.dtype),
            pltpu.SemaphoreType.DMA((n,)),
            pltpu.SemaphoreType.DMA((n,)),
        ],
        compiler_params=pltpu.CompilerParams(
            collective_id=cid, has_side_effects=True, vmem_limit_bytes=48 * 1024 * 1024
        ),
    )(x)


def _allreduce_kernel(n, stride, x_ref, o_ref, first, middle, second, send_sem, recv_sem):
    rank = lax.axis_index("replica")
    me = lax.rem(lax.div(rank, stride), n)
    base = rank - me * stride
    mp = lax.axis_index("mp")

    def device(peer):
        return (base + peer * stride, mp)

    barrier = pltpu.get_barrier_semaphore()
    for d in range(1, n):
        peer = lax.rem(me + d, n)
        pl.semaphore_signal(barrier, inc=1, device_id=device(peer), device_id_type=MESH_IDS)
    pl.semaphore_wait(barrier, n - 1)

    def round_trip(phase, source_of, landing):
        copies = []
        for d in range(1, n):
            peer = lax.rem(me + d, n)
            copy = pltpu.make_async_remote_copy(
                src_ref=source_of(peer),
                dst_ref=landing.at[me],
                send_sem=send_sem.at[phase, d],
                recv_sem=recv_sem.at[phase, me],
                device_id=device(peer),
                device_id_type=MESH_IDS,
            )
            copy.start()
            copies.append(copy)
        landing[me] = source_of(me)[...]
        for d in range(1, n):
            source = lax.rem(me + n - d, n)
            pltpu.make_async_remote_copy(
                src_ref=source_of(source),
                dst_ref=landing.at[source],
                send_sem=send_sem.at[phase, d],
                recv_sem=recv_sem.at[phase, source],
                device_id=device(source),
                device_id_type=MESH_IDS,
            ).wait_recv()
        for copy in copies:
            copy.wait_send()

    round_trip(0, lambda peer: x_ref.at[peer], first)
    total = first[0]
    for s in range(1, n):
        total = total + first[s]
    middle[...] = total
    round_trip(1, lambda peer: middle, second)
    o_ref[...] = second[...]


def allreduce_replica(x, cid, stride=1):
    n = x.shape[0]
    return pl.pallas_call(
        functools.partial(_allreduce_kernel, n, stride),
        out_shape=jax.ShapeDtypeStruct(x.shape, x.dtype),
        in_specs=[pl.BlockSpec(memory_space=pltpu.VMEM)],
        out_specs=pl.BlockSpec(memory_space=pltpu.VMEM),
        scratch_shapes=[
            pltpu.VMEM(x.shape, x.dtype),
            pltpu.VMEM(x.shape[1:], x.dtype),
            pltpu.VMEM(x.shape, x.dtype),
            pltpu.SemaphoreType.DMA((2, n)),
            pltpu.SemaphoreType.DMA((2, n)),
        ],
        compiler_params=pltpu.CompilerParams(collective_id=cid, has_side_effects=True),
    )(x)


def _reduce_kernel(
    n, chips, x_ref, o_ref, pair, mine, recv, acc, first, middle, second, mp_sem, z_sem
):
    rank = lax.axis_index("replica")
    me = lax.axis_index("mp")
    core = lax.rem(rank, 2)
    partner = rank + 1 - 2 * core
    spot = lax.rem(lax.div(rank, 2), chips)
    base = rank - spot * 2
    rows, cols = first.shape[1], first.shape[2]

    def chip(peer):
        return (base + peer * 2, me)

    def piece(p):
        r = pl.multiple_of(lax.div(p, 2) * rows, rows)
        c = pl.multiple_of(lax.rem(p, 2) * cols, cols)
        return acc.at[pl.ds(r, rows), pl.ds(c, cols)]

    barrier = pltpu.get_barrier_semaphore()
    for d in range(1, n):
        peer = lax.rem(me + d, n)
        pl.semaphore_signal(barrier, inc=1, device_id=(rank, peer), device_id_type=MESH_IDS)
    for d in range(1, chips):
        peer = lax.rem(spot + d, chips)
        pl.semaphore_signal(barrier, inc=1, device_id=chip(peer), device_id_type=MESH_IDS)
    pl.semaphore_signal(barrier, inc=1, device_id=(partner, me), device_id_type=MESH_IDS)
    pl.semaphore_wait(barrier, n - 1 + chips - 1 + 1)
    swap = pltpu.make_async_remote_copy(
        src_ref=x_ref.at[1 - core],
        dst_ref=pair,
        send_sem=z_sem.at[2, 0, 0],
        recv_sem=z_sem.at[2, 1, 0],
        device_id=(partner, me),
        device_id_type=MESH_IDS,
    )
    swap.start()
    swap.wait()
    mine[...] = (x_ref[core].astype(jnp.float32) + pair[...].astype(jnp.float32)).astype(
        mine.dtype
    )
    copies = []
    for d in range(1, n):
        peer = lax.rem(me + d, n)
        copy = pltpu.make_async_remote_copy(
            src_ref=mine.at[peer],
            dst_ref=recv.at[me],
            send_sem=mp_sem.at[0, d],
            recv_sem=mp_sem.at[1, me],
            device_id=(rank, peer),
            device_id_type=MESH_IDS,
        )
        copy.start()
        copies.append(copy)
    recv[me] = mine[me]
    for d in range(1, n):
        source = lax.rem(me + n - d, n)
        pltpu.make_async_remote_copy(
            src_ref=mine.at[source],
            dst_ref=recv.at[source],
            send_sem=mp_sem.at[0, d],
            recv_sem=mp_sem.at[1, source],
            device_id=(rank, source),
            device_id_type=MESH_IDS,
        ).wait_recv()
    for copy in copies:
        copy.wait_send()
    total = recv[0].astype(jnp.float32)
    for s in range(1, n):
        total = total + recv[s].astype(jnp.float32)
    acc[...] = total

    def round_trip(phase, source_of, landing):
        sent = []
        for d in range(1, chips):
            peer = lax.rem(spot + d, chips)
            copy = pltpu.make_async_remote_copy(
                src_ref=source_of(peer),
                dst_ref=landing.at[spot],
                send_sem=z_sem.at[phase, 0, d],
                recv_sem=z_sem.at[phase, 1, spot],
                device_id=chip(peer),
                device_id_type=MESH_IDS,
            )
            copy.start()
            sent.append(copy)
        landing[spot] = source_of(spot)[...]
        for d in range(1, chips):
            source = lax.rem(spot + chips - d, chips)
            pltpu.make_async_remote_copy(
                src_ref=source_of(source),
                dst_ref=landing.at[source],
                send_sem=z_sem.at[phase, 0, d],
                recv_sem=z_sem.at[phase, 1, source],
                device_id=chip(source),
                device_id_type=MESH_IDS,
            ).wait_recv()
        for copy in sent:
            copy.wait_send()

    round_trip(0, piece, first)
    part = first[0]
    for s in range(1, chips):
        part = part + first[s]
    middle[...] = part
    round_trip(1, lambda peer: middle, second)
    for p in range(chips):
        r, c = (p // 2) * rows, (p % 2) * cols
        o_ref[r : r + rows, c : c + cols] = second[p]


def reduce_right(x, chips, cid):
    n = x.shape[1]
    rows, cols = x.shape[2] // (chips // 2), x.shape[3] // 2
    return pl.pallas_call(
        functools.partial(_reduce_kernel, n, chips),
        out_shape=jax.ShapeDtypeStruct(x.shape[2:], jnp.float32),
        in_specs=[pl.BlockSpec(memory_space=pltpu.VMEM)],
        out_specs=pl.BlockSpec(memory_space=pltpu.VMEM),
        scratch_shapes=[
            pltpu.VMEM(x.shape[1:], x.dtype),
            pltpu.VMEM(x.shape[1:], x.dtype),
            pltpu.VMEM(x.shape[1:], x.dtype),
            pltpu.VMEM(x.shape[2:], jnp.float32),
            pltpu.VMEM((chips, rows, cols), jnp.float32),
            pltpu.VMEM((rows, cols), jnp.float32),
            pltpu.VMEM((chips, rows, cols), jnp.float32),
            pltpu.SemaphoreType.DMA((2, n)),
            pltpu.SemaphoreType.DMA((3, 2, chips)),
        ],
        compiler_params=pltpu.CompilerParams(
            collective_id=cid, has_side_effects=True, vmem_limit_bytes=48 * 1024 * 1024
        ),
    )(x)


def _gather_kernel(n, x_ref, o_ref, mine, half, full, sems):
    rank = lax.axis_index("replica")
    me = lax.axis_index("mp")
    core = lax.rem(rank, 2)
    partner = rank + 1 - 2 * core
    barrier = pltpu.get_barrier_semaphore()
    for d in range(1, n):
        peer = lax.rem(me + d, n)
        pl.semaphore_signal(barrier, inc=1, device_id=(rank, peer), device_id_type=MESH_IDS)
    pl.semaphore_signal(barrier, inc=1, device_id=(partner, me), device_id_type=MESH_IDS)
    pl.semaphore_wait(barrier, n)
    mine[...] = x_ref[...].astype(mine.dtype)
    copies = []
    for d in range(1, n):
        peer = lax.rem(me + d, n)
        copy = pltpu.make_async_remote_copy(
            src_ref=mine,
            dst_ref=half.at[me],
            send_sem=sems.at[0, d],
            recv_sem=sems.at[1, me],
            device_id=(rank, peer),
            device_id_type=MESH_IDS,
        )
        copy.start()
        copies.append(copy)
    half[me] = mine[...]
    for d in range(1, n):
        source = lax.rem(me + n - d, n)
        pltpu.make_async_remote_copy(
            src_ref=mine,
            dst_ref=half.at[source],
            send_sem=sems.at[0, d],
            recv_sem=sems.at[1, source],
            device_id=(rank, source),
            device_id_type=MESH_IDS,
        ).wait_recv()
    for copy in copies:
        copy.wait_send()
    swap = pltpu.make_async_remote_copy(
        src_ref=half,
        dst_ref=full.at[core],
        send_sem=sems.at[2, 0],
        recv_sem=sems.at[2, 1],
        device_id=(partner, me),
        device_id_type=MESH_IDS,
    )
    swap.start()
    full[core] = half[...]
    swap.wait()
    o_ref[...] = full[...]


def gather_right(x, n, cid):
    return pl.pallas_call(
        functools.partial(_gather_kernel, n),
        out_shape=jax.ShapeDtypeStruct((2, n) + x.shape, jnp.bfloat16),
        in_specs=[pl.BlockSpec(memory_space=pltpu.VMEM)],
        out_specs=pl.BlockSpec(memory_space=pltpu.VMEM),
        scratch_shapes=[
            pltpu.VMEM(x.shape, jnp.bfloat16),
            pltpu.VMEM((n,) + x.shape, jnp.bfloat16),
            pltpu.VMEM((2, n) + x.shape, jnp.bfloat16),
            pltpu.SemaphoreType.DMA((3, n)),
        ],
        compiler_params=pltpu.CompilerParams(
            collective_id=cid, has_side_effects=True, vmem_limit_bytes=48 * 1024 * 1024
        ),
    )(x)


def per_device(
    gradients,
    feedback,
    right_init,
    gram_root,
    owners,
    momentum,
    master_weights,
    vector_grads,
    vector_momentum,
    vector_params,
):
    highest = lax.Precision.HIGHEST
    compensated = (gradients[0].astype(jnp.float32) + feedback[0].astype(jnp.float32)).astype(
        jnp.bfloat16
    )
    owner_count = lax.axis_size("mp")
    capacity = momentum.shape[1]
    matrices = owners.shape[0]
    replica_rows = momentum.shape[2]
    mp_index = lax.axis_index("mp")
    replica_index = lax.axis_index("replica")
    same_owner = owners[:, None] == owners[None, :]
    earlier = jnp.arange(matrices)[:, None] < jnp.arange(matrices)[None, :]
    ranks = jnp.sum((same_owner & earlier).astype(jnp.int32), axis=0)
    slots = owners * capacity + ranks
    mine = slots[None, :] == (mp_index * capacity + jnp.arange(capacity))[:, None]
    has = jnp.any(mine, axis=1)
    chosen = jnp.argmax(mine, axis=1)
    weight_base = master_weights[0] - 0.1 * (0.9 * momentum[0])
    weight_slots = lax.all_gather(weight_base.astype(jnp.bfloat16), "mp", axis=0, tiled=True)
    left_terms = jnp.einsum(
        "kmn,knr->kmr", compensated, right_init, preferred_element_type=jnp.float32
    )
    replicas = lax.axis_size("replica")
    vector_len = vector_grads.shape[1]
    packed = jnp.concatenate([left_terms.reshape(-1), vector_grads[0]])
    lanes = 128
    rows = -(-packed.shape[0] // (replicas * 8 * lanes)) * 8
    packed = jnp.pad(packed, (0, replicas * rows * lanes - packed.shape[0]))
    packed = allreduce_replica(packed.reshape(replicas, rows, lanes), 0).reshape(-1)
    left_sum = packed[: left_terms.size].reshape(left_terms.shape)
    vector_total = packed[left_terms.size : left_terms.size + vector_len]
    left_rows = jnp.einsum("kmr,krs->kms", left_sum, gram_root, precision=highest).astype(
        jnp.bfloat16
    )
    owners_count = lax.axis_size("mp")
    cores = 2
    chips = replicas // cores
    pieces = owners_count // (matrices // cores)
    width = compensated.shape[2] // pieces
    right_terms = jnp.einsum(
        "kmn,kms->ksn", compensated, left_rows, preferred_element_type=jnp.float32
    )
    right_terms = right_terms.reshape(matrices, -1, pieces, width).transpose(0, 2, 1, 3)
    right_terms = right_terms.astype(jnp.bfloat16).reshape(cores, owners_count, -1, width)
    right_part = reduce_right(right_terms, chips, 2)
    right_new = gather_right(right_part, owners_count, 4)
    right_new = right_new.reshape(matrices, pieces, -1, width).transpose(0, 2, 1, 3)
    right_new = right_new.reshape(matrices, -1, compensated.shape[2])
    pairs = [
        (a * owners_count + b, b * owners_count + a)
        for a in range(replicas)
        for b in range(owners_count)
    ]
    left_block = lax.ppermute(left_rows, ("replica", "mp"), pairs)
    approx_rows = jnp.einsum(
        "kms,ksn->kmn", left_rows, right_new, preferred_element_type=jnp.float32
    )
    new_feedback = (compensated.astype(jnp.float32) - approx_rows).astype(jnp.bfloat16)
    scale = has.astype(jnp.float32)[:, None, None]
    left_chosen = left_block[chosen].astype(jnp.float32) * scale
    right_chosen = right_new[chosen].astype(jnp.float32) * scale
    approx_slots = jnp.einsum("cmr,crn->cmn", left_chosen, right_chosen, precision=highest)
    new_momentum = 0.9 * momentum[0] + approx_slots
    new_master = master_weights[0] - 0.1 * new_momentum
    block_approx = jnp.einsum(
        "kms,ksn->kmn", left_block, right_new, preferred_element_type=jnp.float32
    )
    new_weights = (
        jnp.take(weight_slots, slots, axis=0).astype(jnp.float32) - 0.1 * block_approx
    ).astype(jnp.bfloat16)
    new_vector_momentum = 0.9 * vector_momentum + vector_total
    new_vector_params = vector_params - 0.1 * new_vector_momentum
    return (
        new_feedback[None],
        new_momentum[None],
        new_master[None],
        new_weights,
        new_vector_momentum,
        new_vector_params,
    )


def solution(mesh):
    return jax.shard_map(
        per_device,
        mesh=mesh,
        in_specs=(
            P("replica", None, "mp", None),
            P("replica", None, "mp", None),
            P(),
            P(),
            P(),
            P("mp", None, "replica", None),
            P("mp", None, "replica", None),
            P("replica", "mp"),
            P("mp"),
            P("mp"),
        ),
        out_specs=(
            P("replica", None, "mp", None),
            P("mp", None, "replica", None),
            P("mp", None, "replica", None),
            P(None, "replica", None),
            P("mp"),
            P("mp"),
        ),
        check_vma=False,
    )
```
